128 devices in a mesh: row: 16 (over z, y), col: 8 (over x, core).
Axes of the slice: x: 4, y: 4, z: 4, core: 2. Of those that a mesh axis runs over, the one named last changes fastest.
Arguments:
- activations: bfloat16 [32768, 4096], P(('row', 'col')), may hold values from -6 to 6
- out_grads: bfloat16 [32768, 4096], P(('row', 'col')), may hold values from -6 to 6
- proj_in: bfloat16 [4096, 128], replicated, may hold values from -0.09375 to 0.09375
- proj_out: bfloat16 [4096, 128], replicated, may hold values from -0.09375 to 0.09375
- lengths: int32 [1024], P(('row', 'col')), may hold values from 1 to 32, 24576 in all
- gram_old: float32 [16384, 16384], P('row', 'col'), as said below
- queries: float32 [16384, 256], P('row'), may hold values from -96 to 96
Outputs:
- gram_new: float32 [16384, 16384], P('row', 'col')
- solution: float32 [16384, 256], P('row')
The draws below stay inside these ranges and needn't reach their ends.
Inputs may be any that keep to these rules, and one draw needn't show every extreme that they name: `gram_old`: symmetric and positive definite. Example e's token slots from lengths[e] on are padding.
All inputs are finite; a program needn't handle non-finite values. No bound on the sum of `lengths` on one device may be relied on, other than what follows from the above.
Results may differ from the reference program's by a relative error of at most 0.0055.
Values may be sent and summed in bfloat16 or wider, within the bound.
A program may use at most 192 MiB of HBM per device.

```python
import math
import jax
import jax.numpy as jnp
import numpy as np
from jax import lax

D = 4096
R = 128
SEQ = 32
ITERS = 2
NQ = 256
EXAMPLES = 1024
TOKENS = 32768
FEAT = 16384


def draw_gram_old(key, part):
    order_size = R * R
    factor_count = R
    key_noise, key_levels, key_factor = jax.random.split(key, 3)
    entries = jax.random.normal(key_noise, (order_size, order_size), jnp.float32)
    levels = jnp.exp(jax.random.uniform(key_levels, (order_size,), jnp.float32, math.log(4.0), math.log(16.0)))
    factor = jax.random.normal(key_factor, (order_size, factor_count), jnp.float32)
    factor = factor * math.sqrt(8.0 / factor_count)
    coupled = jnp.dot(factor, factor.T, precision=lax.Precision.HIGHEST)
    coupled = 0.5 * (coupled + coupled.T)
    shared = (entries + entries.T) * 0.5 ** 0.5 / math.sqrt(order_size)
    return shared + coupled + jnp.diag(levels)


def level_of(stream_key, dims, cuts, least, top_value):
    loudness = 1.0
    for axis_at, parts in cuts:
        steps = jax.random.uniform(jax.random.fold_in(jax.random.fold_in(stream_key, 6), axis_at), (parts,), jnp.float32, least / len(cuts), top_value / len(cuts))
        loudness = loudness * jnp.repeat(jnp.exp(steps), dims[axis_at] // parts).reshape((-1,) + (1,) * (len(dims) - 1 - axis_at))
    return loudness


def length_profile(amount, total, bound, lean):
    loads = [(1 << 20) // math.isqrt(standing ** lean) + 1 for standing in range(2, amount + 1)]
    surplus, holding = total - bound - (amount - 1), [1] * (amount - 1)
    while surplus > 0:
        movable = [i for i in range(amount - 1) if holding[i] < bound]
        whole, budget = sum([loads[i] for i in movable]), surplus
        for i in movable:
            more = min(bound - holding[i], max(1, budget * loads[i] // whole), surplus)
            holding[i] = holding[i] + more
            surplus = surplus - more
    return np.array([bound] + holding)


def uneven_parts(key, amount, total, bound, slope):
    if amount == 2:
        one = jax.random.randint(key, (), max(1, total - bound), min(bound, total - 1) + 1)
        return jnp.stack([one, total - one])
    sizes = jnp.asarray(length_profile(amount, total, bound, slope), jnp.int32)
    twos = (amount - 1) // 2
    giver, taker = sizes[1:1 + 2 * twos:2], sizes[2:2 + 2 * twos:2]
    room = jnp.minimum(giver - 1, bound - taker)
    passed = jax.random.randint(jax.random.fold_in(key, 1), (twos,), 0, 1 << 20) % (room + 1)
    sizes = sizes.at[1:1 + 2 * twos:2].set(giver - passed).at[2:2 + 2 * twos:2].set(taker + passed)
    return sizes[jax.random.permutation(jax.random.fold_in(key, 2), amount)]


def scatter_about(key, dims, scale, bound, pieces=(), held_as=jnp.bfloat16):
    values = jax.random.normal(key, dims, jnp.float32) * scale
    if len(pieces) > 0:
        values = level_of(key, dims, pieces, -0.22, 0.18) * values
    return jnp.clip(values, min=-bound, max=bound).astype(held_as)


def setup_inputs(seed: int = 0) -> dict:
    streams_of = jax.random.split(jax.random.key(seed), 8)
    activations = scatter_about(streams_of[0], (TOKENS, D), 1.0, 6.0, ((0, 128),))
    out_grads = scatter_about(streams_of[1], (TOKENS, D), 1.0, 6.0, ((0, 128),))
    proj_in = scatter_about(streams_of[2], (D, R), D ** -0.5, 0.09375)
    proj_out = scatter_about(streams_of[3], (D, R), D ** -0.5, 0.09375)
    lengths = uneven_parts(streams_of[4], EXAMPLES, EXAMPLES * 24, SEQ, 1).astype(jnp.int32)
    gram_old = draw_gram_old(jax.random.fold_in(streams_of[7], 71), 0)
    queries = scatter_about(streams_of[6], (FEAT, NQ), 16.0, 96.0, ((0, 16),), jnp.float32)
    return dict(activations=activations, out_grads=out_grads, proj_in=proj_in, proj_out=proj_out, lengths=lengths, gram_old=gram_old, queries=queries)


decay_rate = 0.5
damping = 1.0


def reference(activations, out_grads, proj_in, proj_out, lengths, gram_old, queries):
    low_in = jnp.dot(activations, proj_in, preferred_element_type=jnp.float32).astype(jnp.bfloat16)
    low_out = jnp.dot(out_grads, proj_out, preferred_element_type=jnp.float32).astype(jnp.bfloat16)
    low_in = low_in.reshape(EXAMPLES, SEQ, R)
    low_out = low_out.reshape(EXAMPLES, SEQ, R)
    valid_mask = jnp.arange(SEQ)[None, :] < lengths[:, None]
    low_out = jnp.where(valid_mask[:, :, None], low_out, jnp.zeros((), jnp.bfloat16))
    grads = jnp.einsum("eto,eti->eoi", low_out.astype(jnp.float32), low_in.astype(jnp.float32))
    grads = grads.reshape(EXAMPLES, FEAT).astype(jnp.bfloat16)
    product = lax.dot_general(grads, grads, (((0,), (0,)), ((), ())), preferred_element_type=jnp.float32)
    gram_new = decay_rate * gram_old + ((1.0 - decay_rate) / EXAMPLES) * product
    diag_index = jnp.arange(FEAT)
    gram_new = gram_new.at[diag_index, diag_index].add(damping)
    solution = jnp.zeros_like(queries)
    residual = queries
    direction = queries
    norm_now = jnp.sum(residual * residual, axis=0)
    for sweep in range(ITERS):
        mapped = jnp.dot(gram_new, direction, precision=lax.Precision.HIGHEST)
        step_size = norm_now / jnp.sum(direction * mapped, axis=0)
        solution = solution + step_size * direction
        if sweep + 1 < ITERS:
            residual = residual - step_size * mapped
            norm_next = jnp.sum(residual * residual, axis=0)
            direction = residual + (norm_next / norm_now) * direction
            norm_now = norm_next
    return gram_new, solution
```

```python
import functools

import jax
import jax.numpy as jnp
from jax import lax
from jax.experimental import pallas as pl
from jax.experimental.pallas import tpu as pltpu
from jax.sharding import PartitionSpec as P

MESH = pl.DeviceIdType.MESH
SEQ = 32
ITERS = 2
decay_rate = 0.5
damping = 1.0
HBM = pl.ANY


class Ring:
    def __init__(self, go, slot, lo, hi, ss, rs, base, plus, minus):
        self.go, self.slot, self.lo, self.hi = go, slot, lo, hi
        self.ss, self.rs, self.base = ss, rs, base
        self.plus, self.minus = plus, minus

    def copy(self, ref, k, dev):
        return self.go(pltpu.make_async_remote_copy(
            src_ref=ref, dst_ref=ref, send_sem=self.ss.at[self.base + k], recv_sem=self.rs.at[self.base + k],
            device_id=dev, device_id_type=MESH))

    def start(self):
        own = self.slot(0)
        self.f0 = self.copy(own, 0, self.plus)
        self.f1 = self.copy(own, 1, self.minus)

    def forward(self):
        self.f0.wait_recv()
        self.h0 = self.copy(self.lo(self.slot(3)), 2, self.plus)
        self.f1.wait_recv()
        self.h1 = self.copy(self.hi(self.slot(1)), 3, self.minus)

    def finish(self):
        self.h0.wait_recv()
        self.h1.wait_recv()


def greet(row, col):
    barrier = pltpu.get_barrier_semaphore()
    for k in range(1, 8):
        pl.semaphore_signal(barrier, inc=1, device_id=(row, lax.rem(col + k, 8)), device_id_type=MESH)
    for k in range(1, 16):
        pl.semaphore_signal(barrier, inc=1, device_id=(lax.rem(row + k, 16), col), device_id_type=MESH)
    pl.semaphore_wait(barrier, 22)


def gather_kernel(lg, left, right, loc_sem, c_send, c_recv, r_send, r_recv,
                  ya_send, ya_recv, za_send, za_recv, x_send, x_recv, p_send, p_recv):
    row = lax.axis_index("row")
    col = lax.axis_index("col")
    z, y = row // 4, row % 4
    x, core = col // 2, col % 2

    def at_col(k):
        return lax.rem(col + k, 8)

    def at_row(k):
        return lax.rem(row + k, 16)

    greet(row, col)

    def remote(src, dst, ssem, rsem, dev):
        return pltpu.make_async_remote_copy(src_ref=src, dst_ref=dst, send_sem=ssem, recv_sem=rsem,
                                            device_id=dev, device_id_type=MESH)

    sends = []

    def go(copy):
        copy.start()
        sends.append(copy)
        return copy

    own_right = pltpu.make_async_copy(lg.at[pl.ds(2 * col, 2)], right.at[:, z, y, col], loc_sem.at[0])
    own_right.start()
    own_left = pltpu.make_async_copy(lg.at[row], left.at[z, y, col], loc_sem.at[1])
    own_left.start()
    stage_c = []
    for k in (2, 6, 1, 7, 3, 5, 4):
        to = at_col(k)
        stage_c.append(go(remote(lg.at[pl.ds(2 * to, 2)], right.at[:, z, y, col],
                                 c_send.at[k], c_recv.at[k], (row, to))))
    stage_r = []
    for k in range(1, 16):
        to = at_row(k)
        stage_r.append(go(remote(lg.at[to], left.at[z, y, col], r_send.at[k], r_recv.at[k], (to, col))))

    yp, ym = z * 4 + lax.rem(y + 1, 4), z * 4 + lax.rem(y + 3, 4)
    zp, zm = lax.rem(z + 1, 4) * 4 + y, lax.rem(z + 3, 4) * 4 + y
    xp, xm = lax.rem(x + 1, 4) * 2 + core, lax.rem(x + 3, 4) * 2 + core
    partner = x * 2 + (1 - core)

    def ymod(k):
        return lax.rem(y + k, 4)

    def zmod(k):
        return lax.rem(z + k, 4)

    lo5, hi5 = (lambda r: r.at[pl.ds(0, 4)]), (lambda r: r.at[pl.ds(4, 4)])
    a0 = Ring(go, lambda k: right.at[0, z, ymod(k)], lo5, hi5, ya_send, ya_recv, 0, (yp, col), (ym, col))
    a1 = Ring(go, lambda k: right.at[1, zmod(k), y], lo5, hi5, za_send, za_recv, 0, (zp, col), (zm, col))
    b0 = [Ring(go, lambda k, j=j: right.at[0, zmod(k), ymod(j)], lo5, hi5, za_send, za_recv, 4 + 4 * j, (zp, col), (zm, col))
          for j in range(4)]
    b1 = [Ring(go, lambda k, j=j: right.at[1, zmod(j), ymod(k)], lo5, hi5, ya_send, ya_recv, 4 + 4 * j, (yp, col), (ym, col))
          for j in range(4)]
    xr = Ring(go, lambda k: left.at[:, :, lax.rem(x + k, 4) * 2 + core], lambda r: r.at[pl.ds(0, 2)], lambda r: r.at[pl.ds(2, 2)],
              x_send, x_recv, 0, (row, xp), (row, xm))

    def to_partner(k):
        c = left.at[:, :, lax.rem(x + k, 4) * 2 + core]
        return go(remote(c, c, p_send.at[k], p_recv.at[k], (row, partner)))

    own_right.wait()
    for c in stage_c:
        c.wait_recv()
    a0.start(); a1.start()
    b0[0].start(); b1[0].start()
    own_left.wait()
    for c in stage_r:
        c.wait_recv()
    xr.start()
    pp = [to_partner(0)]
    a0.forward(); a1.forward()
    for j in (3, 1):
        b0[j].start(); b1[j].start()
    xr.forward()
    pp += [to_partner(3), to_partner(1)]
    b0[0].forward(); b1[0].forward()
    a0.finish(); a1.finish()
    b0[2].start(); b1[2].start()
    xr.finish()
    pp += [to_partner(2)]
    for j in (3, 1, 2):
        b0[j].forward(); b1[j].forward()
    for j in range(4):
        b0[j].finish(); b1[j].finish()
    for c in pp:
        c.wait_recv()
    for c in sends:
        c.wait_send()


def gather(lg):
    dma = pltpu.SemaphoreType.DMA
    return pl.pallas_call(
        gather_kernel,
        out_shape=(jax.ShapeDtypeStruct((4, 4, 8, 8, 1024), jnp.bfloat16),
                   jax.ShapeDtypeStruct((2, 4, 4, 8, 8, 1024), jnp.bfloat16)),
        in_specs=[pl.BlockSpec(memory_space=pltpu.VMEM)],
        out_specs=(pl.BlockSpec(memory_space=HBM), pl.BlockSpec(memory_space=HBM)),
        scratch_shapes=[dma((2,)), dma((8,)), dma((8,)), dma((16,)), dma((16,)),
                        dma((20,)), dma((20,)), dma((20,)), dma((20,)), dma((4,)), dma((4,)), dma((4,)), dma((4,))],
        compiler_params=pltpu.CompilerParams(collective_id=0, has_side_effects=True),
        name="gather_grads",
    )(lg)


def gram_kernel(left, right, old, qt, new, gb, part, acc):
    i = pl.program_id(0)
    rows = new.shape[0]
    lt = left[...].T
    r0 = lax.axis_index("row") * 1024 + i * rows
    c0 = lax.axis_index("col") * 2048
    for h in range(2):
        sl = pl.ds(h * 1024, 1024)
        prod = jnp.dot(lt, right[h], preferred_element_type=jnp.float32)
        ri = lax.broadcasted_iota(jnp.int32, (rows, 1024), 0) + r0
        ci = lax.broadcasted_iota(jnp.int32, (rows, 1024), 1) + (c0 + h * 1024)
        g = decay_rate * old[:, sl] + ((1.0 - decay_rate) / 1024) * prod
        g = g + jnp.where(ri == ci, damping, 0.0).astype(jnp.float32)
        new[:, sl] = g
        g16 = g.astype(jnp.bfloat16)
        gb[:, sl] = g16
        add = jnp.dot(qt[...], g16, preferred_element_type=jnp.float32)

        @pl.when(i == 0)
        def _():
            acc[h] = add

        @pl.when(i > 0)
        def _():
            acc[h] += add

    @pl.when(i == pl.num_programs(0) - 1)
    def _():
        part[...] = acc[...].astype(jnp.bfloat16)


def gram(left, right, old, qt):
    rows = 256
    return pl.pallas_call(
        gram_kernel,
        grid=(1024 // rows,),
        out_shape=(jax.ShapeDtypeStruct((1024, 2048), jnp.float32),
                   jax.ShapeDtypeStruct((1024, 2048), jnp.bfloat16),
                   jax.ShapeDtypeStruct((2, 256, 1024), jnp.bfloat16)),
        in_specs=[pl.BlockSpec((1024, rows), lambda i: (0, i)),
                  pl.BlockSpec((2, 1024, 1024), lambda i: (0, 0, 0), pipeline_mode=pl.Buffered(1)),
                  pl.BlockSpec((rows, 2048), lambda i: (i, 0)),
                  pl.BlockSpec((256, rows), lambda i: (0, i))],
        out_specs=(pl.BlockSpec((rows, 2048), lambda i: (i, 0)),
                   pl.BlockSpec((rows, 2048), lambda i: (i, 0)),
                   pl.BlockSpec((2, 256, 1024), lambda i: (0, 0, 0))),
        scratch_shapes=[pltpu.VMEM((2, 256, 1024), jnp.float32)],
        name="gram_tile",
    )(left, right, old, qt)


def solve_kernel(part, gb, q, x_out, a0, a1, b0, b1, bs0, bs1, wc, wr, msg, got_r, msg2, got_c,
                 s_a, r_a, s_b, r_b, ys, yr, zs, zr, xs, xrecv, ps, pr, loc, s_r, r_r, s_c, r_c):
    row = lax.axis_index("row")
    col = lax.axis_index("col")
    z, y = row // 4, row % 4
    x, core = col // 2, col % 2
    greet(row, col)
    sends = []

    def go(copy):
        copy.start()
        sends.append(copy)
        return copy

    def remote(src, dst, ssem, rsem, dev):
        return pltpu.make_async_remote_copy(src_ref=src, dst_ref=dst, send_sem=ssem, recv_sem=rsem,
                                            device_id=dev, device_id_type=MESH)

    def ymod(k):
        return lax.rem(y + k, 4)

    def zmod(k):
        return lax.rem(z + k, 4)

    def at_y(k):
        return (z * 4 + ymod(k), col)

    def at_z(k):
        return (zmod(k) * 4 + y, col)

    c0, c1 = [], []
    for k in (1, 3, 2):
        c0.append(go(remote(part.at[0, :, ymod(k)], a0.at[k - 1], s_a.at[k], r_a.at[k], at_y(k))))
        c1.append(go(remote(part.at[1, zmod(k)], a1.at[k - 1], s_a.at[4 + k], r_a.at[4 + k], at_z(k))))
    for c in c0:
        c.wait_recv()
    f32 = jnp.float32
    t = part[0, :, y].astype(f32)
    for k in range(3):
        t += a0[k].astype(f32)
    b0[...] = t.astype(jnp.bfloat16)
    d0, d1 = [], []
    for k in (1, 3, 2):
        d0.append(go(remote(b0.at[zmod(k)], bs0.at[k - 1], s_b.at[k], r_b.at[k], at_z(k))))
    for c in c1:
        c.wait_recv()
    t = part[1, z].astype(f32)
    for k in range(3):
        t += a1[k].astype(f32)
    b1[...] = t.astype(jnp.bfloat16)
    for k in (1, 3, 2):
        d1.append(go(remote(b1.at[ymod(k)], bs1.at[k - 1], s_b.at[4 + k], r_b.at[4 + k], at_y(k))))
    lo, hi = (lambda r: r.at[:, pl.ds(0, 512)]), (lambda r: r.at[:, pl.ds(512, 512)])
    yp, ym, zp, zm = at_y(1), at_y(3), at_z(1), at_z(3)
    e0 = Ring(go, lambda k: wc.at[0, z, ymod(k)], lo, hi, ys, yr, 0, yp, ym)
    e1 = Ring(go, lambda k: wc.at[1, zmod(k), y], lo, hi, zs, zr, 0, zp, zm)
    f0 = [Ring(go, lambda k, j=j: wc.at[0, zmod(k), ymod(j)], lo, hi, zs, zr, 4 + 4 * j, zp, zm) for j in range(4)]
    f1 = [Ring(go, lambda k, j=j: wc.at[1, zmod(j), ymod(k)], lo, hi, ys, yr, 4 + 4 * j, yp, ym) for j in range(4)]
    for c in d0:
        c.wait_recv()
    t = b0[z].astype(f32)
    for k in range(3):
        t += bs0[k].astype(f32)
    wc[0, z, y] = t.astype(jnp.bfloat16)
    e0.start()
    f0[0].start()
    for c in d1:
        c.wait_recv()
    t = b1[y].astype(f32)
    for k in range(3):
        t += bs1[k].astype(f32)
    wc[1, z, y] = t.astype(jnp.bfloat16)
    e1.start()
    f1[0].start()
    e0.forward(); e1.forward()
    for j in (3, 1):
        f0[j].start(); f1[j].start()
    f0[0].forward(); f1[0].forward()
    e0.finish(); e1.finish()
    f0[2].start(); f1[2].start()
    for j in (3, 1, 2):
        f0[j].forward(); f1[j].forward()
    for j in range(4):
        f0[j].finish(); f1[j].finish()

    away = lax.rem(x - z + 4, 4)
    mine = core == y // 2
    right_dev = (row, lax.rem(x + 1, 4) * 2 + core)
    left_dev = (row, lax.rem(x + 3, 4) * 2 + core)
    partner = (row, x * 2 + 1 - core)

    def piece(ref, n):
        return ref.at[n // 2, pl.ds((n % 2) * 2, 2)]

    order = (0, 4, 1, 5, 2, 6, 3, 7)

    def along(n, dev):
        return remote(piece(wr, n), piece(wr, n), xs.at[n], xrecv.at[n], dev)

    def across(n):
        return remote(piece(wr, n), piece(wr, n), ps.at[n], pr.at[n], partner)

    @pl.when(mine)
    def _():
        @pl.when(away == 0)
        def _():
            own = pltpu.make_async_copy(wc.at[y % 2], wr, loc)
            own.start()
            own.wait()
            for n in order:
                along(n, right_dev if n < 4 else left_dev).start()
            for n in order:
                across(n).start()
            for n in order:
                along(n, right_dev).wait_send()
                across(n).wait_send()

        @pl.when(away != 0)
        def _():
            for n in order:
                along(n, right_dev).wait_recv()
                last = away == (3 if n < 4 else 1)

                @pl.when(jnp.logical_not(last))
                def _():
                    along(n, right_dev if n < 4 else left_dev).start()
                across(n).start()
            for n in order:
                last = away == (3 if n < 4 else 1)

                @pl.when(jnp.logical_not(last))
                def _():
                    along(n, right_dev).wait_send()
                across(n).wait_send()

    @pl.when(jnp.logical_not(mine))
    def _():
        for n in order:
            across(n).wait_recv()

    wrv = wr[...].reshape(256, 1024)
    v0 = jnp.dot(wrv, gb[:, :1024], preferred_element_type=f32) * wc[0].reshape(256, 1024).astype(f32)
    v1 = jnp.dot(wrv, gb[:, 1024:], preferred_element_type=f32) * wc[1].reshape(256, 1024).astype(f32)
    curve = jnp.broadcast_to(jnp.sum(v0 + v1, axis=1, keepdims=True), (256, 128)).T
    w = wrv.astype(f32).T
    qv = q[...]
    once = jnp.where(col == 0, 1.0, 0.0).astype(f32)
    msg[0:1] = jnp.sum(qv * qv, axis=0, keepdims=True) * once
    msg[1:2] = jnp.sum(qv * w, axis=0, keepdims=True) * once
    msg[2:3] = jnp.sum(w * w, axis=0, keepdims=True) * once
    msg[3:8] = curve[3:8]
    cr = [go(remote(msg, got_r.at[k], s_r.at[k], r_r.at[k], (lax.rem(row + k, 16), col))) for k in range(1, 16)]
    t = msg[...]
    for k, c in enumerate(cr):
        c.wait_recv()
        t += got_r[k + 1]
    msg2[...] = t
    cc = [go(remote(msg2, got_c.at[k], s_c.at[k], r_c.at[k], (row, lax.rem(col + k, 8)))) for k in range(1, 8)]
    for k, c in enumerate(cc):
        c.wait_recv()
        t += got_c[k + 1]
    rr, qw, ww, gg = t[0:1], t[1:2], t[2:3], t[3:4]
    s1 = rr / qw
    new = s1 * s1 * ww - rr
    beta = new / rr
    up = 1.0 + beta
    s2 = new / (up * up * qw - 2.0 * up * s1 * ww + s1 * s1 * gg)
    x_out[...] = (s1 + s2 * up) * qv - (s2 * s1) * w
    for c in sends:
        c.wait_send()


def solve(part, gb, q):
    dma = pltpu.SemaphoreType.DMA
    bf, f32 = jnp.bfloat16, jnp.float32
    vm = pltpu.VMEM
    spec = pl.BlockSpec(memory_space=pltpu.VMEM)
    return pl.pallas_call(
        solve_kernel,
        out_shape=jax.ShapeDtypeStruct((1024, 256), f32),
        in_specs=[spec, spec, spec],
        out_specs=spec,
        scratch_shapes=[vm((3, 4, 16, 1024), bf), vm((3, 4, 16, 1024), bf), vm((4, 16, 1024), bf), vm((4, 16, 1024), bf),
                        vm((3, 16, 1024), bf), vm((3, 16, 1024), bf), vm((2, 4, 4, 16, 1024), bf), vm((4, 4, 16, 1024), bf),
                        vm((8, 256), f32), vm((16, 8, 256), f32), vm((8, 256), f32), vm((8, 8, 256), f32),
                        dma((8,)), dma((8,)), dma((8,)), dma((8,)), dma((20,)), dma((20,)), dma((20,)), dma((20,)),
                        dma((8,)), dma((8,)), dma((8,)), dma((8,)), dma, dma((16,)), dma((16,)), dma((8,)), dma((8,))],
        compiler_params=pltpu.CompilerParams(collective_id=1, has_side_effects=True),
        name="solve",
    )(part, gb, q)


def shards(activations, out_grads, proj_in, proj_out, lengths, gram_old, queries):
    local_count = lengths.shape[0]
    rank = proj_in.shape[1]
    low_in = jnp.dot(activations, proj_in, preferred_element_type=jnp.float32).astype(jnp.bfloat16)
    low_out = jnp.dot(out_grads, proj_out, preferred_element_type=jnp.float32).astype(jnp.bfloat16)
    low_in = low_in.reshape(local_count, SEQ, rank)
    low_out = low_out.reshape(local_count, SEQ, rank)
    valid_mask = jnp.arange(SEQ)[None, :] < lengths[:, None]
    low_out = jnp.where(valid_mask[:, :, None], low_out, jnp.zeros((), jnp.bfloat16))
    grads = jnp.einsum("eto,eti->eoi", low_out, low_in, preferred_element_type=jnp.float32)
    lg = grads.astype(jnp.bfloat16).reshape(local_count, 16, 1024).transpose(1, 0, 2)
    left, right = gather(lg)
    left = left.reshape(1024, 1024)
    right = right.reshape(2, 1024, 1024)
    qt = queries.T.astype(jnp.bfloat16)
    gram_new, gb, part = gram(left, right, gram_old, qt)
    part = part.reshape(2, 4, 4, 16, 1024)
    return gram_new, solve(part, gb, queries)


def solution(mesh):
    in_specs = (
        P(("row", "col"), None),
        P(("row", "col"), None),
        P(),
        P(),
        P(("row", "col")),
        P("row", "col"),
        P("row", None),
    )
    out_specs = (P("row", "col"), P("row", None))
    return jax.shard_map(shards, mesh=mesh, in_specs=in_specs, out_specs=out_specs, check_vma=False)
```

```python
import functools

import jax
import jax.numpy as jnp
from jax import lax
from jax.experimental import pallas as pl
from jax.experimental.pallas import tpu as pltpu
from jax.sharding import PartitionSpec as P

MESH = pl.DeviceIdType.MESH
SEQ = 32
ITERS = 2
decay_rate = 0.5
damping = 1.0
HBM = pl.ANY


class Ring:
    def __init__(self, go, slot, lo, hi, ss, rs, base, plus, minus):
        self.go, self.slot, self.lo, self.hi = go, slot, lo, hi
        self.ss, self.rs, self.base = ss, rs, base
        self.plus, self.minus = plus, minus

    def copy(self, ref, k, dev):
        return self.go(pltpu.make_async_remote_copy(
            src_ref=ref, dst_ref=ref, send_sem=self.ss.at[self.base + k], recv_sem=self.rs.at[self.base + k],
            device_id=dev, device_id_type=MESH))

    def start(self):
        own = self.slot(0)
        self.f0 = self.copy(own, 0, self.plus)
        self.f1 = self.copy(own, 1, self.minus)

    def forward(self):
        self.f0.wait_recv()
        self.h0 = self.copy(self.lo(self.slot(3)), 2, self.plus)
        self.f1.wait_recv()
        self.h1 = self.copy(self.hi(self.slot(1)), 3, self.minus)

    def finish(self):
        self.h0.wait_recv()
        self.h1.wait_recv()


def greet(row, col):
    barrier = pltpu.get_barrier_semaphore()
    for k in range(1, 8):
        pl.semaphore_signal(barrier, inc=1, device_id=(row, lax.rem(col + k, 8)), device_id_type=MESH)
    for k in range(1, 16):
        pl.semaphore_signal(barrier, inc=1, device_id=(lax.rem(row + k, 16), col), device_id_type=MESH)
    pl.semaphore_wait(barrier, 22)


def gather_kernel(lg, q, left_t, right, qt, left, loc_sem, c_send, c_recv, r_send, r_recv,
                  ya_send, ya_recv, za_send, za_recv, x_send, x_recv, p_send, p_recv):
    row = lax.axis_index("row")
    col = lax.axis_index("col")
    z, y = row // 4, row % 4
    x, core = col // 2, col % 2

    def at_col(k):
        return lax.rem(col + k, 8)

    def at_row(k):
        return lax.rem(row + k, 16)

    greet(row, col)

    def remote(src, dst, ssem, rsem, dev):
        return pltpu.make_async_remote_copy(src_ref=src, dst_ref=dst, send_sem=ssem, recv_sem=rsem,
                                            device_id=dev, device_id_type=MESH)

    sends = []

    def go(copy):
        copy.start()
        sends.append(copy)
        return copy

    own_right = pltpu.make_async_copy(lg.at[pl.ds(2 * col, 2)], right.at[:, z, y, col], loc_sem.at[0])
    own_right.start()
    own_left = pltpu.make_async_copy(lg.at[row], left.at[z, y, col], loc_sem.at[1])
    own_left.start()
    stage_c = []
    for k in (2, 6, 1, 7, 3, 5, 4):
        to = at_col(k)
        stage_c.append(go(remote(lg.at[pl.ds(2 * to, 2)], right.at[:, z, y, col],
                                 c_send.at[k], c_recv.at[k], (row, to))))
    stage_r = []
    for k in range(1, 16):
        to = at_row(k)
        stage_r.append(go(remote(lg.at[to], left.at[z, y, col], r_send.at[k], r_recv.at[k], (to, col))))

    yp, ym = z * 4 + lax.rem(y + 1, 4), z * 4 + lax.rem(y + 3, 4)
    zp, zm = lax.rem(z + 1, 4) * 4 + y, lax.rem(z + 3, 4) * 4 + y
    xp, xm = lax.rem(x + 1, 4) * 2 + core, lax.rem(x + 3, 4) * 2 + core
    partner = x * 2 + (1 - core)

    def ymod(k):
        return lax.rem(y + k, 4)

    def zmod(k):
        return lax.rem(z + k, 4)

    lo5, hi5 = (lambda r: r.at[pl.ds(0, 4)]), (lambda r: r.at[pl.ds(4, 4)])
    a0 = Ring(go, lambda k: right.at[0, z, ymod(k)], lo5, hi5, ya_send, ya_recv, 0, (yp, col), (ym, col))
    a1 = Ring(go, lambda k: right.at[1, zmod(k), y], lo5, hi5, za_send, za_recv, 0, (zp, col), (zm, col))
    b0 = [Ring(go, lambda k, j=j: right.at[0, zmod(k), ymod(j)], lo5, hi5, za_send, za_recv, 4 + 4 * j, (zp, col), (zm, col))
          for j in range(4)]
    b1 = [Ring(go, lambda k, j=j: right.at[1, zmod(j), ymod(k)], lo5, hi5, ya_send, ya_recv, 4 + 4 * j, (yp, col), (ym, col))
          for j in range(4)]
    xr = Ring(go, lambda k: left.at[:, :, lax.rem(x + k, 4) * 2 + core], lambda r: r.at[pl.ds(0, 2)], lambda r: r.at[pl.ds(2, 2)],
              x_send, x_recv, 0, (row, xp), (row, xm))

    def to_partner(k):
        c = left.at[:, :, lax.rem(x + k, 4) * 2 + core]
        return go(remote(c, c, p_send.at[k], p_recv.at[k], (row, partner)))

    own_right.wait()
    own_left.wait()
    for c in stage_c:
        c.wait_recv()
    a0.start(); a1.start()
    b0[0].start(); b1[0].start()
    for c in stage_r:
        c.wait_recv()
    xr.start()
    pp = [to_partner(0)]
    a0.forward(); a1.forward()
    for j in (3, 1):
        b0[j].start(); b1[j].start()
    xr.forward()
    pp += [to_partner(3), to_partner(1)]
    b0[0].forward(); b1[0].forward()
    a0.finish(); a1.finish()
    b0[2].start(); b1[2].start()
    xr.finish()
    pp += [to_partner(2)]
    for j in (3, 1, 2):
        b0[j].forward(); b1[j].forward()
    for c in pp:
        c.wait_recv()
    for n in range(8):
        pair = left[n // 2, pl.ds(2 * (n % 2), 2)].astype(jnp.float32).reshape(128, 1024)
        left_t[:, pl.ds(n * 128, 128)] = pair.T.astype(jnp.bfloat16)
    qt[...] = q[...].T.astype(jnp.bfloat16)
    for j in range(4):
        b0[j].finish(); b1[j].finish()
    for c in sends:
        c.wait_send()


def gather(lg, q):
    dma = pltpu.SemaphoreType.DMA
    return pl.pallas_call(
        gather_kernel,
        out_shape=(jax.ShapeDtypeStruct((1024, 1024), jnp.bfloat16),
                   jax.ShapeDtypeStruct((2, 4, 4, 8, 8, 1024), jnp.bfloat16),
                   jax.ShapeDtypeStruct((256, 1024), jnp.bfloat16)),
        in_specs=[pl.BlockSpec(memory_space=pltpu.VMEM)] * 2,
        out_specs=(pl.BlockSpec(memory_space=pltpu.VMEM), pl.BlockSpec(memory_space=HBM),
                   pl.BlockSpec(memory_space=pltpu.VMEM)),
        scratch_shapes=[pltpu.VMEM((4, 4, 8, 8, 1024), jnp.bfloat16), dma((2,)), dma((8,)), dma((8,)), dma((16,)), dma((16,)),
                        dma((20,)), dma((20,)), dma((20,)), dma((20,)), dma((4,)), dma((4,)), dma((4,)), dma((4,))],
        compiler_params=pltpu.CompilerParams(collective_id=0, has_side_effects=True),
        name="gather_grads",
    )(lg, q)


def gram_kernel(left_t, right, old, qt, new, gb, part):
    j = pl.program_id(0)
    cols = new.shape[1]
    f32 = jnp.float32
    prod = jnp.dot(left_t[...], right[0], preferred_element_type=f32)
    off = lax.axis_index("col") * 2048 + j * cols - lax.axis_index("row") * 1024
    ri = lax.broadcasted_iota(jnp.int32, prod.shape, 0)
    ci = lax.broadcasted_iota(jnp.int32, prod.shape, 1) + off
    g = decay_rate * old[...] + ((1.0 - decay_rate) / 1024) * prod
    g = g + jnp.where(ri == ci, damping, 0.0).astype(f32)
    new[...] = g
    g16 = g.astype(jnp.bfloat16)
    gb[...] = g16
    part[0] = jnp.dot(qt[...], g16, preferred_element_type=f32).astype(jnp.bfloat16)


def gram(left_t, right, old, qt):
    cols = 256
    n = 1024 // cols
    return pl.pallas_call(
        gram_kernel,
        grid=(2048 // cols,),
        out_shape=(jax.ShapeDtypeStruct((1024, 2048), jnp.float32),
                   jax.ShapeDtypeStruct((1024, 2048), jnp.bfloat16),
                   jax.ShapeDtypeStruct((2, 256, 1024), jnp.bfloat16)),
        in_specs=[pl.BlockSpec((1024, 1024), lambda j: (0, 0), pipeline_mode=pl.Buffered(1)),
                  pl.BlockSpec((1, 1024, cols), lambda j: (j // n, 0, j % n)),
                  pl.BlockSpec((1024, cols), lambda j: (0, j)),
                  pl.BlockSpec((256, 1024), lambda j: (0, 0), pipeline_mode=pl.Buffered(1))],
        out_specs=(pl.BlockSpec((1024, cols), lambda j: (0, j)),
                   pl.BlockSpec((1024, cols), lambda j: (0, j)),
                   pl.BlockSpec((1, 256, cols), lambda j: (j // n, 0, j % n))),
        name="gram_tile",
    )(left_t, right, old, qt)


def solve_kernel(part, gb, q, x_out, a_far, a_got, a_sum, b_sum, b_got, wc, wr, msg, got_r, msg2, got_c,
                 s_a, r_a, s_b, r_b, ys, yr, zs, zr, xs, xrecv, ps, pr, s_r, r_r, s_c, r_c):
    row = lax.axis_index("row")
    col = lax.axis_index("col")
    z, y = row // 4, row % 4
    x, core = col // 2, col % 2
    greet(row, col)
    sends = []

    def go(copy):
        copy.start()
        sends.append(copy)
        return copy

    def remote(src, dst, ssem, rsem, dev):
        return pltpu.make_async_remote_copy(src_ref=src, dst_ref=dst, send_sem=ssem, recv_sem=rsem,
                                            device_id=dev, device_id_type=MESH)

    def ymod(k):
        return lax.rem(y + k, 4)

    def zmod(k):
        return lax.rem(z + k, 4)

    def at_y(k):
        return (z * 4 + ymod(k), col)

    def at_z(k):
        return (zmod(k) * 4 + y, col)

    f32, bf = jnp.float32, jnp.bfloat16
    yp, ym, zp, zm = at_y(1), at_y(3), at_z(1), at_z(3)
    lo, hi = pl.ds(0, 512), pl.ds(512, 512)

    def chunk(h, k):
        return part.at[0, :, ymod(k)] if h == 0 else part.at[1, zmod(k)]

    near = ((yp, ym), (zp, zm))
    far, plain = [], []
    for h in range(2):
        plus, minus = near[h]
        far.append((go(remote(chunk(h, 2).at[:, :, lo], a_far.at[h, 0], s_a.at[h, 0], r_a.at[h, 0], plus)),
                    go(remote(chunk(h, 2).at[:, :, hi], a_far.at[h, 1], s_a.at[h, 1], r_a.at[h, 1], minus))))
    for h in range(2):
        plus, minus = near[h]
        plain.append((go(remote(chunk(h, 1).at[:, :, hi], a_got.at[h, 0, 1], s_a.at[h, 2], r_a.at[h, 2], plus)),
                      go(remote(chunk(h, 3).at[:, :, lo], a_got.at[h, 1, 0], s_a.at[h, 3], r_a.at[h, 3], minus))))
    joined = []
    for h in range(2):
        plus, minus = near[h]
        far[h][0].wait_recv()
        a_sum[h, 0] = (chunk(h, 1)[:, :, lo].astype(f32) + a_far[h, 0].astype(f32)).astype(bf)
        up = go(remote(a_sum.at[h, 0], a_got.at[h, 0, 0], s_a.at[h, 4], r_a.at[h, 4], plus))
        far[h][1].wait_recv()
        a_sum[h, 1] = (chunk(h, 3)[:, :, hi].astype(f32) + a_far[h, 1].astype(f32)).astype(bf)
        joined.append((up, go(remote(a_sum.at[h, 1], a_got.at[h, 1, 1], s_a.at[h, 5], r_a.at[h, 5], minus))))
    second = []
    for h in range(2):
        for c in plain[h] + joined[h]:
            c.wait_recv()
        for n, lanes in enumerate((lo, hi)):
            t = chunk(h, 0)[:, :, lanes].astype(f32) + a_got[h, 0, n].astype(f32) + a_got[h, 1, n].astype(f32)
            b_sum[h, :, :, lanes] = t.astype(bf)
        second.append([])
        for k in (1, 3, 2):
            to, dev = (zmod(k), at_z(k)) if h == 0 else (ymod(k), at_y(k))
            second[h].append(go(remote(b_sum.at[h, to], b_got.at[h, k - 1], s_b.at[h, k], r_b.at[h, k], dev)))

    lol, hil = (lambda r: r.at[:, lo]), (lambda r: r.at[:, hi])
    e0 = Ring(go, lambda k: wc.at[0, z, ymod(k)], lol, hil, ys, yr, 0, yp, ym)
    e1 = Ring(go, lambda k: wc.at[1, zmod(k), y], lol, hil, zs, zr, 0, zp, zm)
    f0 = [Ring(go, lambda k, j=j: wc.at[0, zmod(k), ymod(j)], lol, hil, zs, zr, 4 + 4 * j, zp, zm) for j in range(4)]
    f1 = [Ring(go, lambda k, j=j: wc.at[1, zmod(j), ymod(k)], lol, hil, ys, yr, 4 + 4 * j, yp, ym) for j in range(4)]
    half = y % 2
    mine = core == y // 2
    root = jnp.logical_and(mine, x == z)
    partner = (row, x * 2 + 1 - core)
    pieces = []

    def group(late, early):
        dz = jnp.where(half == 0, late, early)
        dy = jnp.where(half == 0, early, late)
        return zmod(dz), ymod(dy)

    def along(n, k):
        gz, gy = pieces[n]
        return remote(wc.at[half, gz, gy], wr.at[gz, gy], xs.at[n, k], xrecv.at[n], (row, lax.rem(x + k, 4) * 2 + core))

    def across(n, src):
        gz, gy = pieces[n]
        return remote(src.at[gz, gy], wr.at[gz, gy], ps.at[n], pr.at[n], partner)

    def publish(*which):
        first = len(pieces)
        pieces.extend(group(*w) for w in which)

        @pl.when(root)
        def _():
            for n in range(first, len(pieces)):
                for k in (1, 3, 2):
                    along(n, k).start()
                across(n, wc.at[half]).start()

    for h in range(2):
        for c in second[h]:
            c.wait_recv()
        t = b_sum[h, z if h == 0 else y].astype(f32)
        for k in range(3):
            t += b_got[h, k].astype(f32)
        wc[h, z, y] = t.astype(bf)
        (e0, e1)[h].start()
        (f0, f1)[h][0].start()
    publish((0, 0))
    e0.forward(); e1.forward()
    for j in (3, 1):
        f0[j].start(); f1[j].start()
    publish((0, 3), (0, 1))
    f0[0].forward(); f1[0].forward()
    e0.finish(); e1.finish()
    f0[2].start(); f1[2].start()
    publish((3, 0), (1, 0), (0, 2))
    for j in (3, 1, 2):
        f0[j].forward(); f1[j].forward()
        publish((3, j), (1, j))
    for j in (0, 3, 1, 2):
        f0[j].finish(); f1[j].finish()
        publish((2, j))

    @pl.when(root)
    def _():
        wr[...] = wc[half]
        for n in range(16):
            for k in (1, 3, 2):
                along(n, k).wait_send()
            across(n, wc.at[half]).wait_send()

    @pl.when(jnp.logical_and(mine, x != z))
    def _():
        for n in range(16):
            along(n, 1).wait_recv()
            across(n, wr).start()
        for n in range(16):
            across(n, wr).wait_send()

    @pl.when(jnp.logical_not(mine))
    def _():
        for n in range(16):
            across(n, wr).wait_recv()

    wrv = wr[...].reshape(256, 1024)
    v0 = jnp.dot(wrv, gb[:, :1024], preferred_element_type=f32) * wc[0].reshape(256, 1024).astype(f32)
    v1 = jnp.dot(wrv, gb[:, 1024:], preferred_element_type=f32) * wc[1].reshape(256, 1024).astype(f32)
    curve = jnp.broadcast_to(jnp.sum(v0 + v1, axis=1, keepdims=True), (256, 128)).T
    w = wrv.astype(f32).T
    qv = q[...]
    once = jnp.where(col == 0, 1.0, 0.0).astype(f32)
    msg[0:1] = jnp.sum(qv * qv, axis=0, keepdims=True) * once
    msg[1:2] = jnp.sum(qv * w, axis=0, keepdims=True) * once
    msg[2:3] = jnp.sum(w * w, axis=0, keepdims=True) * once
    msg[3:4] = curve[3:4]
    cr = [go(remote(msg, got_r.at[k], s_r.at[k], r_r.at[k], (lax.rem(row + k, 16), col))) for k in range(1, 16)]
    t = msg[...]
    for k, c in enumerate(cr):
        c.wait_recv()
        t += got_r[k + 1]
    msg2[...] = t
    cc = [go(remote(msg2, got_c.at[k], s_c.at[k], r_c.at[k], (row, lax.rem(col + k, 8)))) for k in range(1, 8)]
    for k, c in enumerate(cc):
        c.wait_recv()
        t += got_c[k + 1]
    rr, qw, ww, gg = t[0:1], t[1:2], t[2:3], t[3:4]
    s1 = rr / qw
    new = s1 * s1 * ww - rr
    beta = new / rr
    up = 1.0 + beta
    s2 = new / (up * up * qw - 2.0 * up * s1 * ww + s1 * s1 * gg)
    x_out[...] = (s1 + s2 * up) * qv - (s2 * s1) * w
    for c in sends:
        c.wait_send()


def solve(part, gb, q):
    dma = pltpu.SemaphoreType.DMA
    bf, f32 = jnp.bfloat16, jnp.float32
    vm = pltpu.VMEM
    spec = pl.BlockSpec(memory_space=pltpu.VMEM)
    return pl.pallas_call(
        solve_kernel,
        out_shape=jax.ShapeDtypeStruct((1024, 256), f32),
        in_specs=[spec, spec, spec],
        out_specs=spec,
        scratch_shapes=[vm((2, 2, 4, 16, 512), bf), vm((2, 2, 2, 4, 16, 512), bf), vm((2, 2, 4, 16, 512), bf), vm((2, 4, 16, 1024), bf),
                        vm((2, 3, 16, 1024), bf), vm((2, 4, 4, 16, 1024), bf), vm((4, 4, 16, 1024), bf),
                        vm((4, 256), f32), vm((16, 4, 256), f32), vm((4, 256), f32), vm((8, 4, 256), f32),
                        dma((2, 6)), dma((2, 6)), dma((2, 4)), dma((2, 4)), dma((20,)), dma((20,)), dma((20,)), dma((20,)),
                        dma((16, 4)), dma((16,)), dma((16,)), dma((16,)), dma((16,)), dma((16,)), dma((8,)), dma((8,))],
        compiler_params=pltpu.CompilerParams(collective_id=1, has_side_effects=True),
        name="solve",
    )(part, gb, q)


def shards(activations, out_grads, proj_in, proj_out, lengths, gram_old, queries):
    local_count = lengths.shape[0]
    rank = proj_in.shape[1]
    low_in = jnp.dot(activations, proj_in, preferred_element_type=jnp.float32).astype(jnp.bfloat16)
    low_out = jnp.dot(out_grads, proj_out, preferred_element_type=jnp.float32).astype(jnp.bfloat16)
    low_in = low_in.reshape(local_count, SEQ, rank)
    low_out = low_out.reshape(local_count, SEQ, rank)
    valid_mask = jnp.arange(SEQ)[None, :] < lengths[:, None]
    low_out = jnp.where(valid_mask[:, :, None], low_out, jnp.zeros((), jnp.bfloat16))
    grads = jnp.einsum("eto,eti->eoi", low_out, low_in, preferred_element_type=jnp.float32)
    lg = grads.astype(jnp.bfloat16).reshape(local_count, 16, 1024).transpose(1, 0, 2)
    left, right, qt = gather(lg, queries)
    right = right.reshape(2, 1024, 1024)
    gram_new, gb, part = gram(left, right, gram_old, qt)
    part = part.reshape(2, 4, 4, 16, 1024)
    return gram_new, solve(part, gb, queries)


def solution(mesh):
    in_specs = (
        P(("row", "col"), None),
        P(("row", "col"), None),
        P(),
        P(),
        P(("row", "col")),
        P("row", "col"),
        P("row", None),
    )
    out_specs = (P("row", "col"), P("row", None))
    return jax.shard_map(shards, mesh=mesh, in_specs=in_specs, out_specs=out_specs, check_vma=False)
```

```python
import functools

import jax
import jax.numpy as jnp
from jax import lax
from jax.experimental import pallas as pl
from jax.experimental.pallas import tpu as pltpu
from jax.sharding import PartitionSpec as P

MESH = pl.DeviceIdType.MESH
SEQ = 32
ITERS = 2
decay_rate = 0.5
damping = 1.0
HBM = pl.ANY


class Ring:
    def __init__(self, go, slot, lo, hi, ss, rs, base, plus, minus):
        self.go, self.slot, self.lo, self.hi = go, slot, lo, hi
        self.ss, self.rs, self.base = ss, rs, base
        self.plus, self.minus = plus, minus

    def copy(self, ref, k, dev):
        return self.go(pltpu.make_async_remote_copy(
            src_ref=ref, dst_ref=ref, send_sem=self.ss.at[self.base + k], recv_sem=self.rs.at[self.base + k],
            device_id=dev, device_id_type=MESH))

    def start(self):
        own = self.slot(0)
        self.f0 = self.copy(own, 0, self.plus)
        self.f1 = self.copy(own, 1, self.minus)

    def forward(self):
        self.f0.wait_recv()
        self.h0 = self.copy(self.lo(self.slot(3)), 2, self.plus)
        self.f1.wait_recv()
        self.h1 = self.copy(self.hi(self.slot(1)), 3, self.minus)

    def finish(self):
        self.h0.wait_recv()
        self.h1.wait_recv()


def greet(row, col):
    barrier = pltpu.get_barrier_semaphore()
    for k in range(1, 8):
        pl.semaphore_signal(barrier, inc=1, device_id=(row, lax.rem(col + k, 8)), device_id_type=MESH)
    for k in range(1, 16):
        pl.semaphore_signal(barrier, inc=1, device_id=(lax.rem(row + k, 16), col), device_id_type=MESH)
    return barrier


def kernel(act, og, p_in, p_out, lens, old_hbm, q_hbm, new, x_out,
           act_v, og_v, pin_v, pout_v, old, q, lg, left, right, qt, acc, gb, part,
           a_far, a_got, a_sum, b_sum, b_got, wc, wr, msg, got_r, msg2, got_c,
           in_sem, out_sem, loc_sem, c_send, c_recv, r_send, r_recv, ya_send, ya_recv, za_send, za_recv,
           x_send, x_recv, p_send, p_recv,
           s_a, r_a, s_b, r_b, ys, yr, zs, zr, xs, xrecv, ps, pr, s_r, r_r, s_c, r_c):
    f32, bf = jnp.float32, jnp.bfloat16
    row = lax.axis_index("row")
    col = lax.axis_index("col")
    z, y = row // 4, row % 4
    x, core = col // 2, col % 2
    barrier = greet(row, col)
    loads = [pltpu.make_async_copy(a, b, in_sem.at[n]) for n, (a, b) in enumerate(
        ((p_out, pout_v), (og, og_v), (p_in, pin_v), (act, act_v), (q_hbm, q), (old_hbm, old)))]
    for c in loads[:4]:
        c.start()
    sends = []

    def go(copy):
        copy.start()
        sends.append(copy)
        return copy

    def remote(src, dst, ssem, rsem, dev):
        return pltpu.make_async_remote_copy(src_ref=src, dst_ref=dst, send_sem=ssem, recv_sem=rsem,
                                            device_id=dev, device_id_type=MESH)

    def ymod(k):
        return lax.rem(y + k, 4)

    def zmod(k):
        return lax.rem(z + k, 4)

    def at_y(k):
        return (z * 4 + ymod(k), col)

    def at_z(k):
        return (zmod(k) * 4 + y, col)

    loads[0].wait()
    loads[1].wait()
    low_out = jnp.dot(og_v[...], pout_v[...], preferred_element_type=f32).astype(bf).astype(f32).T
    ex = lax.broadcasted_iota(jnp.int32, (8, 256), 0)
    slot = lax.broadcasted_iota(jnp.int32, (8, 256), 1) - SEQ * ex
    count = jnp.zeros((8, 256), jnp.int32)
    for e in range(8):
        count = jnp.where(ex == e, lens[e], count)
    valid = jnp.logical_and(slot >= 0, slot < jnp.minimum(count, SEQ))
    spread = jnp.where(valid[None], low_out[:, None, :], 0.0).reshape(1024, 256).astype(bf)
    loads[2].wait()
    loads[3].wait()
    low_in = jnp.dot(act_v[...], pin_v[...], preferred_element_type=f32).astype(bf)
    grads = jnp.dot(spread, low_in, preferred_element_type=f32).reshape(16, 8, 8, 128)
    for j in range(8):
        lg[:, :, pl.ds(j * 128, 128)] = grads[:, j].astype(bf)
    pl.semaphore_wait(barrier, 22)

    own_right = pltpu.make_async_copy(lg.at[pl.ds(2 * col, 2)], right.at[:, z, y, col], loc_sem.at[0])
    own_right.start()
    own_left = pltpu.make_async_copy(lg.at[row], left.at[z, y, col], loc_sem.at[1])
    own_left.start()
    stage_c, stage_r = [], []
    for k in (2, 6, 1, 7, 3, 5, 4):
        to = lax.rem(col + k, 8)
        stage_c.append(go(remote(lg.at[pl.ds(2 * to, 2)], right.at[:, z, y, col],
                                 c_send.at[k], c_recv.at[k], (row, to))))
    for k in range(1, 16):
        to = lax.rem(row + k, 16)
        stage_r.append(go(remote(lg.at[to], left.at[z, y, col], r_send.at[k], r_recv.at[k], (to, col))))
    loads[4].start()
    loads[5].start()

    yp, ym, zp, zm = at_y(1), at_y(3), at_z(1), at_z(3)
    xp = (row, lax.rem(x + 1, 4) * 2 + core)
    xm = (row, lax.rem(x + 3, 4) * 2 + core)
    partner = (row, x * 2 + 1 - core)
    lo5, hi5 = (lambda r: r.at[pl.ds(0, 4)]), (lambda r: r.at[pl.ds(4, 4)])
    a0 = Ring(go, lambda k: right.at[0, z, ymod(k)], lo5, hi5, ya_send, ya_recv, 0, yp, ym)
    a1 = Ring(go, lambda k: right.at[1, zmod(k), y], lo5, hi5, za_send, za_recv, 0, zp, zm)
    b0 = [Ring(go, lambda k, j=j: right.at[0, zmod(k), ymod(j)], lo5, hi5, za_send, za_recv, 4 + 4 * j, zp, zm)
          for j in range(4)]
    b1 = [Ring(go, lambda k, j=j: right.at[1, zmod(j), ymod(k)], lo5, hi5, ya_send, ya_recv, 4 + 4 * j, yp, ym)
          for j in range(4)]
    xr = Ring(go, lambda k: left.at[:, :, lax.rem(x + k, 4) * 2 + core], lambda r: r.at[pl.ds(0, 2)],
              lambda r: r.at[pl.ds(2, 2)], x_send, x_recv, 0, xp, xm)

    def to_partner(k):
        c = left.at[:, :, lax.rem(x + k, 4) * 2 + core]
        return go(remote(c, c, p_send.at[k], p_recv.at[k], partner))

    own_right.wait()
    own_left.wait()
    for c in stage_c:
        c.wait_recv()
    a0.start(); a1.start()
    b0[0].start(); b1[0].start()
    for c in stage_r:
        c.wait_recv()
    xr.start()
    pp = [to_partner(0)]
    a0.forward(); a1.forward()
    for j in (3, 1):
        b0[j].start(); b1[j].start()
    xr.forward()
    pp += [to_partner(3), to_partner(1)]
    b0[0].forward(); b1[0].forward()
    a0.finish(); a1.finish()
    b0[2].start(); b1[2].start()
    xr.finish()
    pp += [to_partner(2)]
    loads[4].wait()
    qt[...] = q[...].T.astype(bf)
    for c in pp:
        c.wait_recv()

    def left_of(h, j):
        block = left[:, ymod(j)] if h == 0 else left[zmod(j)]
        return block.astype(f32).reshape(256, 1024).T.astype(bf)

    def right_of(h, j):
        block = right[0, :, ymod(j)] if h == 0 else right[1, zmod(j)]
        return block.astype(f32).reshape(256, 1024).astype(bf)

    def multiply(h, j):
        add = jnp.dot(left_of(h, j), right_of(h, j), preferred_element_type=f32)
        acc[h] = add if j == 0 else acc[h] + add

    for j in (3, 1):
        b0[j].forward(); b1[j].forward()
    b0[0].finish(); b1[0].finish()
    multiply(0, 0)
    b0[2].forward(); b1[2].forward()
    multiply(1, 0)
    for j in (3, 1):
        b0[j].finish(); b1[j].finish()
        multiply(0, j); multiply(1, j)
    last = [left_of(h, 2) for h in range(2)]
    b0[2].finish(); b1[2].finish()
    loads[5].wait()

    lo, hi = pl.ds(0, 512), pl.ds(512, 512)

    def chunk(h, k):
        return part.at[0, :, ymod(k)] if h == 0 else part.at[1, zmod(k)]

    near = ((yp, ym), (zp, zm))
    far, plain, out = [], [], []
    for h in range(2):
        plus, minus = near[h]
        lanes = pl.ds(h * 1024, 1024)
        prod = acc[h] + jnp.dot(last[h], right_of(h, 2), preferred_element_type=f32)
        ri = lax.broadcasted_iota(jnp.int32, (1024, 1024), 0) + row * 1024
        ci = lax.broadcasted_iota(jnp.int32, (1024, 1024), 1) + (col * 2048 + h * 1024)
        g = decay_rate * old[:, lanes] + ((1.0 - decay_rate) / 1024) * prod
        g = g + jnp.where(ri == ci, damping, 0.0).astype(f32)
        acc[h] = g
        gb[h] = g.astype(bf)
        pt = jnp.dot(qt[...], gb[h], preferred_element_type=f32)
        part[h] = pt.astype(bf).reshape(4, 4, 16, 1024)
        far.append((go(remote(chunk(h, 2).at[:, :, lo], a_far.at[h, 0], s_a.at[h, 0], r_a.at[h, 0], plus)),
                    go(remote(chunk(h, 2).at[:, :, hi], a_far.at[h, 1], s_a.at[h, 1], r_a.at[h, 1], minus))))
        plain.append((go(remote(chunk(h, 1).at[:, :, hi], a_got.at[h, 0, 1], s_a.at[h, 2], r_a.at[h, 2], plus)),
                      go(remote(chunk(h, 3).at[:, :, lo], a_got.at[h, 1, 0], s_a.at[h, 3], r_a.at[h, 3], minus))))
        out.append(pltpu.make_async_copy(acc.at[h], new.at[:, lanes], out_sem.at[h]))
        out[h].start()
    joined = []
    for h in range(2):
        plus, minus = near[h]
        far[h][0].wait_recv()
        a_sum[h, 0] = (chunk(h, 1)[:, :, lo].astype(f32) + a_far[h, 0].astype(f32)).astype(bf)
        up = go(remote(a_sum.at[h, 0], a_got.at[h, 0, 0], s_a.at[h, 4], r_a.at[h, 4], plus))
        far[h][1].wait_recv()
        a_sum[h, 1] = (chunk(h, 3)[:, :, hi].astype(f32) + a_far[h, 1].astype(f32)).astype(bf)
        joined.append((up, go(remote(a_sum.at[h, 1], a_got.at[h, 1, 1], s_a.at[h, 5], r_a.at[h, 5], minus))))
    second = []
    for h in range(2):
        for c in plain[h] + joined[h]:
            c.wait_recv()
        for n, lanes in enumerate((lo, hi)):
            t = chunk(h, 0)[:, :, lanes].astype(f32) + a_got[h, 0, n].astype(f32) + a_got[h, 1, n].astype(f32)
            b_sum[h, :, :, lanes] = t.astype(bf)
        second.append([])
        for k in (1, 3, 2):
            to, dev = (zmod(k), at_z(k)) if h == 0 else (ymod(k), at_y(k))
            second[h].append(go(remote(b_sum.at[h, to], b_got.at[h, k - 1], s_b.at[h, k], r_b.at[h, k], dev)))

    lol, hil = (lambda r: r.at[:, lo]), (lambda r: r.at[:, hi])
    e0 = Ring(go, lambda k: wc.at[0, z, ymod(k)], lol, hil, ys, yr, 0, yp, ym)
    e1 = Ring(go, lambda k: wc.at[1, zmod(k), y], lol, hil, zs, zr, 0, zp, zm)
    f0 = [Ring(go, lambda k, j=j: wc.at[0, zmod(k), ymod(j)], lol, hil, zs, zr, 4 + 4 * j, zp, zm) for j in range(4)]
    f1 = [Ring(go, lambda k, j=j: wc.at[1, zmod(j), ymod(k)], lol, hil, ys, yr, 4 + 4 * j, yp, ym) for j in range(4)]
    half = y % 2
    mine = core == y // 2
    root = jnp.logical_and(mine, x == z)
    pieces = []

    def group(late, early):
        dz = jnp.where(half == 0, late, early)
        dy = jnp.where(half == 0, early, late)
        return zmod(dz), ymod(dy)

    def along(n, k):
        gz, gy = pieces[n]
        return remote(wc.at[half, gz, gy], wr.at[gz, gy], xs.at[n, k], xrecv.at[n], (row, lax.rem(x + k, 4) * 2 + core))

    def across(n, src):
        gz, gy = pieces[n]
        return remote(src.at[gz, gy], wr.at[gz, gy], ps.at[n], pr.at[n], partner)

    def publish(*which):
        first = len(pieces)
        pieces.extend(group(*w) for w in which)

        @pl.when(root)
        def _():
            for n in range(first, len(pieces)):
                for k in (1, 3, 2):
                    along(n, k).start()
                across(n, wc.at[half]).start()

    for h in range(2):
        for c in second[h]:
            c.wait_recv()
        t = b_sum[h, z if h == 0 else y].astype(f32)
        for k in range(3):
            t += b_got[h, k].astype(f32)
        wc[h, z, y] = t.astype(bf)
        (e0, e1)[h].start()
        (f0, f1)[h][0].start()
    publish((0, 0))
    e0.forward(); e1.forward()
    for j in (3, 1):
        f0[j].start(); f1[j].start()
    publish((0, 3), (0, 1))
    f0[0].forward(); f1[0].forward()
    e0.finish(); e1.finish()
    f0[2].start(); f1[2].start()
    publish((3, 0), (1, 0), (0, 2))
    for j in (3, 1, 2):
        f0[j].forward(); f1[j].forward()
        publish((3, j), (1, j))
    for j in (0, 3, 1, 2):
        f0[j].finish(); f1[j].finish()
        publish((2, j))

    @pl.when(root)
    def _():
        wr[...] = wc[half]
        for n in range(16):
            for k in (1, 3, 2):
                along(n, k).wait_send()
            across(n, wc.at[half]).wait_send()

    @pl.when(jnp.logical_and(mine, x != z))
    def _():
        for n in range(16):
            along(n, 1).wait_recv()
            across(n, wr).start()
        for n in range(16):
            across(n, wr).wait_send()

    @pl.when(jnp.logical_not(mine))
    def _():
        for n in range(16):
            across(n, wr).wait_recv()

    wrv = wr[...].reshape(256, 1024)
    v0 = jnp.dot(wrv, gb[0], preferred_element_type=f32) * wc[0].reshape(256, 1024).astype(f32)
    v1 = jnp.dot(wrv, gb[1], preferred_element_type=f32) * wc[1].reshape(256, 1024).astype(f32)
    curve = jnp.broadcast_to(jnp.sum(v0 + v1, axis=1, keepdims=True), (256, 128)).T
    w = wrv.astype(f32).T
    qv = q[...]
    once = jnp.where(col == 0, 1.0, 0.0).astype(f32)
    msg[0:1] = jnp.sum(qv * qv, axis=0, keepdims=True) * once
    msg[1:2] = jnp.sum(qv * w, axis=0, keepdims=True) * once
    msg[2:3] = jnp.sum(w * w, axis=0, keepdims=True) * once
    msg[3:4] = curve[3:4]
    cr = [go(remote(msg, got_r.at[k], s_r.at[k], r_r.at[k], (lax.rem(row + k, 16), col))) for k in range(1, 16)]
    t = msg[...]
    for k, c in enumerate(cr):
        c.wait_recv()
        t += got_r[k + 1]
    msg2[...] = t
    cc = [go(remote(msg2, got_c.at[k], s_c.at[k], r_c.at[k], (row, lax.rem(col + k, 8)))) for k in range(1, 8)]
    for k, c in enumerate(cc):
        c.wait_recv()
        t += got_c[k + 1]
    rr, qw, ww, gg = t[0:1], t[1:2], t[2:3], t[3:4]
    s1 = rr / qw
    new = s1 * s1 * ww - rr
    beta = new / rr
    up = 1.0 + beta
    s2 = new / (up * up * qw - 2.0 * up * s1 * ww + s1 * s1 * gg)
    x_out[...] = (s1 + s2 * up) * qv - (s2 * s1) * w
    for c in sends:
        c.wait_send()
    for c in out:
        c.wait()


def run(*args):
    dma = pltpu.SemaphoreType.DMA
    bf, f32 = jnp.bfloat16, jnp.float32
    vm = pltpu.VMEM
    hbm = pl.BlockSpec(memory_space=pl.ANY)
    return pl.pallas_call(
        kernel,
        out_shape=(jax.ShapeDtypeStruct((1024, 2048), f32), jax.ShapeDtypeStruct((1024, 256), f32)),
        in_specs=[hbm] * 4 + [pl.BlockSpec(memory_space=pltpu.SMEM)] + [hbm] * 2,
        out_specs=(hbm, pl.BlockSpec(memory_space=pltpu.VMEM)),
        scratch_shapes=[vm((256, 4096), bf), vm((256, 4096), bf), vm((4096, 128), bf), vm((4096, 128), bf),
                        vm((1024, 2048), f32), vm((1024, 256), f32), vm((16, 8, 1024), bf),
                        vm((4, 4, 8, 8, 1024), bf), vm((2, 4, 4, 8, 8, 1024), bf), vm((256, 1024), bf),
                        vm((2, 1024, 1024), f32), vm((2, 1024, 1024), bf), vm((2, 4, 4, 16, 1024), bf),
                        vm((2, 2, 4, 16, 512), bf), vm((2, 2, 2, 4, 16, 512), bf), vm((2, 2, 4, 16, 512), bf),
                        vm((2, 4, 16, 1024), bf), vm((2, 3, 16, 1024), bf), vm((2, 4, 4, 16, 1024), bf),
                        vm((4, 4, 16, 1024), bf),
                        vm((4, 256), f32), vm((16, 4, 256), f32), vm((4, 256), f32), vm((8, 4, 256), f32),
                        dma((6,)), dma((2,)), dma((2,)), dma((8,)), dma((8,)), dma((16,)), dma((16,)),
                        dma((20,)), dma((20,)), dma((20,)), dma((20,)), dma((4,)), dma((4,)), dma((4,)), dma((4,)),
                        dma((2, 6)), dma((2, 6)), dma((2, 4)), dma((2, 4)), dma((20,)), dma((20,)), dma((20,)), dma((20,)),
                        dma((16, 4)), dma((16,)), dma((16,)), dma((16,)), dma((16,)), dma((16,)), dma((8,)), dma((8,))],
        compiler_params=pltpu.CompilerParams(collective_id=0, has_side_effects=True, vmem_limit_bytes=62 * 1024 * 1024),
        name="influence",
    )(*args)


def solution(mesh):
    in_specs = (
        P(("row", "col"), None),
        P(("row", "col"), None),
        P(),
        P(),
        P(("row", "col")),
        P("row", "col"),
        P("row", None),
    )
    out_specs = (P("row", "col"), P("row", None))
    return jax.shard_map(run, mesh=mesh, in_specs=in_specs, out_specs=out_specs, check_vma=False)
```

```python
import functools

import jax
import jax.numpy as jnp
from jax import lax
from jax.experimental import pallas as pl
from jax.experimental.pallas import tpu as pltpu
from jax.sharding import PartitionSpec as P

MESH = pl.DeviceIdType.MESH
SEQ = 32
ITERS = 2
decay_rate = 0.5
damping = 1.0
HBM = pl.ANY


class Ring:
    def __init__(self, go, slot, lo, hi, ss, rs, base, plus, minus):
        self.go, self.slot, self.lo, self.hi = go, slot, lo, hi
        self.ss, self.rs, self.base = ss, rs, base
        self.plus, self.minus = plus, minus

    def copy(self, ref, k, dev):
        return self.go(pltpu.make_async_remote_copy(
            src_ref=ref, dst_ref=ref, send_sem=self.ss.at[self.base + k], recv_sem=self.rs.at[self.base + k],
            device_id=dev, device_id_type=MESH))

    def start(self):
        own = self.slot(0)
        self.f0 = self.copy(own, 0, self.plus)
        self.f1 = self.copy(own, 1, self.minus)

    def forward(self):
        self.f0.wait_recv()
        self.h0 = self.copy(self.lo(self.slot(3)), 2, self.plus)
        self.f1.wait_recv()
        self.h1 = self.copy(self.hi(self.slot(1)), 3, self.minus)

    def finish(self):
        self.h0.wait_recv()
        self.h1.wait_recv()


def greet(row, col):
    barrier = pltpu.get_barrier_semaphore()
    for k in range(1, 8):
        pl.semaphore_signal(barrier, inc=1, device_id=(row, lax.rem(col + k, 8)), device_id_type=MESH)
    for k in range(1, 16):
        pl.semaphore_signal(barrier, inc=1, device_id=(lax.rem(row + k, 16), col), device_id_type=MESH)
    return barrier


def kernel(act, og, p_in, p_out, lens, old_hbm, q_hbm, acc, x_out,
           act_v, og_v, pin_v, pout_v, old, q, lg, left, right, qt, gb, part,
           a_far, a_got, a_sum, b_sum, b_got, wc, wr, msg, got_r, msg2, got_c,
           in_sem, loc_sem, c_send, c_recv, r_send, r_recv, ya_send, ya_recv, za_send, za_recv,
           x_send, x_recv, p_send, p_recv,
           s_a, r_a, s_b, r_b, ys, yr, zs, zr, xs, xrecv, ps, pr, s_r, r_r, s_c, r_c):
    f32, bf = jnp.float32, jnp.bfloat16
    row = lax.axis_index("row")
    col = lax.axis_index("col")
    z, y = row // 4, row % 4
    x, core = col // 2, col % 2
    barrier = greet(row, col)
    loads = [pltpu.make_async_copy(a, b, in_sem.at[n]) for n, (a, b) in enumerate(
        ((p_out, pout_v), (og, og_v), (p_in, pin_v), (act, act_v), (q_hbm, q), (old_hbm, old)))]
    for c in loads[:4]:
        c.start()
    sends = []

    def go(copy):
        copy.start()
        sends.append(copy)
        return copy

    def remote(src, dst, ssem, rsem, dev):
        return pltpu.make_async_remote_copy(src_ref=src, dst_ref=dst, send_sem=ssem, recv_sem=rsem,
                                            device_id=dev, device_id_type=MESH)

    def ymod(k):
        return lax.rem(y + k, 4)

    def zmod(k):
        return lax.rem(z + k, 4)

    def at_y(k):
        return (z * 4 + ymod(k), col)

    def at_z(k):
        return (zmod(k) * 4 + y, col)

    loads[0].wait()
    loads[1].wait()
    low_out = jnp.dot(og_v[...], pout_v[...], preferred_element_type=f32).astype(bf).astype(f32).T
    ex = lax.broadcasted_iota(jnp.int32, (8, 256), 0)
    slot = lax.broadcasted_iota(jnp.int32, (8, 256), 1) - SEQ * ex
    count = jnp.zeros((8, 256), jnp.int32)
    for e in range(8):
        count = jnp.where(ex == e, lens[e], count)
    valid = jnp.logical_and(slot >= 0, slot < jnp.minimum(count, SEQ))
    spread = jnp.where(valid[None], low_out[:, None, :], 0.0).reshape(1024, 256).astype(bf)
    loads[2].wait()
    loads[3].wait()
    low_in = jnp.dot(act_v[...], pin_v[...], preferred_element_type=f32).astype(bf)
    grads = jnp.dot(spread, low_in, preferred_element_type=f32).reshape(16, 8, 8, 128)
    for j in range(8):
        lg[:, :, pl.ds(j * 128, 128)] = grads[:, j].astype(bf)
    pl.semaphore_wait(barrier, 22)

    own_right = pltpu.make_async_copy(lg.at[pl.ds(2 * col, 2)], right.at[:, z, y, col], loc_sem.at[0])
    own_right.start()
    own_left = pltpu.make_async_copy(lg.at[row], left.at[z, y, col], loc_sem.at[1])
    own_left.start()
    stage_c, stage_r = [], []
    for k in (2, 6, 1, 7, 3, 5, 4):
        to = lax.rem(col + k, 8)
        stage_c.append(go(remote(lg.at[pl.ds(2 * to, 2)], right.at[:, z, y, col],
                                 c_send.at[k], c_recv.at[k], (row, to))))
    for k in range(1, 16):
        to = lax.rem(row + k, 16)
        stage_r.append(go(remote(lg.at[to], left.at[z, y, col], r_send.at[k], r_recv.at[k], (to, col))))
    loads[4].start()
    loads[5].start()

    yp, ym, zp, zm = at_y(1), at_y(3), at_z(1), at_z(3)
    xp = (row, lax.rem(x + 1, 4) * 2 + core)
    xm = (row, lax.rem(x + 3, 4) * 2 + core)
    partner = (row, x * 2 + 1 - core)
    lo5, hi5 = (lambda r: r.at[pl.ds(0, 4)]), (lambda r: r.at[pl.ds(4, 4)])
    a0 = Ring(go, lambda k: right.at[0, z, ymod(k)], lo5, hi5, ya_send, ya_recv, 0, yp, ym)
    a1 = Ring(go, lambda k: right.at[1, zmod(k), y], lo5, hi5, za_send, za_recv, 0, zp, zm)
    b0 = [Ring(go, lambda k, j=j: right.at[0, zmod(k), ymod(j)], lo5, hi5, za_send, za_recv, 4 + 4 * j, zp, zm)
          for j in range(4)]
    b1 = [Ring(go, lambda k, j=j: right.at[1, zmod(j), ymod(k)], lo5, hi5, ya_send, ya_recv, 4 + 4 * j, yp, ym)
          for j in range(4)]
    xr = Ring(go, lambda k: left.at[:, :, lax.rem(x + k, 4) * 2 + core], lambda r: r.at[pl.ds(0, 2)],
              lambda r: r.at[pl.ds(2, 2)], x_send, x_recv, 0, xp, xm)

    def to_partner(k):
        c = left.at[:, :, lax.rem(x + k, 4) * 2 + core]
        return go(remote(c, c, p_send.at[k], p_recv.at[k], partner))

    own_right.wait()
    own_left.wait()
    for c in stage_c:
        c.wait_recv()
    a0.start(); a1.start()
    b0[0].start(); b1[0].start()
    for c in stage_r:
        c.wait_recv()
    xr.start()
    pp = [to_partner(0)]
    a0.forward(); a1.forward()
    for j in (3, 1):
        b0[j].start(); b1[j].start()
    xr.forward()
    pp += [to_partner(3), to_partner(1)]
    b0[0].forward(); b1[0].forward()
    a0.finish(); a1.finish()
    b0[2].start(); b1[2].start()
    xr.finish()
    pp += [to_partner(2)]
    loads[4].wait()
    qt[...] = q[...].T.astype(bf)
    for c in pp:
        c.wait_recv()

    def left_of(h, j):
        block = left[:, ymod(j)] if h == 0 else left[zmod(j)]
        return block.astype(f32).reshape(256, 1024).T.astype(bf)

    def right_of(h, j):
        block = right[0, :, ymod(j)] if h == 0 else right[1, zmod(j)]
        return block.astype(f32).reshape(256, 1024).astype(bf)

    def multiply(h, j):
        add = jnp.dot(left_of(h, j), right_of(h, j), preferred_element_type=f32)
        acc[h] = add if j == 0 else acc[h] + add

    for j in (3, 1):
        b0[j].forward(); b1[j].forward()
    b0[0].finish(); b1[0].finish()
    multiply(0, 0)
    b0[2].forward(); b1[2].forward()
    multiply(1, 0)
    for j in (3, 1):
        b0[j].finish(); b1[j].finish()
        multiply(0, j); multiply(1, j)
    last = [left_of(h, 2) for h in range(2)]
    b0[2].finish(); b1[2].finish()
    loads[5].wait()

    lo, hi = pl.ds(0, 512), pl.ds(512, 512)

    def chunk(h, k):
        return part.at[0, :, ymod(k)] if h == 0 else part.at[1, zmod(k)]

    near = ((yp, ym), (zp, zm))
    far, plain = [], []
    for h in range(2):
        plus, minus = near[h]
        lanes = pl.ds(h * 1024, 1024)
        prod = acc[h] + jnp.dot(last[h], right_of(h, 2), preferred_element_type=f32)
        ri = lax.broadcasted_iota(jnp.int32, (1024, 1024), 0) + row * 1024
        ci = lax.broadcasted_iota(jnp.int32, (1024, 1024), 1) + (col * 2048 + h * 1024)
        g = decay_rate * old[:, lanes] + ((1.0 - decay_rate) / 1024) * prod
        g = g + jnp.where(ri == ci, damping, 0.0).astype(f32)
        acc[h] = g
        gb[h] = g.astype(bf)
        pt = jnp.dot(qt[...], gb[h], preferred_element_type=f32)
        part[h] = pt.astype(bf).reshape(4, 4, 16, 1024)
        far.append((go(remote(chunk(h, 2).at[:, :, lo], a_far.at[h, 0], s_a.at[h, 0], r_a.at[h, 0], plus)),
                    go(remote(chunk(h, 2).at[:, :, hi], a_far.at[h, 1], s_a.at[h, 1], r_a.at[h, 1], minus))))
        plain.append((go(remote(chunk(h, 1).at[:, :, hi], a_got.at[h, 0, 1], s_a.at[h, 2], r_a.at[h, 2], plus)),
                      go(remote(chunk(h, 3).at[:, :, lo], a_got.at[h, 1, 0], s_a.at[h, 3], r_a.at[h, 3], minus))))
    joined = []
    for h in range(2):
        plus, minus = near[h]
        far[h][0].wait_recv()
        a_sum[h, 0] = (chunk(h, 1)[:, :, lo].astype(f32) + a_far[h, 0].astype(f32)).astype(bf)
        up = go(remote(a_sum.at[h, 0], a_got.at[h, 0, 0], s_a.at[h, 4], r_a.at[h, 4], plus))
        far[h][1].wait_recv()
        a_sum[h, 1] = (chunk(h, 3)[:, :, hi].astype(f32) + a_far[h, 1].astype(f32)).astype(bf)
        joined.append((up, go(remote(a_sum.at[h, 1], a_got.at[h, 1, 1], s_a.at[h, 5], r_a.at[h, 5], minus))))
    second = []
    for h in range(2):
        for c in plain[h] + joined[h]:
            c.wait_recv()
        for n, lanes in enumerate((lo, hi)):
            t = chunk(h, 0)[:, :, lanes].astype(f32) + a_got[h, 0, n].astype(f32) + a_got[h, 1, n].astype(f32)
            b_sum[h, :, :, lanes] = t.astype(bf)
        second.append([])
        for k in (1, 3, 2):
            to, dev = (zmod(k), at_z(k)) if h == 0 else (ymod(k), at_y(k))
            second[h].append(go(remote(b_sum.at[h, to], b_got.at[h, k - 1], s_b.at[h, k], r_b.at[h, k], dev)))

    lol, hil = (lambda r: r.at[:, lo]), (lambda r: r.at[:, hi])
    e0 = Ring(go, lambda k: wc.at[0, z, ymod(k)], lol, hil, ys, yr, 0, yp, ym)
    e1 = Ring(go, lambda k: wc.at[1, zmod(k), y], lol, hil, zs, zr, 0, zp, zm)
    f0 = [Ring(go, lambda k, j=j: wc.at[0, zmod(k), ymod(j)], lol, hil, zs, zr, 4 + 4 * j, zp, zm) for j in range(4)]
    f1 = [Ring(go, lambda k, j=j: wc.at[1, zmod(j), ymod(k)], lol, hil, ys, yr, 4 + 4 * j, yp, ym) for j in range(4)]
    half = y % 2
    mine = core == y // 2
    root = jnp.logical_and(mine, x == z)
    pieces = []

    def group(late, early):
        dz = jnp.where(half == 0, late, early)
        dy = jnp.where(half == 0, early, late)
        return zmod(dz), ymod(dy)

    def along(n, k):
        gz, gy = pieces[n]
        return remote(wc.at[half, gz, gy], wr.at[gz, gy], xs.at[n, k], xrecv.at[n], (row, lax.rem(x + k, 4) * 2 + core))

    def across(n, src):
        gz, gy = pieces[n]
        return remote(src.at[gz, gy], wr.at[gz, gy], ps.at[n], pr.at[n], partner)

    def publish(*which):
        first = len(pieces)
        pieces.extend(group(*w) for w in which)

        @pl.when(root)
        def _():
            for n in range(first, len(pieces)):
                for k in (1, 3, 2):
                    along(n, k).start()
                across(n, wc.at[half]).start()

    for h in range(2):
        for c in second[h]:
            c.wait_recv()
        t = b_sum[h, z if h == 0 else y].astype(f32)
        for k in range(3):
            t += b_got[h, k].astype(f32)
        wc[h, z, y] = t.astype(bf)
        (e0, e1)[h].start()
        (f0, f1)[h][0].start()
    publish((0, 0))
    e0.forward(); e1.forward()
    for j in (3, 1):
        f0[j].start(); f1[j].start()
    publish((0, 3), (0, 1))
    f0[0].forward(); f1[0].forward()
    e0.finish(); e1.finish()
    f0[2].start(); f1[2].start()
    publish((3, 0), (1, 0), (0, 2))
    for j in (3, 1, 2):
        f0[j].forward(); f1[j].forward()
        publish((3, j), (1, j))
    for j in (0, 3, 1, 2):
        f0[j].finish(); f1[j].finish()
        publish((2, j))

    @pl.when(root)
    def _():
        wr[...] = wc[half]
        for n in range(16):
            for k in (1, 3, 2):
                along(n, k).wait_send()
            across(n, wc.at[half]).wait_send()

    @pl.when(jnp.logical_and(mine, x != z))
    def _():
        for n in range(16):
            along(n, 1).wait_recv()
            across(n, wr).start()
        for n in range(16):
            across(n, wr).wait_send()

    @pl.when(jnp.logical_not(mine))
    def _():
        for n in range(16):
            across(n, wr).wait_recv()

    wrv = wr[...].reshape(256, 1024)
    v0 = jnp.dot(wrv, gb[0], preferred_element_type=f32) * wc[0].reshape(256, 1024).astype(f32)
    v1 = jnp.dot(wrv, gb[1], preferred_element_type=f32) * wc[1].reshape(256, 1024).astype(f32)
    curve = jnp.broadcast_to(jnp.sum(v0 + v1, axis=1, keepdims=True), (256, 128)).T
    w = wrv.astype(f32).T
    qv = q[...]
    once = jnp.where(col == 0, 1.0, 0.0).astype(f32)
    msg[0:1] = jnp.sum(qv * qv, axis=0, keepdims=True) * once
    msg[1:2] = jnp.sum(qv * w, axis=0, keepdims=True) * once
    msg[2:3] = jnp.sum(w * w, axis=0, keepdims=True) * once
    msg[3:4] = curve[3:4]
    cr = [go(remote(msg, got_r.at[k], s_r.at[k], r_r.at[k], (lax.rem(row + k, 16), col))) for k in range(1, 16)]
    t = msg[...]
    for k, c in enumerate(cr):
        c.wait_recv()
        t += got_r[k + 1]
    msg2[...] = t
    cc = [go(remote(msg2, got_c.at[k], s_c.at[k], r_c.at[k], (row, lax.rem(col + k, 8)))) for k in range(1, 8)]
    for k, c in enumerate(cc):
        c.wait_recv()
        t += got_c[k + 1]
    rr, qw, ww, gg = t[0:1], t[1:2], t[2:3], t[3:4]
    s1 = rr / qw
    new = s1 * s1 * ww - rr
    beta = new / rr
    up = 1.0 + beta
    s2 = new / (up * up * qw - 2.0 * up * s1 * ww + s1 * s1 * gg)
    x_out[...] = (s1 + s2 * up) * qv - (s2 * s1) * w
    for c in sends:
        c.wait_send()


def run(*args):
    dma = pltpu.SemaphoreType.DMA
    bf, f32 = jnp.bfloat16, jnp.float32
    vm = pltpu.VMEM
    hbm = pl.BlockSpec(memory_space=pl.ANY)
    return pl.pallas_call(
        kernel,
        out_shape=(vm((2, 1024, 1024), f32), vm((1024, 256), f32)),
        in_specs=[hbm] * 4 + [pl.BlockSpec(memory_space=pltpu.SMEM)] + [hbm] * 2,
        out_specs=(pl.BlockSpec(memory_space=pltpu.VMEM),) * 2,
        scratch_shapes=[vm((256, 4096), bf), vm((256, 4096), bf), vm((4096, 128), bf), vm((4096, 128), bf),
                        vm((1024, 2048), f32), vm((1024, 256), f32), vm((16, 8, 1024), bf),
                        vm((4, 4, 8, 8, 1024), bf), vm((2, 4, 4, 8, 8, 1024), bf), vm((256, 1024), bf),
                        vm((2, 1024, 1024), bf), vm((2, 4, 4, 16, 1024), bf),
                        vm((2, 2, 4, 16, 512), bf), vm((2, 2, 2, 4, 16, 512), bf), vm((2, 2, 4, 16, 512), bf),
                        vm((2, 4, 16, 1024), bf), vm((2, 3, 16, 1024), bf), vm((2, 4, 4, 16, 1024), bf),
                        vm((4, 4, 16, 1024), bf),
                        vm((4, 256), f32), vm((16, 4, 256), f32), vm((4, 256), f32), vm((8, 4, 256), f32),
                        dma((6,)), dma((2,)), dma((8,)), dma((8,)), dma((16,)), dma((16,)),
                        dma((20,)), dma((20,)), dma((20,)), dma((20,)), dma((4,)), dma((4,)), dma((4,)), dma((4,)),
                        dma((2, 6)), dma((2, 6)), dma((2, 4)), dma((2, 4)), dma((20,)), dma((20,)), dma((20,)), dma((20,)),
                        dma((16, 4)), dma((16,)), dma((16,)), dma((16,)), dma((16,)), dma((16,)), dma((8,)), dma((8,))],
        compiler_params=pltpu.CompilerParams(collective_id=0, has_side_effects=True, vmem_limit_bytes=44 * 1024 * 1024),
        name="influence",
    )(*args)


def store_kernel(g, x, g_out, x_out, sem):
    copies = [pltpu.make_async_copy(g.at[h, pl.ds(n * 256, 256)], g_out.at[pl.ds(n * 256, 256), pl.ds(h * 1024, 1024)],
                                    sem.at[4 * h + n]) for h in range(2) for n in range(4)]
    copies.append(pltpu.make_async_copy(x, x_out, sem.at[8]))
    for c in copies:
        c.start()
    for c in copies:
        c.wait()


def store(g, x):
    f32 = jnp.float32
    inside, hbm = pl.BlockSpec(memory_space=pltpu.VMEM), pl.BlockSpec(memory_space=pltpu.HBM)
    return pl.pallas_call(
        store_kernel,
        out_shape=(jax.ShapeDtypeStruct((1024, 2048), f32), jax.ShapeDtypeStruct((1024, 256), f32)),
        in_specs=[inside] * 2,
        out_specs=(hbm, hbm),
        scratch_shapes=[pltpu.SemaphoreType.DMA((9,))],
        compiler_params=pltpu.CompilerParams(vmem_limit_bytes=16 * 1024 * 1024),
        name="store",
    )(pltpu.with_memory_space_constraint(g, pltpu.VMEM), pltpu.with_memory_space_constraint(x, pltpu.VMEM))


def whole(*args):
    return store(*run(*args))


def solution(mesh):
    in_specs = (
        P(("row", "col"), None),
        P(("row", "col"), None),
        P(),
        P(),
        P(("row", "col")),
        P("row", "col"),
        P("row", None),
    )
    out_specs = (P("row", "col"), P("row", None))
    return jax.shard_map(whole, mesh=mesh, in_specs=in_specs, out_specs=out_specs, check_vma=False)
```

```python
import functools

import jax
import jax.numpy as jnp
from jax import lax
from jax.experimental import pallas as pl
from jax.experimental.pallas import tpu as pltpu
from jax.sharding import PartitionSpec as P

MESH = pl.DeviceIdType.MESH
SEQ = 32
ITERS = 2
decay_rate = 0.5
damping = 1.0
HBM = pl.ANY


class Ring:
    def __init__(self, go, slot, lo, hi, ss, rs, base, plus, minus):
        self.go, self.slot, self.lo, self.hi = go, slot, lo, hi
        self.ss, self.rs, self.base = ss, rs, base
        self.plus, self.minus = plus, minus

    def copy(self, ref, k, dev):
        return self.go(pltpu.make_async_remote_copy(
            src_ref=ref, dst_ref=ref, send_sem=self.ss.at[self.base + k], recv_sem=self.rs.at[self.base + k],
            device_id=dev, device_id_type=MESH))

    def start(self):
        own = self.slot(0)
        self.f0 = self.copy(own, 0, self.plus)
        self.f1 = self.copy(own, 1, self.minus)

    def forward(self):
        self.f0.wait_recv()
        self.h0 = self.copy(self.lo(self.slot(3)), 2, self.plus)
        self.f1.wait_recv()
        self.h1 = self.copy(self.hi(self.slot(1)), 3, self.minus)

    def finish(self):
        self.h0.wait_recv()
        self.h1.wait_recv()


def greet(row, col):
    barrier = pltpu.get_barrier_semaphore()
    for k in range(1, 8):
        pl.semaphore_signal(barrier, inc=1, device_id=(row, lax.rem(col + k, 8)), device_id_type=MESH)
    for k in range(1, 16):
        pl.semaphore_signal(barrier, inc=1, device_id=(lax.rem(row + k, 16), col), device_id_type=MESH)
    return barrier


def kernel(act, og, p_in, p_out, lens, old_hbm, q_hbm, acc, x_out,
           act_v, og_v, pin_v, pout_v, old, q, lg, left, right, qt, pt, last, y_last, gb, part,
           a_far, a_got, a_sum, b_sum, b_got, wc, wr, msg, got_r, msg2, got_c,
           in_sem, loc_sem, c_send, c_recv, r_send, r_recv, ya_send, ya_recv, za_send, za_recv,
           x_send, x_recv, p_send, p_recv,
           s_a, r_a, s_b, r_b, ys, yr, zs, zr, xs, xrecv, ps, pr, s_r, r_r, s_c, r_c):
    f32, bf = jnp.float32, jnp.bfloat16
    row = lax.axis_index("row")
    col = lax.axis_index("col")
    z, y = row // 4, row % 4
    x, core = col // 2, col % 2
    barrier = greet(row, col)
    loads = [pltpu.make_async_copy(a, b, in_sem.at[n]) for n, (a, b) in enumerate(
        ((p_out, pout_v), (og, og_v), (p_in, pin_v), (act, act_v), (q_hbm, q), (old_hbm, old)))]
    for c in loads[:4]:
        c.start()
    sends = []

    def go(copy):
        copy.start()
        sends.append(copy)
        return copy

    def remote(src, dst, ssem, rsem, dev):
        return pltpu.make_async_remote_copy(src_ref=src, dst_ref=dst, send_sem=ssem, recv_sem=rsem,
                                            device_id=dev, device_id_type=MESH)

    def ymod(k):
        return lax.rem(y + k, 4)

    def zmod(k):
        return lax.rem(z + k, 4)

    def at_y(k):
        return (z * 4 + ymod(k), col)

    def at_z(k):
        return (zmod(k) * 4 + y, col)

    loads[0].wait()
    loads[1].wait()
    low_out = jnp.dot(og_v[...], pout_v[...], preferred_element_type=f32).astype(bf).astype(f32).T
    ex = lax.broadcasted_iota(jnp.int32, (8, 256), 0)
    slot = lax.broadcasted_iota(jnp.int32, (8, 256), 1) - SEQ * ex
    count = jnp.zeros((8, 256), jnp.int32)
    for e in range(8):
        count = jnp.where(ex == e, lens[e], count)
    valid = jnp.logical_and(slot >= 0, slot < jnp.minimum(count, SEQ))
    spread = jnp.where(valid[None], low_out[:, None, :], 0.0).reshape(1024, 256).astype(bf)
    loads[2].wait()
    loads[3].wait()
    low_in = jnp.dot(act_v[...], pin_v[...], preferred_element_type=f32).astype(bf)
    grads = jnp.dot(spread, low_in, preferred_element_type=f32).reshape(16, 8, 8, 128)
    for j in range(8):
        lg[:, :, pl.ds(j * 128, 128)] = grads[:, j].astype(bf)
    pl.semaphore_wait(barrier, 22)

    own_right = pltpu.make_async_copy(lg.at[pl.ds(2 * col, 2)], right.at[:, z, y, col], loc_sem.at[0])
    own_right.start()
    own_left = pltpu.make_async_copy(lg.at[row], left.at[z, y, col], loc_sem.at[1])
    own_left.start()
    stage_c, stage_r = [], []
    for k in (2, 6, 1, 7, 3, 5, 4):
        to = lax.rem(col + k, 8)
        stage_c.append(go(remote(lg.at[pl.ds(2 * to, 2)], right.at[:, z, y, col],
                                 c_send.at[k], c_recv.at[k], (row, to))))
    for k in range(1, 16):
        to = lax.rem(row + k, 16)
        stage_r.append(go(remote(lg.at[to], left.at[z, y, col], r_send.at[k], r_recv.at[k], (to, col))))
    loads[4].start()
    loads[5].start()

    yp, ym, zp, zm = at_y(1), at_y(3), at_z(1), at_z(3)
    xp = (row, lax.rem(x + 1, 4) * 2 + core)
    xm = (row, lax.rem(x + 3, 4) * 2 + core)
    partner = (row, x * 2 + 1 - core)
    lo5, hi5 = (lambda r: r.at[pl.ds(0, 4)]), (lambda r: r.at[pl.ds(4, 4)])
    a0 = Ring(go, lambda k: right.at[0, z, ymod(k)], lo5, hi5, ya_send, ya_recv, 0, yp, ym)
    a1 = Ring(go, lambda k: right.at[1, zmod(k), y], lo5, hi5, za_send, za_recv, 0, zp, zm)
    b0 = [Ring(go, lambda k, j=j: right.at[0, zmod(k), ymod(j)], lo5, hi5, za_send, za_recv, 4 + 4 * j, zp, zm)
          for j in range(4)]
    b1 = [Ring(go, lambda k, j=j: right.at[1, zmod(j), ymod(k)], lo5, hi5, ya_send, ya_recv, 4 + 4 * j, yp, ym)
          for j in range(4)]
    xr = Ring(go, lambda k: left.at[:, :, lax.rem(x + k, 4) * 2 + core], lambda r: r.at[pl.ds(0, 2)],
              lambda r: r.at[pl.ds(2, 2)], x_send, x_recv, 0, xp, xm)

    def to_partner(k):
        c = left.at[:, :, lax.rem(x + k, 4) * 2 + core]
        return go(remote(c, c, p_send.at[k], p_recv.at[k], partner))

    own_right.wait()
    own_left.wait()
    for c in stage_c:
        c.wait_recv()
    a0.start(); a1.start()
    b0[0].start(); b1[0].start()
    for c in stage_r:
        c.wait_recv()
    xr.start()
    pp = [to_partner(0)]
    a0.forward(); a1.forward()
    for j in (3, 1):
        b0[j].start(); b1[j].start()
    xr.forward()
    pp += [to_partner(3), to_partner(1)]
    b0[0].forward(); b1[0].forward()
    a0.finish(); a1.finish()
    b0[2].start(); b1[2].start()
    xr.finish()
    pp += [to_partner(2)]
    loads[4].wait()
    qt[...] = q[...].T.astype(bf)
    for c in pp:
        c.wait_recv()

    lo, hi = pl.ds(0, 512), pl.ds(512, 512)
    scale = (1.0 - decay_rate) / 1024

    def left_of(h, j):
        block = left[:, ymod(j)] if h == 0 else left[zmod(j)]
        return block.astype(f32).reshape(256, 1024).T.astype(bf)

    def right_of(h, j):
        block = right[0, :, ymod(j)] if h == 0 else right[1, zmod(j)]
        return block.astype(f32).reshape(256, 1024).astype(bf)

    def multiply(h, j):
        lt = left_of(h, j)
        rt = right_of(h, j)
        y16 = (scale * jnp.dot(qt[...], lt, preferred_element_type=f32)).astype(bf)
        pt[h] += jnp.dot(y16, rt, preferred_element_type=f32)
        add = scale * jnp.dot(lt, rt, preferred_element_type=f32)
        acc[h] += add

    def begin(h):
        ri = lax.broadcasted_iota(jnp.int32, (1024, 1024), 0) + row * 1024
        ci = lax.broadcasted_iota(jnp.int32, (1024, 1024), 1) + (col * 2048 + h * 1024)
        g = decay_rate * old[:, pl.ds(h * 1024, 1024)] + jnp.where(ri == ci, damping, 0.0).astype(f32)
        acc[h] = g
        pt[h] = jnp.dot(qt[...], g.astype(bf), preferred_element_type=f32)

    loads[5].wait()
    for j in (3, 1):
        b0[j].forward(); b1[j].forward()
    begin(0)
    b0[0].finish()
    multiply(0, 0)
    b0[2].forward(); b1[2].forward()
    begin(1)
    b1[0].finish()
    multiply(1, 0)
    for j in (3, 1):
        b0[j].finish(); b1[j].finish()
        multiply(0, j); multiply(1, j)
    for h in range(2):
        lt = left_of(h, 2)
        last[h] = lt
        y_last[h] = (scale * jnp.dot(qt[...], lt, preferred_element_type=f32)).astype(bf)

    def chunk(h, k):
        return part.at[0, :, ymod(k)] if h == 0 else part.at[1, zmod(k)]

    def tile(h):
        g = acc[h] + scale * jnp.dot(last[h], right_of(h, 2), preferred_element_type=f32)
        acc[h] = g
        gb[h] = g.astype(bf)

    near = ((yp, ym), (zp, zm))
    far, plain = [], []
    for h in range(2):
        (b0, b1)[h][2].finish()
        plus, minus = near[h]
        whole_pt = pt[h] + jnp.dot(y_last[h], right_of(h, 2), preferred_element_type=f32)
        part[h] = whole_pt.astype(bf).reshape(4, 4, 16, 1024)
        far.append((go(remote(chunk(h, 2).at[:, :, lo], a_far.at[h, 0], s_a.at[h, 0], r_a.at[h, 0], plus)),
                    go(remote(chunk(h, 2).at[:, :, hi], a_far.at[h, 1], s_a.at[h, 1], r_a.at[h, 1], minus))))
        plain.append((go(remote(chunk(h, 1).at[:, :, hi], a_got.at[h, 0, 1], s_a.at[h, 2], r_a.at[h, 2], plus)),
                      go(remote(chunk(h, 3).at[:, :, lo], a_got.at[h, 1, 0], s_a.at[h, 3], r_a.at[h, 3], minus))))
    tile(0)
    joined = []
    for h in range(2):
        plus, minus = near[h]
        far[h][0].wait_recv()
        a_sum[h, 0] = (chunk(h, 1)[:, :, lo].astype(f32) + a_far[h, 0].astype(f32)).astype(bf)
        up = go(remote(a_sum.at[h, 0], a_got.at[h, 0, 0], s_a.at[h, 4], r_a.at[h, 4], plus))
        far[h][1].wait_recv()
        a_sum[h, 1] = (chunk(h, 3)[:, :, hi].astype(f32) + a_far[h, 1].astype(f32)).astype(bf)
        joined.append((up, go(remote(a_sum.at[h, 1], a_got.at[h, 1, 1], s_a.at[h, 5], r_a.at[h, 5], minus))))
    tile(1)
    second = []
    for h in range(2):
        for c in plain[h] + joined[h]:
            c.wait_recv()
        for n, lanes in enumerate((lo, hi)):
            t = chunk(h, 0)[:, :, lanes].astype(f32) + a_got[h, 0, n].astype(f32) + a_got[h, 1, n].astype(f32)
            b_sum[h, :, :, lanes] = t.astype(bf)
        second.append([])
        for k in (1, 3, 2):
            to, dev = (zmod(k), at_z(k)) if h == 0 else (ymod(k), at_y(k))
            second[h].append(go(remote(b_sum.at[h, to], b_got.at[h, k - 1], s_b.at[h, k], r_b.at[h, k], dev)))

    lol, hil = (lambda r: r.at[:, lo]), (lambda r: r.at[:, hi])
    e0 = Ring(go, lambda k: wc.at[0, z, ymod(k)], lol, hil, ys, yr, 0, yp, ym)
    e1 = Ring(go, lambda k: wc.at[1, zmod(k), y], lol, hil, zs, zr, 0, zp, zm)
    f0 = [Ring(go, lambda k, j=j: wc.at[0, zmod(k), ymod(j)], lol, hil, zs, zr, 4 + 4 * j, zp, zm) for j in range(4)]
    f1 = [Ring(go, lambda k, j=j: wc.at[1, zmod(j), ymod(k)], lol, hil, ys, yr, 4 + 4 * j, yp, ym) for j in range(4)]
    half = y % 2
    mine = core == y // 2
    root = jnp.logical_and(mine, x == z)
    pieces = []

    def group(late, early):
        dz = jnp.where(half == 0, late, early)
        dy = jnp.where(half == 0, early, late)
        return zmod(dz), ymod(dy)

    def along(n, k):
        gz, gy = pieces[n]
        return remote(wc.at[half, gz, gy], wr.at[gz, gy], xs.at[n, k], xrecv.at[n], (row, lax.rem(x + k, 4) * 2 + core))

    def across(n, src):
        gz, gy = pieces[n]
        return remote(src.at[gz, gy], wr.at[gz, gy], ps.at[n], pr.at[n], partner)

    def publish(*which):
        first = len(pieces)
        pieces.extend(group(*w) for w in which)

        @pl.when(root)
        def _():
            for n in range(first, len(pieces)):
                for k in (1, 3, 2):
                    along(n, k).start()
                across(n, wc.at[half]).start()

    for h in range(2):
        for c in second[h]:
            c.wait_recv()
        t = b_sum[h, z if h == 0 else y].astype(f32)
        for k in range(3):
            t += b_got[h, k].astype(f32)
        wc[h, z, y] = t.astype(bf)
        (e0, e1)[h].start()
        (f0, f1)[h][0].start()
    publish((0, 0))
    e0.forward(); e1.forward()
    for j in (3, 1):
        f0[j].start(); f1[j].start()
    publish((0, 3), (0, 1))
    f0[0].forward(); f1[0].forward()
    e0.finish(); e1.finish()
    f0[2].start(); f1[2].start()
    publish((3, 0), (1, 0), (0, 2))
    for j in (3, 1, 2):
        f0[j].forward(); f1[j].forward()
        publish((3, j), (1, j))
    for j in (0, 3, 1, 2):
        f0[j].finish(); f1[j].finish()
        publish((2, j))

    @pl.when(root)
    def _():
        wr[...] = wc[half]
        for n in range(16):
            for k in (1, 3, 2):
                along(n, k).wait_send()
            across(n, wc.at[half]).wait_send()

    @pl.when(jnp.logical_and(mine, x != z))
    def _():
        for n in range(16):
            along(n, 1).wait_recv()
            across(n, wr).start()
        for n in range(16):
            across(n, wr).wait_send()

    @pl.when(jnp.logical_not(mine))
    def _():
        for n in range(16):
            across(n, wr).wait_recv()

    wrv = wr[...].reshape(256, 1024)
    v0 = jnp.dot(wrv, gb[0], preferred_element_type=f32) * wc[0].reshape(256, 1024).astype(f32)
    v1 = jnp.dot(wrv, gb[1], preferred_element_type=f32) * wc[1].reshape(256, 1024).astype(f32)
    curve = jnp.broadcast_to(jnp.sum(v0 + v1, axis=1, keepdims=True), (256, 128)).T
    w = wrv.astype(f32).T
    qv = q[...]
    once = jnp.where(col == 0, 1.0, 0.0).astype(f32)
    msg[0:1] = jnp.sum(qv * qv, axis=0, keepdims=True) * once
    msg[1:2] = jnp.sum(qv * w, axis=0, keepdims=True) * once
    msg[2:3] = jnp.sum(w * w, axis=0, keepdims=True) * once
    msg[3:4] = curve[3:4]
    cr = [go(remote(msg, got_r.at[k], s_r.at[k], r_r.at[k], (lax.rem(row + k, 16), col))) for k in range(1, 16)]
    t = msg[...]
    for k, c in enumerate(cr):
        c.wait_recv()
        t += got_r[k + 1]
    msg2[...] = t
    cc = [go(remote(msg2, got_c.at[k], s_c.at[k], r_c.at[k], (row, lax.rem(col + k, 8)))) for k in range(1, 8)]
    for k, c in enumerate(cc):
        c.wait_recv()
        t += got_c[k + 1]
    rr, qw, ww, gg = t[0:1], t[1:2], t[2:3], t[3:4]
    s1 = rr / qw
    new = s1 * s1 * ww - rr
    beta = new / rr
    up = 1.0 + beta
    s2 = new / (up * up * qw - 2.0 * up * s1 * ww + s1 * s1 * gg)
    x_out[...] = (s1 + s2 * up) * qv - (s2 * s1) * w
    for c in sends:
        c.wait_send()


def run(*args):
    dma = pltpu.SemaphoreType.DMA
    bf, f32 = jnp.bfloat16, jnp.float32
    vm = pltpu.VMEM
    hbm = pl.BlockSpec(memory_space=pl.ANY)
    return pl.pallas_call(
        kernel,
        out_shape=(vm((2, 1024, 1024), f32), vm((1024, 256), f32)),
        in_specs=[hbm] * 4 + [pl.BlockSpec(memory_space=pltpu.SMEM)] + [hbm] * 2,
        out_specs=(pl.BlockSpec(memory_space=pltpu.VMEM),) * 2,
        scratch_shapes=[vm((256, 4096), bf), vm((256, 4096), bf), vm((4096, 128), bf), vm((4096, 128), bf),
                        vm((1024, 2048), f32), vm((1024, 256), f32), vm((16, 8, 1024), bf),
                        vm((4, 4, 8, 8, 1024), bf), vm((2, 4, 4, 8, 8, 1024), bf), vm((256, 1024), bf),
                        vm((2, 256, 1024), f32), vm((2, 1024, 256), bf), vm((2, 256, 256), bf),
                        vm((2, 1024, 1024), bf), vm((2, 4, 4, 16, 1024), bf),
                        vm((2, 2, 4, 16, 512), bf), vm((2, 2, 2, 4, 16, 512), bf), vm((2, 2, 4, 16, 512), bf),
                        vm((2, 4, 16, 1024), bf), vm((2, 3, 16, 1024), bf), vm((2, 4, 4, 16, 1024), bf),
                        vm((4, 4, 16, 1024), bf),
                        vm((4, 256), f32), vm((16, 4, 256), f32), vm((4, 256), f32), vm((8, 4, 256), f32),
                        dma((6,)), dma((2,)), dma((8,)), dma((8,)), dma((16,)), dma((16,)),
                        dma((20,)), dma((20,)), dma((20,)), dma((20,)), dma((4,)), dma((4,)), dma((4,)), dma((4,)),
                        dma((2, 6)), dma((2, 6)), dma((2, 4)), dma((2, 4)), dma((20,)), dma((20,)), dma((20,)), dma((20,)),
                        dma((16, 4)), dma((16,)), dma((16,)), dma((16,)), dma((16,)), dma((16,)), dma((8,)), dma((8,))],
        compiler_params=pltpu.CompilerParams(collective_id=0, has_side_effects=True, vmem_limit_bytes=44 * 1024 * 1024),
        name="influence",
    )(*args)


def store_kernel(g, x, g_out, x_out, sem):
    copies = [pltpu.make_async_copy(g.at[h, pl.ds(n * 256, 256)], g_out.at[pl.ds(n * 256, 256), pl.ds(h * 1024, 1024)],
                                    sem.at[4 * h + n]) for h in range(2) for n in range(4)]
    copies.append(pltpu.make_async_copy(x, x_out, sem.at[8]))
    for c in copies:
        c.start()
    for c in copies:
        c.wait()


def store(g, x):
    f32 = jnp.float32
    inside, hbm = pl.BlockSpec(memory_space=pltpu.VMEM), pl.BlockSpec(memory_space=pltpu.HBM)
    return pl.pallas_call(
        store_kernel,
        out_shape=(jax.ShapeDtypeStruct((1024, 2048), f32), jax.ShapeDtypeStruct((1024, 256), f32)),
        in_specs=[inside] * 2,
        out_specs=(hbm, hbm),
        scratch_shapes=[pltpu.SemaphoreType.DMA((9,))],
        compiler_params=pltpu.CompilerParams(vmem_limit_bytes=16 * 1024 * 1024),
        name="store",
    )(pltpu.with_memory_space_constraint(g, pltpu.VMEM), pltpu.with_memory_space_constraint(x, pltpu.VMEM))


def whole(*args):
    return store(*run(*args))


def solution(mesh):
    in_specs = (
        P(("row", "col"), None),
        P(("row", "col"), None),
        P(),
        P(),
        P(("row", "col")),
        P("row", "col"),
        P("row", None),
    )
    out_specs = (P("row", "col"), P("row", None))
    return jax.shard_map(whole, mesh=mesh, in_specs=in_specs, out_specs=out_specs, check_vma=False)
```

```python
import functools

import jax
import jax.numpy as jnp
from jax import lax
from jax.experimental import pallas as pl
from jax.experimental.pallas import tpu as pltpu
from jax.sharding import PartitionSpec as P

MESH = pl.DeviceIdType.MESH
SEQ = 32
ITERS = 2
decay_rate = 0.5
damping = 1.0
HBM = pl.ANY


class Ring:
    def __init__(self, go, slot, lo, hi, ss, rs, base, plus, minus):
        self.go, self.slot, self.lo, self.hi = go, slot, lo, hi
        self.ss, self.rs, self.base = ss, rs, base
        self.plus, self.minus = plus, minus

    def copy(self, ref, k, dev):
        return self.go(pltpu.make_async_remote_copy(
            src_ref=ref, dst_ref=ref, send_sem=self.ss.at[self.base + k], recv_sem=self.rs.at[self.base + k],
            device_id=dev, device_id_type=MESH))

    def start(self):
        own = self.slot(0)
        self.f0 = self.copy(own, 0, self.plus)
        self.f1 = self.copy(own, 1, self.minus)

    def forward(self):
        self.f0.wait_recv()
        self.h0 = self.copy(self.lo(self.slot(3)), 2, self.plus)
        self.f1.wait_recv()
        self.h1 = self.copy(self.hi(self.slot(1)), 3, self.minus)

    def finish(self):
        self.h0.wait_recv()
        self.h1.wait_recv()


def greet(row, col):
    barrier = pltpu.get_barrier_semaphore()
    for k in range(1, 8):
        pl.semaphore_signal(barrier, inc=1, device_id=(row, lax.rem(col + k, 8)), device_id_type=MESH)
    for k in range(1, 16):
        pl.semaphore_signal(barrier, inc=1, device_id=(lax.rem(row + k, 16), col), device_id_type=MESH)
    return barrier


def kernel(act, og, p_in, p_out, lens, old_hbm, q_hbm, acc, x_out,
           act_v, og_v, pin_v, pout_v, old, q, lg, left, right, qt, y_mine, y_got, proj, w_row, w_col, gb, part,
           a_far, a_got, a_sum, b_sum, b_got, wc, wr, msg, got_r, msg2, got_c,
           in_sem, loc_sem, c_send, c_recv, r_send, r_recv, ya_send, ya_recv, za_send, za_recv,
           x_send, x_recv, p_send, p_recv,
           s_y, r_y, s_z, r_z, s_a, r_a, s_b, r_b, ys, yr, zs, zr, xs, xrecv, ps, pr, s_r, r_r, s_c, r_c):
    f32, bf = jnp.float32, jnp.bfloat16
    row = lax.axis_index("row")
    col = lax.axis_index("col")
    z, y = row // 4, row % 4
    x, core = col // 2, col % 2
    barrier = greet(row, col)
    loads = [pltpu.make_async_copy(a, b, in_sem.at[n]) for n, (a, b) in enumerate(
        ((p_out, pout_v), (og, og_v), (p_in, pin_v), (act, act_v), (q_hbm, q), (old_hbm, old)))]
    for c in loads:
        c.start()
    sends = []

    def go(copy):
        copy.start()
        sends.append(copy)
        return copy

    def remote(src, dst, ssem, rsem, dev):
        return pltpu.make_async_remote_copy(src_ref=src, dst_ref=dst, send_sem=ssem, recv_sem=rsem,
                                            device_id=dev, device_id_type=MESH)

    def ymod(k):
        return lax.rem(y + k, 4)

    def zmod(k):
        return lax.rem(z + k, 4)

    def at_y(k):
        return (z * 4 + ymod(k), col)

    def at_z(k):
        return (zmod(k) * 4 + y, col)

    loads[0].wait()
    loads[1].wait()
    low_out = jnp.dot(og_v[...], pout_v[...], preferred_element_type=f32).astype(bf).astype(f32).T
    ex = lax.broadcasted_iota(jnp.int32, (8, 256), 0)
    slot = lax.broadcasted_iota(jnp.int32, (8, 256), 1) - SEQ * ex
    count = jnp.zeros((8, 256), jnp.int32)
    for e in range(8):
        count = jnp.where(ex == e, lens[e], count)
    valid = jnp.logical_and(slot >= 0, slot < jnp.minimum(count, SEQ))
    spread = jnp.where(valid[None], low_out[:, None, :], 0.0).reshape(1024, 256).astype(bf)
    loads[2].wait()
    loads[3].wait()
    low_in = jnp.dot(act_v[...], pin_v[...], preferred_element_type=f32).astype(bf)
    grads = jnp.dot(spread, low_in, preferred_element_type=f32).reshape(16, 8, 8, 128)
    for j in range(8):
        lg[:, :, pl.ds(j * 128, 128)] = grads[:, j].astype(bf)
    loads[4].wait()
    q16 = q[...].T.astype(bf)
    qt[...] = q16
    scale = (1.0 - decay_rate) / 1024

    def begin(h):
        ri = lax.broadcasted_iota(jnp.int32, (1024, 1024), 0) + row * 1024
        ci = lax.broadcasted_iota(jnp.int32, (1024, 1024), 1) + (col * 2048 + h * 1024)
        g = decay_rate * old[:, pl.ds(h * 1024, 1024)] + jnp.where(ri == ci, damping, 0.0).astype(f32)
        acc[h] = g
        pt = jnp.dot(qt[...], g.astype(bf), preferred_element_type=f32)
        part[h] = pt.astype(bf).reshape(4, 4, 16, 1024)

    loads[5].wait()
    begin(0)
    pl.semaphore_wait(barrier, 22)

    own_right = pltpu.make_async_copy(lg.at[pl.ds(2 * col, 2)], right.at[:, z, y, col], loc_sem.at[0])
    own_right.start()
    own_left = pltpu.make_async_copy(lg.at[row], left.at[z, y, col], loc_sem.at[1])
    own_left.start()
    stage_c, stage_r = [], []
    for k in (2, 6, 1, 7, 3, 5, 4):
        to = lax.rem(col + k, 8)
        stage_c.append(go(remote(lg.at[pl.ds(2 * to, 2)], right.at[:, z, y, col],
                                 c_send.at[k], c_recv.at[k], (row, to))))
    for k in range(1, 16):
        to = lax.rem(row + k, 16)
        stage_r.append(go(remote(lg.at[to], left.at[z, y, col], r_send.at[k], r_recv.at[k], (to, col))))
    begin(1)
    yp, ym, zp, zm = at_y(1), at_y(3), at_z(1), at_z(3)
    xp = (row, lax.rem(x + 1, 4) * 2 + core)
    xm = (row, lax.rem(x + 3, 4) * 2 + core)
    partner = (row, x * 2 + 1 - core)
    lo5, hi5 = (lambda r: r.at[pl.ds(0, 4)]), (lambda r: r.at[pl.ds(4, 4)])
    a0 = Ring(go, lambda k: right.at[0, z, ymod(k)], lo5, hi5, ya_send, ya_recv, 0, yp, ym)
    a1 = Ring(go, lambda k: right.at[1, zmod(k), y], lo5, hi5, za_send, za_recv, 0, zp, zm)
    b0 = [Ring(go, lambda k, j=j: right.at[0, zmod(k), ymod(j)], lo5, hi5, za_send, za_recv, 4 + 4 * j, zp, zm)
          for j in range(4)]
    b1 = [Ring(go, lambda k, j=j: right.at[1, zmod(j), ymod(k)], lo5, hi5, ya_send, ya_recv, 4 + 4 * j, yp, ym)
          for j in range(4)]
    xr = Ring(go, lambda k: left.at[:, :, lax.rem(x + k, 4) * 2 + core], lambda r: r.at[pl.ds(0, 2)],
              lambda r: r.at[pl.ds(2, 2)], x_send, x_recv, 0, xp, xm)

    def to_partner(k):
        c = left.at[:, :, lax.rem(x + k, 4) * 2 + core]
        return go(remote(c, c, p_send.at[k], p_recv.at[k], partner))

    lo, hi = pl.ds(0, 512), pl.ds(512, 512)

    def chunk(h, k):
        return part.at[0, :, ymod(k)] if h == 0 else part.at[1, zmod(k)]

    near = ((yp, ym), (zp, zm))
    far, plain, joined, second = [], [], [], []

    def reduce_first(h):
        plus, minus = near[h]
        far.append((go(remote(chunk(h, 2).at[:, :, lo], a_far.at[h, 0], s_a.at[h, 0], r_a.at[h, 0], plus)),
                    go(remote(chunk(h, 2).at[:, :, hi], a_far.at[h, 1], s_a.at[h, 1], r_a.at[h, 1], minus))))
        plain.append((go(remote(chunk(h, 1).at[:, :, hi], a_got.at[h, 0, 1], s_a.at[h, 2], r_a.at[h, 2], plus)),
                      go(remote(chunk(h, 3).at[:, :, lo], a_got.at[h, 1, 0], s_a.at[h, 3], r_a.at[h, 3], minus))))

    def reduce_join(h):
        plus, minus = near[h]
        far[h][0].wait_recv()
        a_sum[h, 0] = (chunk(h, 1)[:, :, lo].astype(f32) + a_far[h, 0].astype(f32)).astype(bf)
        up = go(remote(a_sum.at[h, 0], a_got.at[h, 0, 0], s_a.at[h, 4], r_a.at[h, 4], plus))
        far[h][1].wait_recv()
        a_sum[h, 1] = (chunk(h, 3)[:, :, hi].astype(f32) + a_far[h, 1].astype(f32)).astype(bf)
        joined.append((up, go(remote(a_sum.at[h, 1], a_got.at[h, 1, 1], s_a.at[h, 5], r_a.at[h, 5], minus))))

    def reduce_second(h):
        for c in plain[h] + joined[h]:
            c.wait_recv()
        for n, lanes in enumerate((lo, hi)):
            t = chunk(h, 0)[:, :, lanes].astype(f32) + a_got[h, 0, n].astype(f32) + a_got[h, 1, n].astype(f32)
            b_sum[h, :, :, lanes] = t.astype(bf)
        second.append([])
        for k in (1, 3, 2):
            to, dev = (zmod(k), at_z(k)) if h == 0 else (ymod(k), at_y(k))
            second[h].append(go(remote(b_sum.at[h, to], b_got.at[h, k - 1], s_b.at[h, k], r_b.at[h, k], dev)))

    lol, hil = (lambda r: r.at[:, lo]), (lambda r: r.at[:, hi])
    e0 = Ring(go, lambda k: wc.at[0, z, ymod(k)], lol, hil, ys, yr, 0, yp, ym)
    e1 = Ring(go, lambda k: wc.at[1, zmod(k), y], lol, hil, zs, zr, 0, zp, zm)
    f0 = [Ring(go, lambda k, j=j: wc.at[0, zmod(k), ymod(j)], lol, hil, zs, zr, 4 + 4 * j, zp, zm) for j in range(4)]
    f1 = [Ring(go, lambda k, j=j: wc.at[1, zmod(j), ymod(k)], lol, hil, ys, yr, 4 + 4 * j, yp, ym) for j in range(4)]
    half = y % 2
    mine = core == y // 2
    root = jnp.logical_and(mine, x == z)
    pieces = []

    def group(late, early):
        dz = jnp.where(half == 0, late, early)
        dy = jnp.where(half == 0, early, late)
        return zmod(dz), ymod(dy)

    def along(n, k):
        gz, gy = pieces[n]
        return remote(wc.at[half, gz, gy], wr.at[gz, gy], xs.at[n, k], xrecv.at[n], (row, lax.rem(x + k, 4) * 2 + core))

    def across(n, src):
        gz, gy = pieces[n]
        return remote(src.at[gz, gy], wr.at[gz, gy], ps.at[n], pr.at[n], partner)

    def publish(*which):
        first = len(pieces)
        pieces.extend(group(*w) for w in which)

        @pl.when(root)
        def _():
            for n in range(first, len(pieces)):
                for k in (1, 3, 2):
                    along(n, k).start()
                across(n, wc.at[half]).start()

    def gather_first(h):
        for c in second[h]:
            c.wait_recv()
        t = b_sum[h, z if h == 0 else y].astype(f32)
        for k in range(3):
            t += b_got[h, k].astype(f32)
        wc[h, z, y] = t.astype(bf)
        (e0, e1)[h].start()
        (f0, f1)[h][0].start()

    def left_of(h, j):
        block = left[:, ymod(j)] if h == 0 else left[zmod(j)]
        return block.astype(f32).reshape(256, 1024).T.astype(bf)

    def right_of(h, j):
        block = right[0, :, ymod(j)] if h == 0 else right[1, zmod(j)]
        return block.astype(f32).reshape(256, 1024).astype(bf)

    def multiply(h, j):
        acc[h] += scale * jnp.dot(left_of(h, j), right_of(h, j), preferred_element_type=f32)

    def examples_of(ref, c):
        return ref[:, :, c].astype(f32).reshape(128, 1024)

    def spread_of(ref):
        total = jnp.zeros((256, 1024), f32)
        for m in range(0, 8, 2):
            pair = jnp.concatenate([proj[m + n].reshape(256, 128) for n in range(2)], axis=1)
            rows = jnp.concatenate([examples_of(ref, m + n) for n in range(2)], axis=0).astype(bf)
            total += jnp.dot(pair, rows, preferred_element_type=f32)
        return total

    reduce_first(0)
    own_right.wait()
    own_left.wait()
    for c in stage_c:
        c.wait_recv()
    a0.start(); a1.start()
    b0[0].start(); b1[0].start()
    reduce_first(1)
    for c in stage_r:
        c.wait_recv()
    xr.start()
    pp = [to_partner(0)]
    mine_t = examples_of(left, col).T.astype(bf)
    y_mine[...] = (scale * jnp.dot(qt[...], mine_t, preferred_element_type=f32)).astype(bf).reshape(16, 16, 128)
    ysum = [go(remote(y_mine.at[lax.rem(row + k, 16)], y_got.at[k], s_y.at[0, k], r_y.at[0, k],
                      (lax.rem(row + k, 16), col))) for k in range(1, 16)]
    reduce_join(0); reduce_join(1)
    a0.forward(); a1.forward()
    for j in (3, 1):
        b0[j].start(); b1[j].start()
    xr.forward()
    pp += [to_partner(3), to_partner(1)]
    reduce_second(0); reduce_second(1)
    b0[0].forward(); b1[0].forward()
    a0.finish(); a1.finish()
    b0[2].start(); b1[2].start()
    xr.finish()
    pp += [to_partner(2)]
    t = y_mine[row].astype(f32)
    for k in range(1, 16):
        ysum[k - 1].wait_recv()
        t += y_got[k].astype(f32)
    proj[col, row] = t.astype(bf)
    yall = [go(remote(proj.at[col, row], proj.at[col, row], s_y.at[1, k], r_y.at[1, k],
                      (lax.rem(row + k, 16), col))) for k in range(1, 16)]
    gather_first(0); gather_first(1)
    publish((0, 0))
    for j in (3, 1):
        b0[j].forward(); b1[j].forward()
    for c in yall:
        c.wait_recv()
    ycol = [go(remote(proj.at[col], proj.at[col], s_z.at[k], r_z.at[k], (row, lax.rem(col + k, 8))))
            for k in range(1, 8)]
    e0.forward(); e1.forward()
    for j in (3, 1):
        f0[j].start(); f1[j].start()
    publish((0, 3), (0, 1))
    for c in pp:
        c.wait_recv()
    b0[2].forward(); b1[2].forward()
    b0[0].finish(); b1[0].finish()
    multiply(0, 0)
    f0[0].forward(); f1[0].forward()
    e0.finish(); e1.finish()
    f0[2].start(); f1[2].start()
    publish((3, 0), (1, 0), (0, 2))
    multiply(1, 0)
    b0[3].finish(); b1[3].finish()
    multiply(0, 3)
    f0[3].forward(); f1[3].forward()
    publish((3, 3), (1, 3))
    multiply(1, 3)
    f0[1].forward(); f1[1].forward()
    publish((3, 1), (1, 1))
    for c in ycol:
        c.wait_recv()
    w_row[...] = spread_of(left)
    f0[2].forward(); f1[2].forward()
    publish((3, 2), (1, 2))
    b0[1].finish(); b1[1].finish()
    multiply(0, 1)
    for j in (0, 3, 1, 2):
        f0[j].finish(); f1[j].finish()
        publish((2, j))
    multiply(1, 1)
    b0[2].finish(); b1[2].finish()
    for h in range(2):
        multiply(h, 2)
        gb[h] = acc[h].astype(bf)
        w_col[h] = spread_of(right.at[h]) + wc[h].reshape(256, 1024).astype(f32)

    @pl.when(root)
    def _():
        wr[...] = wc[half]
        for n in range(16):
            for k in (1, 3, 2):
                along(n, k).wait_send()
            across(n, wc.at[half]).wait_send()

    @pl.when(jnp.logical_and(mine, x != z))
    def _():
        for n in range(16):
            along(n, 1).wait_recv()
            across(n, wr).start()
        for n in range(16):
            across(n, wr).wait_send()

    @pl.when(jnp.logical_not(mine))
    def _():
        for n in range(16):
            across(n, wr).wait_recv()

    wsum = wr[...].reshape(256, 1024).astype(f32) + w_row[...]
    wrv = wsum.astype(bf)
    v0 = jnp.dot(wrv, gb[0], preferred_element_type=f32) * w_col[0]
    v1 = jnp.dot(wrv, gb[1], preferred_element_type=f32) * w_col[1]
    curve = jnp.broadcast_to(jnp.sum(v0 + v1, axis=1, keepdims=True), (256, 128)).T
    w = wsum.T
    qv = q[...]
    once = jnp.where(col == 0, 1.0, 0.0).astype(f32)
    msg[0:1] = jnp.sum(qv * qv, axis=0, keepdims=True) * once
    msg[1:2] = jnp.sum(qv * w, axis=0, keepdims=True) * once
    msg[2:3] = jnp.sum(w * w, axis=0, keepdims=True) * once
    msg[3:4] = curve[3:4]
    cr = [go(remote(msg, got_r.at[k], s_r.at[k], r_r.at[k], (lax.rem(row + k, 16), col))) for k in range(1, 16)]
    t = msg[...]
    for k, c in enumerate(cr):
        c.wait_recv()
        t += got_r[k + 1]
    msg2[...] = t
    cc = [go(remote(msg2, got_c.at[k], s_c.at[k], r_c.at[k], (row, lax.rem(col + k, 8)))) for k in range(1, 8)]
    for k, c in enumerate(cc):
        c.wait_recv()
        t += got_c[k + 1]
    rr, qw, ww, gg = t[0:1], t[1:2], t[2:3], t[3:4]
    s1 = rr / qw
    new = s1 * s1 * ww - rr
    beta = new / rr
    up = 1.0 + beta
    s2 = new / (up * up * qw - 2.0 * up * s1 * ww + s1 * s1 * gg)
    x_out[...] = (s1 + s2 * up) * qv - (s2 * s1) * w
    for c in sends:
        c.wait_send()


def run(*args):
    dma = pltpu.SemaphoreType.DMA
    bf, f32 = jnp.bfloat16, jnp.float32
    vm = pltpu.VMEM
    hbm = pl.BlockSpec(memory_space=pl.ANY)
    return pl.pallas_call(
        kernel,
        out_shape=(vm((2, 1024, 1024), f32), vm((1024, 256), f32)),
        in_specs=[hbm] * 4 + [pl.BlockSpec(memory_space=pltpu.SMEM)] + [hbm] * 2,
        out_specs=(pl.BlockSpec(memory_space=pltpu.VMEM),) * 2,
        scratch_shapes=[vm((256, 4096), bf), vm((256, 4096), bf), vm((4096, 128), bf), vm((4096, 128), bf),
                        vm((1024, 2048), f32), vm((1024, 256), f32), vm((16, 8, 1024), bf),
                        vm((4, 4, 8, 8, 1024), bf), vm((2, 4, 4, 8, 8, 1024), bf), vm((256, 1024), bf),
                        vm((16, 16, 128), bf), vm((16, 16, 128), bf), vm((8, 16, 16, 128), bf), vm((256, 1024), f32),
                        vm((2, 256, 1024), f32),
                        vm((2, 1024, 1024), bf), vm((2, 4, 4, 16, 1024), bf),
                        vm((2, 2, 4, 16, 512), bf), vm((2, 2, 2, 4, 16, 512), bf), vm((2, 2, 4, 16, 512), bf),
                        vm((2, 4, 16, 1024), bf), vm((2, 3, 16, 1024), bf), vm((2, 4, 4, 16, 1024), bf),
                        vm((4, 4, 16, 1024), bf),
                        vm((4, 256), f32), vm((16, 4, 256), f32), vm((4, 256), f32), vm((8, 4, 256), f32),
                        dma((6,)), dma((2,)), dma((8,)), dma((8,)), dma((16,)), dma((16,)),
                        dma((20,)), dma((20,)), dma((20,)), dma((20,)), dma((4,)), dma((4,)), dma((4,)), dma((4,)),
                        dma((2, 16)), dma((2, 16)), dma((8,)), dma((8,)),
                        dma((2, 6)), dma((2, 6)), dma((2, 4)), dma((2, 4)), dma((20,)), dma((20,)), dma((20,)), dma((20,)),
                        dma((16, 4)), dma((16,)), dma((16,)), dma((16,)), dma((16,)), dma((16,)), dma((8,)), dma((8,))],
        compiler_params=pltpu.CompilerParams(collective_id=0, has_side_effects=True, vmem_limit_bytes=44 * 1024 * 1024),
        name="influence",
    )(*args)


def store_kernel(g, x, g_out, x_out, sem):
    copies = [pltpu.make_async_copy(g.at[h, pl.ds(n * 256, 256)], g_out.at[pl.ds(n * 256, 256), pl.ds(h * 1024, 1024)],
                                    sem.at[4 * h + n]) for h in range(2) for n in range(4)]
    copies.append(pltpu.make_async_copy(x, x_out, sem.at[8]))
    for c in copies:
        c.start()
    for c in copies:
        c.wait()


def store(g, x):
    f32 = jnp.float32
    inside, hbm = pl.BlockSpec(memory_space=pltpu.VMEM), pl.BlockSpec(memory_space=pltpu.HBM)
    return pl.pallas_call(
        store_kernel,
        out_shape=(jax.ShapeDtypeStruct((1024, 2048), f32), jax.ShapeDtypeStruct((1024, 256), f32)),
        in_specs=[inside] * 2,
        out_specs=(hbm, hbm),
        scratch_shapes=[pltpu.SemaphoreType.DMA((9,))],
        compiler_params=pltpu.CompilerParams(vmem_limit_bytes=16 * 1024 * 1024),
        name="store",
    )(pltpu.with_memory_space_constraint(g, pltpu.VMEM), pltpu.with_memory_space_constraint(x, pltpu.VMEM))


def whole(*args):
    return store(*run(*args))


def solution(mesh):
    in_specs = (
        P(("row", "col"), None),
        P(("row", "col"), None),
        P(),
        P(),
        P(("row", "col")),
        P("row", "col"),
        P("row", None),
    )
    out_specs = (P("row", "col"), P("row", None))
    return jax.shard_map(whole, mesh=mesh, in_specs=in_specs, out_specs=out_specs, check_vma=False)
```

```python
import functools

import jax
import jax.numpy as jnp
from jax import lax
from jax.experimental import pallas as pl
from jax.experimental.pallas import tpu as pltpu
from jax.sharding import PartitionSpec as P

MESH = pl.DeviceIdType.MESH
SEQ = 32
ITERS = 2
decay_rate = 0.5
damping = 1.0
HBM = pl.ANY


class Ring:
    def __init__(self, go, slot, lo, hi, ss, rs, base, plus, minus):
        self.go, self.slot, self.lo, self.hi = go, slot, lo, hi
        self.ss, self.rs, self.base = ss, rs, base
        self.plus, self.minus = plus, minus

    def copy(self, ref, k, dev):
        return self.go(pltpu.make_async_remote_copy(
            src_ref=ref, dst_ref=ref, send_sem=self.ss.at[self.base + k], recv_sem=self.rs.at[self.base + k],
            device_id=dev, device_id_type=MESH))

    def start(self):
        own = self.slot(0)
        self.f0 = self.copy(own, 0, self.plus)
        self.f1 = self.copy(own, 1, self.minus)

    def forward(self):
        self.f0.wait_recv()
        self.h0 = self.copy(self.lo(self.slot(3)), 2, self.plus)
        self.f1.wait_recv()
        self.h1 = self.copy(self.hi(self.slot(1)), 3, self.minus)

    def finish(self):
        self.h0.wait_recv()
        self.h1.wait_recv()


def greet(row, col):
    barrier = pltpu.get_barrier_semaphore()
    for k in range(1, 8):
        pl.semaphore_signal(barrier, inc=1, device_id=(row, lax.rem(col + k, 8)), device_id_type=MESH)
    for k in range(1, 16):
        pl.semaphore_signal(barrier, inc=1, device_id=(lax.rem(row + k, 16), col), device_id_type=MESH)
    return barrier


def kernel(act, og, p_in, p_out, lens, old_hbm, q_hbm, acc, x_out,
           act_v, og_v, pin_v, pout_v, old, q, lg, left, right, qt, y_mine, y_got, proj, w_row, w_col, last, gb, part,
           a_far, a_got, a_sum, b_sum, b_got, wc, wr, msg, got_r, msg2, got_c,
           in_sem, loc_sem, c_send, c_recv, r_send, r_recv, ya_send, ya_recv, za_send, za_recv,
           x_send, x_recv, p_send, p_recv,
           s_y, r_y, s_z, r_z, s_a, r_a, s_b, r_b, ys, yr, zs, zr, xs, xrecv, ps, pr, s_r, r_r, s_c, r_c):
    f32, bf = jnp.float32, jnp.bfloat16
    row = lax.axis_index("row")
    col = lax.axis_index("col")
    z, y = row // 4, row % 4
    x, core = col // 2, col % 2
    barrier = greet(row, col)
    loads = [pltpu.make_async_copy(a, b, in_sem.at[n]) for n, (a, b) in enumerate(
        ((p_out, pout_v), (og, og_v), (p_in, pin_v), (act, act_v), (q_hbm, q), (old_hbm, old)))]
    for c in loads[:4]:
        c.start()
    sends = []

    def go(copy):
        copy.start()
        sends.append(copy)
        return copy

    def remote(src, dst, ssem, rsem, dev):
        return pltpu.make_async_remote_copy(src_ref=src, dst_ref=dst, send_sem=ssem, recv_sem=rsem,
                                            device_id=dev, device_id_type=MESH)

    def ymod(k):
        return lax.rem(y + k, 4)

    def zmod(k):
        return lax.rem(z + k, 4)

    def at_y(k):
        return (z * 4 + ymod(k), col)

    def at_z(k):
        return (zmod(k) * 4 + y, col)

    loads[0].wait()
    loads[1].wait()
    loads[4].start()
    loads[5].start()
    low_out = jnp.dot(og_v[...], pout_v[...], preferred_element_type=f32).astype(bf).astype(f32).T
    ex = lax.broadcasted_iota(jnp.int32, (8, 256), 0)
    slot = lax.broadcasted_iota(jnp.int32, (8, 256), 1) - SEQ * ex
    count = jnp.zeros((8, 256), jnp.int32)
    for e in range(8):
        count = jnp.where(ex == e, lens[e], count)
    valid = jnp.logical_and(slot >= 0, slot < jnp.minimum(count, SEQ))
    spread = jnp.where(valid[None], low_out[:, None, :], 0.0).reshape(1024, 256).astype(bf)
    loads[2].wait()
    loads[3].wait()
    low_in = jnp.dot(act_v[...], pin_v[...], preferred_element_type=f32).astype(bf)
    grads = jnp.dot(spread, low_in, preferred_element_type=f32).reshape(16, 8, 8, 128)
    for j in range(8):
        lg[:, :, pl.ds(j * 128, 128)] = grads[:, j].astype(bf)
    loads[4].wait()
    q16 = q[...].T.astype(bf)
    qt[...] = q16
    scale = (1.0 - decay_rate) / 1024

    def begin(h):
        ri = lax.broadcasted_iota(jnp.int32, (1024, 1024), 0) + row * 1024
        ci = lax.broadcasted_iota(jnp.int32, (1024, 1024), 1) + (col * 2048 + h * 1024)
        g = decay_rate * old[:, pl.ds(h * 1024, 1024)] + jnp.where(ri == ci, damping, 0.0).astype(f32)
        acc[h] = g
        pt = jnp.dot(qt[...], g.astype(bf), preferred_element_type=f32)
        part[h] = pt.astype(bf).reshape(4, 4, 16, 1024)

    loads[5].wait()
    begin(0)
    pl.semaphore_wait(barrier, 22)

    yp, ym, zp, zm = at_y(1), at_y(3), at_z(1), at_z(3)
    xp = (row, lax.rem(x + 1, 4) * 2 + core)
    xm = (row, lax.rem(x + 3, 4) * 2 + core)
    partner = (row, x * 2 + 1 - core)
    lo5, hi5 = (lambda r: r.at[pl.ds(0, 4)]), (lambda r: r.at[pl.ds(4, 4)])
    a0 = Ring(go, lambda k: right.at[0, z, ymod(k)], lo5, hi5, ya_send, ya_recv, 0, yp, ym)
    a1 = Ring(go, lambda k: right.at[1, zmod(k), y], lo5, hi5, za_send, za_recv, 0, zp, zm)
    b0 = [Ring(go, lambda k, j=j: right.at[0, zmod(k), ymod(j)], lo5, hi5, za_send, za_recv, 4 + 4 * j, zp, zm)
          for j in range(4)]
    b1 = [Ring(go, lambda k, j=j: right.at[1, zmod(j), ymod(k)], lo5, hi5, ya_send, ya_recv, 4 + 4 * j, yp, ym)
          for j in range(4)]
    xr = Ring(go, lambda k: left.at[:, :, lax.rem(x + k, 4) * 2 + core], lambda r: r.at[pl.ds(0, 2)],
              lambda r: r.at[pl.ds(2, 2)], x_send, x_recv, 0, xp, xm)

    def to_partner(k):
        c = left.at[:, :, lax.rem(x + k, 4) * 2 + core]
        return go(remote(c, c, p_send.at[k], p_recv.at[k], partner))

    lo, hi = pl.ds(0, 512), pl.ds(512, 512)

    def chunk(h, k):
        return part.at[0, :, ymod(k)] if h == 0 else part.at[1, zmod(k)]

    near = ((yp, ym), (zp, zm))
    far, plain, joined, second = [], [], [], []

    def reduce_first(h):
        plus, minus = near[h]
        far.append((go(remote(chunk(h, 2).at[:, :, lo], a_far.at[h, 0], s_a.at[h, 0], r_a.at[h, 0], plus)),
                    go(remote(chunk(h, 2).at[:, :, hi], a_far.at[h, 1], s_a.at[h, 1], r_a.at[h, 1], minus))))
        plain.append((go(remote(chunk(h, 1).at[:, :, hi], a_got.at[h, 0, 1], s_a.at[h, 2], r_a.at[h, 2], plus)),
                      go(remote(chunk(h, 3).at[:, :, lo], a_got.at[h, 1, 0], s_a.at[h, 3], r_a.at[h, 3], minus))))

    def reduce_join(h):
        plus, minus = near[h]
        far[h][0].wait_recv()
        a_sum[h, 0] = (chunk(h, 1)[:, :, lo].astype(f32) + a_far[h, 0].astype(f32)).astype(bf)
        up = go(remote(a_sum.at[h, 0], a_got.at[h, 0, 0], s_a.at[h, 4], r_a.at[h, 4], plus))
        far[h][1].wait_recv()
        a_sum[h, 1] = (chunk(h, 3)[:, :, hi].astype(f32) + a_far[h, 1].astype(f32)).astype(bf)
        joined.append((up, go(remote(a_sum.at[h, 1], a_got.at[h, 1, 1], s_a.at[h, 5], r_a.at[h, 5], minus))))

    def reduce_second(h):
        for c in plain[h] + joined[h]:
            c.wait_recv()
        for n, lanes in enumerate((lo, hi)):
            t = chunk(h, 0)[:, :, lanes].astype(f32) + a_got[h, 0, n].astype(f32) + a_got[h, 1, n].astype(f32)
            b_sum[h, :, :, lanes] = t.astype(bf)
        second.append([])
        for k in (1, 3, 2):
            to, dev = (zmod(k), at_z(k)) if h == 0 else (ymod(k), at_y(k))
            second[h].append(go(remote(b_sum.at[h, to], b_got.at[h, k - 1], s_b.at[h, k], r_b.at[h, k], dev)))

    lol, hil = (lambda r: r.at[:, lo]), (lambda r: r.at[:, hi])
    e0 = Ring(go, lambda k: wc.at[0, z, ymod(k)], lol, hil, ys, yr, 0, yp, ym)
    e1 = Ring(go, lambda k: wc.at[1, zmod(k), y], lol, hil, zs, zr, 0, zp, zm)
    f0 = [Ring(go, lambda k, j=j: wc.at[0, zmod(k), ymod(j)], lol, hil, zs, zr, 4 + 4 * j, zp, zm) for j in range(4)]
    f1 = [Ring(go, lambda k, j=j: wc.at[1, zmod(j), ymod(k)], lol, hil, ys, yr, 4 + 4 * j, yp, ym) for j in range(4)]
    half = y % 2
    mine = core == y // 2
    root = jnp.logical_and(mine, x == z)
    pieces = []

    def group(late, early):
        dz = jnp.where(half == 0, late, early)
        dy = jnp.where(half == 0, early, late)
        return zmod(dz), ymod(dy)

    def along(n, k):
        gz, gy = pieces[n]
        return remote(wc.at[half, gz, gy], wr.at[gz, gy], xs.at[n, k], xrecv.at[n], (row, lax.rem(x + k, 4) * 2 + core))

    def across(n, src):
        gz, gy = pieces[n]
        return remote(src.at[gz, gy], wr.at[gz, gy], ps.at[n], pr.at[n], partner)

    def publish(*which):
        first = len(pieces)
        pieces.extend(group(*w) for w in which)

        @pl.when(root)
        def _():
            for n in range(first, len(pieces)):
                for k in (1, 3, 2):
                    along(n, k).start()
                across(n, wc.at[half]).start()

    def gather_first(h):
        for c in second[h]:
            c.wait_recv()
        t = b_sum[h, z if h == 0 else y].astype(f32)
        for k in range(3):
            t += b_got[h, k].astype(f32)
        wc[h, z, y] = t.astype(bf)
        (e0, e1)[h].start()
        (f0, f1)[h][0].start()

    def left_of(h, j):
        block = left[:, ymod(j)] if h == 0 else left[zmod(j)]
        return block.astype(f32).reshape(256, 1024).T.astype(bf)

    def right_of(h, j):
        block = right[0, :, ymod(j)] if h == 0 else right[1, zmod(j)]
        return block.astype(f32).reshape(256, 1024).astype(bf)

    def multiply(h, j):
        acc[h] += scale * jnp.dot(left_of(h, j), right_of(h, j), preferred_element_type=f32)

    def examples_of(ref, c):
        return ref[:, :, c].astype(f32).reshape(128, 1024)

    def spread_of(ref):
        total = jnp.zeros((256, 1024), f32)
        for m in range(0, 8, 2):
            pair = jnp.concatenate([proj[m + n].reshape(256, 128) for n in range(2)], axis=1)
            rows = jnp.concatenate([examples_of(ref, m + n) for n in range(2)], axis=0).astype(bf)
            total += jnp.dot(pair, rows, preferred_element_type=f32)
        return total

    own_right = pltpu.make_async_copy(lg.at[pl.ds(2 * col, 2)], right.at[:, z, y, col], loc_sem.at[0])
    own_right.start()
    own_left = pltpu.make_async_copy(lg.at[row], left.at[z, y, col], loc_sem.at[1])
    own_left.start()
    stage_c, stage_r = [], []
    for k in (2, 6, 1, 7, 3, 5, 4):
        to = lax.rem(col + k, 8)
        stage_c.append(go(remote(lg.at[pl.ds(2 * to, 2)], right.at[:, z, y, col],
                                 c_send.at[k], c_recv.at[k], (row, to))))
    for k in range(1, 16):
        to = lax.rem(row + k, 16)
        stage_r.append(go(remote(lg.at[to], left.at[z, y, col], r_send.at[k], r_recv.at[k], (to, col))))
    reduce_first(0)
    begin(1)
    reduce_first(1)
    own_right.wait()
    own_left.wait()
    for c in stage_c:
        c.wait_recv()
    a0.start(); a1.start()
    b0[0].start(); b1[0].start()
    for c in stage_r:
        c.wait_recv()
    xr.start()
    pp = [to_partner(0)]
    mine_t = examples_of(left, col).T.astype(bf)
    y_mine[...] = (scale * jnp.dot(qt[...], mine_t, preferred_element_type=f32)).astype(bf).reshape(16, 16, 128)
    ysum = [go(remote(y_mine.at[lax.rem(row + k, 16)], y_got.at[k], s_y.at[0, k], r_y.at[0, k],
                      (lax.rem(row + k, 16), col))) for k in range(1, 16)]
    reduce_join(0); reduce_join(1)
    a0.forward(); a1.forward()
    for j in (3, 1):
        b0[j].start(); b1[j].start()
    xr.forward()
    pp += [to_partner(3), to_partner(1)]
    reduce_second(0); reduce_second(1)
    b0[0].forward(); b1[0].forward()
    a0.finish(); a1.finish()
    b0[2].start(); b1[2].start()
    xr.finish()
    pp += [to_partner(2)]
    t = y_mine[row].astype(f32)
    for k in range(1, 16):
        ysum[k - 1].wait_recv()
        t += y_got[k].astype(f32)
    proj[col, row] = t.astype(bf)
    yall = [go(remote(proj.at[col, row], proj.at[col, row], s_y.at[1, k], r_y.at[1, k],
                      (lax.rem(row + k, 16), col))) for k in range(1, 16)]
    gather_first(0); gather_first(1)
    publish((0, 0))
    for j in (3, 1):
        b0[j].forward(); b1[j].forward()
    for c in yall:
        c.wait_recv()
    ycol = [go(remote(proj.at[col], proj.at[col], s_z.at[k], r_z.at[k], (row, lax.rem(col + k, 8))))
            for k in range(1, 8)]
    e0.forward(); e1.forward()
    for j in (3, 1):
        f0[j].start(); f1[j].start()
    publish((0, 3), (0, 1))
    for c in pp:
        c.wait_recv()
    b0[2].forward(); b1[2].forward()
    b0[0].finish(); b1[0].finish()
    multiply(0, 0)
    f0[0].forward(); f1[0].forward()
    e0.finish(); e1.finish()
    f0[2].start(); f1[2].start()
    publish((3, 0), (1, 0), (0, 2))
    multiply(1, 0)
    b0[3].finish(); b1[3].finish()
    multiply(0, 3)
    f0[3].forward(); f1[3].forward()
    publish((3, 3), (1, 3))
    multiply(1, 3)
    f0[1].forward(); f1[1].forward()
    publish((3, 1), (1, 1))
    for c in ycol:
        c.wait_recv()
    w_row[...] = spread_of(left)
    f0[2].forward(); f1[2].forward()
    publish((3, 2), (1, 2))
    b0[1].finish(); b1[1].finish()
    multiply(0, 1)
    for j in (0, 3, 1, 2):
        f0[j].finish(); f1[j].finish()
        publish((2, j))
    multiply(1, 1)
    for h in range(2):
        gb[h] = acc[h].astype(bf)
        last[h] = left_of(h, 2)
    b0[2].finish(); b1[2].finish()
    for h in range(2):
        w_col[h] = spread_of(right.at[h]) + wc[h].reshape(256, 1024).astype(f32)

    @pl.when(root)
    def _():
        wr[...] = wc[half]
        for n in range(16):
            for k in (1, 3, 2):
                along(n, k).wait_send()
            across(n, wc.at[half]).wait_send()

    @pl.when(jnp.logical_and(mine, x != z))
    def _():
        for n in range(16):
            along(n, 1).wait_recv()
            across(n, wr).start()
        for n in range(16):
            across(n, wr).wait_send()

    @pl.when(jnp.logical_not(mine))
    def _():
        for n in range(16):
            across(n, wr).wait_recv()

    wsum = wr[...].reshape(256, 1024).astype(f32) + w_row[...]
    wrv = wsum.astype(bf)
    v = jnp.zeros((256, 1024), f32)
    for h in range(2):
        u = (scale * jnp.dot(wrv, last[h], preferred_element_type=f32)).astype(bf)
        v += (jnp.dot(wrv, gb[h], preferred_element_type=f32)
              + jnp.dot(u, right_of(h, 2), preferred_element_type=f32)) * w_col[h]
    curve = jnp.broadcast_to(jnp.sum(v, axis=1, keepdims=True), (256, 128)).T
    w = wsum.T
    qv = q[...]
    once = jnp.where(col == 0, 1.0, 0.0).astype(f32)
    msg[0:1] = jnp.sum(qv * qv, axis=0, keepdims=True) * once
    msg[1:2] = jnp.sum(qv * w, axis=0, keepdims=True) * once
    msg[2:3] = jnp.sum(w * w, axis=0, keepdims=True) * once
    msg[3:4] = curve[3:4]
    cr = [go(remote(msg, got_r.at[k], s_r.at[k], r_r.at[k], (lax.rem(row + k, 16), col))) for k in range(1, 16)]
    for h in range(2):
        acc[h] += scale * jnp.dot(last[h], right_of(h, 2), preferred_element_type=f32)
    t = msg[...]
    for k, c in enumerate(cr):
        c.wait_recv()
        t += got_r[k + 1]
    msg2[...] = t
    cc = [go(remote(msg2, got_c.at[k], s_c.at[k], r_c.at[k], (row, lax.rem(col + k, 8)))) for k in range(1, 8)]
    for k, c in enumerate(cc):
        c.wait_recv()
        t += got_c[k + 1]
    rr, qw, ww, gg = t[0:1], t[1:2], t[2:3], t[3:4]
    s1 = rr / qw
    new = s1 * s1 * ww - rr
    beta = new / rr
    up = 1.0 + beta
    s2 = new / (up * up * qw - 2.0 * up * s1 * ww + s1 * s1 * gg)
    x_out[...] = (s1 + s2 * up) * qv - (s2 * s1) * w
    for c in sends:
        c.wait_send()


def run(*args):
    dma = pltpu.SemaphoreType.DMA
    bf, f32 = jnp.bfloat16, jnp.float32
    vm = pltpu.VMEM
    hbm = pl.BlockSpec(memory_space=pl.ANY)
    return pl.pallas_call(
        kernel,
        out_shape=(vm((2, 1024, 1024), f32), vm((1024, 256), f32)),
        in_specs=[hbm] * 4 + [pl.BlockSpec(memory_space=pltpu.SMEM)] + [hbm] * 2,
        out_specs=(pl.BlockSpec(memory_space=pltpu.VMEM),) * 2,
        scratch_shapes=[vm((256, 4096), bf), vm((256, 4096), bf), vm((4096, 128), bf), vm((4096, 128), bf),
                        vm((1024, 2048), f32), vm((1024, 256), f32), vm((16, 8, 1024), bf),
                        vm((4, 4, 8, 8, 1024), bf), vm((2, 4, 4, 8, 8, 1024), bf), vm((256, 1024), bf),
                        vm((16, 16, 128), bf), vm((16, 16, 128), bf), vm((8, 16, 16, 128), bf), vm((256, 1024), f32),
                        vm((2, 256, 1024), f32), vm((2, 1024, 256), bf),
                        vm((2, 1024, 1024), bf), vm((2, 4, 4, 16, 1024), bf),
                        vm((2, 2, 4, 16, 512), bf), vm((2, 2, 2, 4, 16, 512), bf), vm((2, 2, 4, 16, 512), bf),
                        vm((2, 4, 16, 1024), bf), vm((2, 3, 16, 1024), bf), vm((2, 4, 4, 16, 1024), bf),
                        vm((4, 4, 16, 1024), bf),
                        vm((4, 256), f32), vm((16, 4, 256), f32), vm((4, 256), f32), vm((8, 4, 256), f32),
                        dma((6,)), dma((2,)), dma((8,)), dma((8,)), dma((16,)), dma((16,)),
                        dma((20,)), dma((20,)), dma((20,)), dma((20,)), dma((4,)), dma((4,)), dma((4,)), dma((4,)),
                        dma((2, 16)), dma((2, 16)), dma((8,)), dma((8,)),
                        dma((2, 6)), dma((2, 6)), dma((2, 4)), dma((2, 4)), dma((20,)), dma((20,)), dma((20,)), dma((20,)),
                        dma((16, 4)), dma((16,)), dma((16,)), dma((16,)), dma((16,)), dma((16,)), dma((8,)), dma((8,))],
        compiler_params=pltpu.CompilerParams(collective_id=0, has_side_effects=True, vmem_limit_bytes=44 * 1024 * 1024),
        name="influence",
    )(*args)


def store_kernel(g, x, g_out, x_out, sem):
    copies = [pltpu.make_async_copy(g.at[h, pl.ds(n * 256, 256)], g_out.at[pl.ds(n * 256, 256), pl.ds(h * 1024, 1024)],
                                    sem.at[4 * h + n]) for h in range(2) for n in range(4)]
    copies.append(pltpu.make_async_copy(x, x_out, sem.at[8]))
    for c in copies:
        c.start()
    for c in copies:
        c.wait()


def store(g, x):
    f32 = jnp.float32
    inside, hbm = pl.BlockSpec(memory_space=pltpu.VMEM), pl.BlockSpec(memory_space=pltpu.HBM)
    return pl.pallas_call(
        store_kernel,
        out_shape=(jax.ShapeDtypeStruct((1024, 2048), f32), jax.ShapeDtypeStruct((1024, 256), f32)),
        in_specs=[inside] * 2,
        out_specs=(hbm, hbm),
        scratch_shapes=[pltpu.SemaphoreType.DMA((9,))],
        compiler_params=pltpu.CompilerParams(vmem_limit_bytes=16 * 1024 * 1024),
        name="store",
    )(pltpu.with_memory_space_constraint(g, pltpu.VMEM), pltpu.with_memory_space_constraint(x, pltpu.VMEM))


def whole(*args):
    return store(*run(*args))


def solution(mesh):
    in_specs = (
        P(("row", "col"), None),
        P(("row", "col"), None),
        P(),
        P(),
        P(("row", "col")),
        P("row", "col"),
        P("row", None),
    )
    out_specs = (P("row", "col"), P("row", None))
    return jax.shard_map(whole, mesh=mesh, in_specs=in_specs, out_specs=out_specs, check_vma=False)
```

```python
import functools

import jax
import jax.numpy as jnp
from jax import lax
from jax.experimental import pallas as pl
from jax.experimental.pallas import tpu as pltpu
from jax.sharding import PartitionSpec as P

MESH = pl.DeviceIdType.MESH
SEQ = 32
ITERS = 2
decay_rate = 0.5
damping = 1.0
HBM = pl.ANY


class Ring:
    def __init__(self, go, slot, lo, hi, ss, rs, base, plus, minus):
        self.go, self.slot, self.lo, self.hi = go, slot, lo, hi
        self.ss, self.rs, self.base = ss, rs, base
        self.plus, self.minus = plus, minus

    def copy(self, ref, k, dev):
        return self.go(pltpu.make_async_remote_copy(
            src_ref=ref, dst_ref=ref, send_sem=self.ss.at[self.base + k], recv_sem=self.rs.at[self.base + k],
            device_id=dev, device_id_type=MESH))

    def start(self):
        own = self.slot(0)
        self.f0 = self.copy(own, 0, self.plus)
        self.f1 = self.copy(own, 1, self.minus)

    def forward(self):
        self.f0.wait_recv()
        self.h0 = self.copy(self.lo(self.slot(3)), 2, self.plus)
        self.f1.wait_recv()
        self.h1 = self.copy(self.hi(self.slot(1)), 3, self.minus)

    def finish(self):
        self.h0.wait_recv()
        self.h1.wait_recv()


def greet(row, col):
    barrier = pltpu.get_barrier_semaphore()
    for k in range(1, 8):
        pl.semaphore_signal(barrier, inc=1, device_id=(row, lax.rem(col + k, 8)), device_id_type=MESH)
    for k in range(1, 16):
        pl.semaphore_signal(barrier, inc=1, device_id=(lax.rem(row + k, 16), col), device_id_type=MESH)
    return barrier


def kernel(act, og, p_in, p_out, lens, old_hbm, q_hbm, acc, x_out,
           act_v, og_v, pin_v, pout_v, old, q, lg, left, right, qt, y_mine, y_got, proj, w_row, w_col, last, gb, part,
           a_far, a_got, a_sum, b_sum, b_got, wc, wr, msg, got_r, msg2, got_c,
           in_sem, loc_sem, c_send, c_recv, r_send, r_recv, ya_send, ya_recv, za_send, za_recv,
           x_send, x_recv, p_send, p_recv,
           s_y, r_y, s_z, r_z, s_a, r_a, s_b, r_b, ys, yr, zs, zr, xs, xrecv, ps, pr, s_r, r_r, s_c, r_c):
    f32, bf = jnp.float32, jnp.bfloat16
    row = lax.axis_index("row")
    col = lax.axis_index("col")
    z, y = row // 4, row % 4
    x, core = col // 2, col % 2
    barrier = greet(row, col)
    loads = [pltpu.make_async_copy(a, b, in_sem.at[n]) for n, (a, b) in enumerate(
        ((p_out, pout_v), (og, og_v), (p_in, pin_v), (act, act_v), (q_hbm, q), (old_hbm, old)))]
    for c in loads[:4]:
        c.start()
    sends = []

    def go(copy):
        copy.start()
        sends.append(copy)
        return copy

    def remote(src, dst, ssem, rsem, dev):
        return pltpu.make_async_remote_copy(src_ref=src, dst_ref=dst, send_sem=ssem, recv_sem=rsem,
                                            device_id=dev, device_id_type=MESH)

    def ymod(k):
        return lax.rem(y + k, 4)

    def zmod(k):
        return lax.rem(z + k, 4)

    def at_y(k):
        return (z * 4 + ymod(k), col)

    def at_z(k):
        return (zmod(k) * 4 + y, col)

    loads[0].wait()
    loads[1].wait()
    loads[4].start()
    loads[5].start()
    low_out = jnp.dot(og_v[...], pout_v[...], preferred_element_type=f32).astype(bf).astype(f32).T
    ex = lax.broadcasted_iota(jnp.int32, (8, 256), 0)
    slot = lax.broadcasted_iota(jnp.int32, (8, 256), 1) - SEQ * ex
    count = jnp.zeros((8, 256), jnp.int32)
    for e in range(8):
        count = jnp.where(ex == e, lens[e], count)
    valid = jnp.logical_and(slot >= 0, slot < jnp.minimum(count, SEQ))
    spread = jnp.where(valid[None], low_out[:, None, :], 0.0).reshape(1024, 256).astype(bf)
    loads[2].wait()
    loads[3].wait()
    low_in = jnp.dot(act_v[...], pin_v[...], preferred_element_type=f32).astype(bf)
    grads = jnp.dot(spread, low_in, preferred_element_type=f32).reshape(16, 8, 8, 128)
    for j in range(8):
        lg[:, :, pl.ds(j * 128, 128)] = grads[:, j].astype(bf)
    loads[4].wait()
    q16 = q[...].T.astype(bf)
    qt[...] = q16
    scale = (1.0 - decay_rate) / 1024

    def begin(h):
        ri = lax.broadcasted_iota(jnp.int32, (1024, 1024), 0) + row * 1024
        ci = lax.broadcasted_iota(jnp.int32, (1024, 1024), 1) + (col * 2048 + h * 1024)
        g = decay_rate * old[:, pl.ds(h * 1024, 1024)] + jnp.where(ri == ci, damping, 0.0).astype(f32)
        acc[h] = g
        pt = jnp.dot(qt[...], g.astype(bf), preferred_element_type=f32)
        part[h] = pt.astype(bf).reshape(4, 4, 16, 1024)

    loads[5].wait()
    begin(0)
    pl.semaphore_wait(barrier, 22)

    yp, ym, zp, zm = at_y(1), at_y(3), at_z(1), at_z(3)
    xp = (row, lax.rem(x + 1, 4) * 2 + core)
    xm = (row, lax.rem(x + 3, 4) * 2 + core)
    partner = (row, x * 2 + 1 - core)
    lo5, hi5 = (lambda r: r.at[pl.ds(0, 4)]), (lambda r: r.at[pl.ds(4, 4)])
    a0 = Ring(go, lambda k: right.at[0, z, ymod(k)], lo5, hi5, ya_send, ya_recv, 0, yp, ym)
    a1 = Ring(go, lambda k: right.at[1, zmod(k), y], lo5, hi5, za_send, za_recv, 0, zp, zm)
    b0 = [Ring(go, lambda k, j=j: right.at[0, zmod(k), ymod(j)], lo5, hi5, za_send, za_recv, 4 + 4 * j, zp, zm)
          for j in range(4)]
    b1 = [Ring(go, lambda k, j=j: right.at[1, zmod(j), ymod(k)], lo5, hi5, ya_send, ya_recv, 4 + 4 * j, yp, ym)
          for j in range(4)]
    xr = Ring(go, lambda k: left.at[:, :, lax.rem(x + k, 4) * 2 + core], lambda r: r.at[pl.ds(0, 2)],
              lambda r: r.at[pl.ds(2, 2)], x_send, x_recv, 0, xp, xm)

    def to_partner(k):
        c = left.at[:, :, lax.rem(x + k, 4) * 2 + core]
        return go(remote(c, c, p_send.at[k], p_recv.at[k], partner))

    lo, hi = pl.ds(0, 512), pl.ds(512, 512)

    def chunk(h, k):
        return part.at[0, :, ymod(k)] if h == 0 else part.at[1, zmod(k)]

    near = ((yp, ym), (zp, zm))
    far, plain, joined, second = [], [], [], []

    def reduce_first(h):
        plus, minus = near[h]
        far.append((go(remote(chunk(h, 2).at[:, :, lo], a_far.at[h, 0], s_a.at[h, 0], r_a.at[h, 0], plus)),
                    go(remote(chunk(h, 2).at[:, :, hi], a_far.at[h, 1], s_a.at[h, 1], r_a.at[h, 1], minus))))
        plain.append((go(remote(chunk(h, 1).at[:, :, hi], a_got.at[h, 0, 1], s_a.at[h, 2], r_a.at[h, 2], plus)),
                      go(remote(chunk(h, 3).at[:, :, lo], a_got.at[h, 1, 0], s_a.at[h, 3], r_a.at[h, 3], minus))))

    def reduce_join(h):
        plus, minus = near[h]
        far[h][0].wait_recv()
        a_sum[h, 0] = (chunk(h, 1)[:, :, lo].astype(f32) + a_far[h, 0].astype(f32)).astype(bf)
        up = go(remote(a_sum.at[h, 0], a_got.at[h, 0, 0], s_a.at[h, 4], r_a.at[h, 4], plus))
        far[h][1].wait_recv()
        a_sum[h, 1] = (chunk(h, 3)[:, :, hi].astype(f32) + a_far[h, 1].astype(f32)).astype(bf)
        joined.append((up, go(remote(a_sum.at[h, 1], a_got.at[h, 1, 1], s_a.at[h, 5], r_a.at[h, 5], minus))))

    def reduce_second(h):
        for c in plain[h] + joined[h]:
            c.wait_recv()
        for n, lanes in enumerate((lo, hi)):
            t = chunk(h, 0)[:, :, lanes].astype(f32) + a_got[h, 0, n].astype(f32) + a_got[h, 1, n].astype(f32)
            b_sum[h, :, :, lanes] = t.astype(bf)
        second.append([])
        for k in (1, 3, 2):
            to, dev = (zmod(k), at_z(k)) if h == 0 else (ymod(k), at_y(k))
            second[h].append(go(remote(b_sum.at[h, to], b_got.at[h, k - 1], s_b.at[h, k], r_b.at[h, k], dev)))

    lol, hil = (lambda r: r.at[:, lo]), (lambda r: r.at[:, hi])
    e0 = Ring(go, lambda k: wc.at[0, z, ymod(k)], lol, hil, ys, yr, 0, yp, ym)
    e1 = Ring(go, lambda k: wc.at[1, zmod(k), y], lol, hil, zs, zr, 0, zp, zm)
    f0 = [Ring(go, lambda k, j=j: wc.at[0, zmod(k), ymod(j)], lol, hil, zs, zr, 4 + 4 * j, zp, zm) for j in range(4)]
    f1 = [Ring(go, lambda k, j=j: wc.at[1, zmod(j), ymod(k)], lol, hil, ys, yr, 4 + 4 * j, yp, ym) for j in range(4)]
    half = y % 2
    mine = core == y // 2
    root = jnp.logical_and(mine, x == z)
    pieces = []

    def group(late, early):
        dz = jnp.where(half == 0, late, early)
        dy = jnp.where(half == 0, early, late)
        return zmod(dz), ymod(dy)

    def along(n, k):
        gz, gy = pieces[n]
        return remote(wc.at[half, gz, gy], wr.at[gz, gy], xs.at[n, k], xrecv.at[n], (row, lax.rem(x + k, 4) * 2 + core))

    def across(n, src):
        gz, gy = pieces[n]
        return remote(src.at[gz, gy], wr.at[gz, gy], ps.at[n], pr.at[n], partner)

    def publish(*which):
        first = len(pieces)
        pieces.extend(group(*w) for w in which)

        @pl.when(root)
        def _():
            for n in range(first, len(pieces)):
                for k in (1, 3, 2):
                    along(n, k).start()
                across(n, wc.at[half]).start()

    def gather_first(h):
        for c in second[h]:
            c.wait_recv()
        t = b_sum[h, z if h == 0 else y].astype(f32)
        for k in range(3):
            t += b_got[h, k].astype(f32)
        wc[h, z, y] = t.astype(bf)
        (e0, e1)[h].start()
        (f0, f1)[h][0].start()

    def left_of(h, j):
        block = left[:, ymod(j)] if h == 0 else left[zmod(j)]
        return block.astype(f32).reshape(256, 1024).T.astype(bf)

    def right_of(h, j):
        block = right[0, :, ymod(j)] if h == 0 else right[1, zmod(j)]
        return block.astype(f32).reshape(256, 1024).astype(bf)

    def multiply(h, j):
        acc[h] += scale * jnp.dot(left_of(h, j), right_of(h, j), preferred_element_type=f32)

    def examples_of(ref, c):
        return ref[:, :, c].astype(f32).reshape(128, 1024)

    def spread_of(ref):
        total = jnp.zeros((256, 1024), f32)
        for m in range(0, 8, 2):
            pair = jnp.concatenate([proj[m + n].reshape(256, 128) for n in range(2)], axis=1)
            rows = jnp.concatenate([examples_of(ref, m + n) for n in range(2)], axis=0).astype(bf)
            total += jnp.dot(pair, rows, preferred_element_type=f32)
        return total

    own_right = pltpu.make_async_copy(lg.at[pl.ds(2 * col, 2)], right.at[:, z, y, col], loc_sem.at[0])
    own_right.start()
    own_left = pltpu.make_async_copy(lg.at[row], left.at[z, y, col], loc_sem.at[1])
    own_left.start()
    stage_c, stage_r = [], []
    for k in (2, 6, 1, 7, 3, 5, 4):
        to = lax.rem(col + k, 8)
        stage_c.append(go(remote(lg.at[pl.ds(2 * to, 2)], right.at[:, z, y, col],
                                 c_send.at[k], c_recv.at[k], (row, to))))
    for k in range(1, 16):
        to = lax.rem(row + k, 16)
        stage_r.append(go(remote(lg.at[to], left.at[z, y, col], r_send.at[k], r_recv.at[k], (to, col))))
    reduce_first(0)
    begin(1)
    reduce_first(1)
    own_right.wait()
    own_left.wait()
    for c in stage_c:
        c.wait_recv()
    a0.start(); a1.start()
    b0[0].start(); b1[0].start()
    for c in stage_r:
        c.wait_recv()
    xr.start()
    pp = [to_partner(0)]
    mine_t = examples_of(left, col).T.astype(bf)
    y_mine[...] = (scale * jnp.dot(qt[...], mine_t, preferred_element_type=f32)).astype(bf).reshape(16, 16, 128)
    ysum = [go(remote(y_mine.at[lax.rem(row + k, 16)], y_got.at[k], s_y.at[0, k], r_y.at[0, k],
                      (lax.rem(row + k, 16), col))) for k in range(1, 16)]
    reduce_join(0); reduce_join(1)
    a0.forward(); a1.forward()
    b0[3].start(); b1[3].start()
    xr.forward()
    pp += [to_partner(3), to_partner(1)]
    reduce_second(0); reduce_second(1)
    b0[0].forward(); b1[0].forward()
    b0[1].start(); b1[1].start()
    a0.finish(); a1.finish()
    xr.finish()
    pp += [to_partner(2)]
    t = y_mine[row].astype(f32)
    for k in range(1, 16):
        ysum[k - 1].wait_recv()
        t += y_got[k].astype(f32)
    proj[col, row] = t.astype(bf)
    yall = [go(remote(proj.at[col, row], proj.at[col, row], s_y.at[1, k], r_y.at[1, k],
                      (lax.rem(row + k, 16), col))) for k in range(1, 16)]
    b0[3].forward(); b1[3].forward()
    b0[2].start(); b1[2].start()
    gather_first(0); gather_first(1)
    publish((0, 0))
    for c in pp:
        c.wait_recv()
    b0[0].finish(); b1[0].finish()
    multiply(0, 0)
    for c in yall:
        c.wait_recv()
    ycol = [go(remote(proj.at[col], proj.at[col], s_z.at[k], r_z.at[k], (row, lax.rem(col + k, 8))))
            for k in range(1, 8)]
    b0[1].forward(); b1[1].forward()
    multiply(1, 0)
    e0.forward(); e1.forward()
    for j in (3, 1):
        f0[j].start(); f1[j].start()
    publish((0, 3), (0, 1))
    b0[3].finish(); b1[3].finish()
    multiply(0, 3)
    f0[0].forward(); f1[0].forward()
    e0.finish(); e1.finish()
    f0[2].start(); f1[2].start()
    publish((3, 0), (1, 0), (0, 2))
    b0[2].forward(); b1[2].forward()
    multiply(1, 3)
    f0[3].forward(); f1[3].forward()
    publish((3, 3), (1, 3))
    for c in ycol:
        c.wait_recv()
    w_row[...] = spread_of(left)
    f0[1].forward(); f1[1].forward()
    publish((3, 1), (1, 1))
    b0[1].finish(); b1[1].finish()
    multiply(0, 1)
    f0[2].forward(); f1[2].forward()
    publish((3, 2), (1, 2))
    multiply(1, 1)
    for j in (0, 3, 1, 2):
        f0[j].finish(); f1[j].finish()
        publish((2, j))
    for h in range(2):
        gb[h] = acc[h].astype(bf)
        last[h] = left_of(h, 2)
    b0[2].finish(); b1[2].finish()
    for h in range(2):
        w_col[h] = spread_of(right.at[h]) + wc[h].reshape(256, 1024).astype(f32)

    @pl.when(root)
    def _():
        wr[...] = wc[half]
        for n in range(16):
            for k in (1, 3, 2):
                along(n, k).wait_send()
            across(n, wc.at[half]).wait_send()

    @pl.when(jnp.logical_and(mine, x != z))
    def _():
        for n in range(16):
            along(n, 1).wait_recv()
            across(n, wr).start()
        for n in range(16):
            across(n, wr).wait_send()

    @pl.when(jnp.logical_not(mine))
    def _():
        for n in range(16):
            across(n, wr).wait_recv()

    wsum = wr[...].reshape(256, 1024).astype(f32) + w_row[...]
    wrv = wsum.astype(bf)
    v = jnp.zeros((256, 1024), f32)
    for h in range(2):
        u = (scale * jnp.dot(wrv, last[h], preferred_element_type=f32)).astype(bf)
        v += (jnp.dot(wrv, gb[h], preferred_element_type=f32)
              + jnp.dot(u, right_of(h, 2), preferred_element_type=f32)) * w_col[h]
    curve = jnp.broadcast_to(jnp.sum(v, axis=1, keepdims=True), (256, 128)).T
    w = wsum.T
    qv = q[...]
    once = jnp.where(col == 0, 1.0, 0.0).astype(f32)
    msg[0:1] = jnp.sum(qv * qv, axis=0, keepdims=True) * once
    msg[1:2] = jnp.sum(qv * w, axis=0, keepdims=True) * once
    msg[2:3] = jnp.sum(w * w, axis=0, keepdims=True) * once
    msg[3:4] = curve[3:4]
    cr = [go(remote(msg, got_r.at[k], s_r.at[k], r_r.at[k], (lax.rem(row + k, 16), col))) for k in range(1, 16)]
    for h in range(2):
        acc[h] += scale * jnp.dot(last[h], right_of(h, 2), preferred_element_type=f32)
    t = msg[...]
    for k, c in enumerate(cr):
        c.wait_recv()
        t += got_r[k + 1]
    msg2[...] = t
    cc = [go(remote(msg2, got_c.at[k], s_c.at[k], r_c.at[k], (row, lax.rem(col + k, 8)))) for k in range(1, 8)]
    for k, c in enumerate(cc):
        c.wait_recv()
        t += got_c[k + 1]
    rr, qw, ww, gg = t[0:1], t[1:2], t[2:3], t[3:4]
    s1 = rr / qw
    new = s1 * s1 * ww - rr
    beta = new / rr
    up = 1.0 + beta
    s2 = new / (up * up * qw - 2.0 * up * s1 * ww + s1 * s1 * gg)
    x_out[...] = (s1 + s2 * up) * qv - (s2 * s1) * w
    for c in sends:
        c.wait_send()


def run(*args):
    dma = pltpu.SemaphoreType.DMA
    bf, f32 = jnp.bfloat16, jnp.float32
    vm = pltpu.VMEM
    hbm = pl.BlockSpec(memory_space=pl.ANY)
    return pl.pallas_call(
        kernel,
        out_shape=(vm((2, 1024, 1024), f32), vm((1024, 256), f32)),
        in_specs=[hbm] * 4 + [pl.BlockSpec(memory_space=pltpu.SMEM)] + [hbm] * 2,
        out_specs=(pl.BlockSpec(memory_space=pltpu.VMEM),) * 2,
        scratch_shapes=[vm((256, 4096), bf), vm((256, 4096), bf), vm((4096, 128), bf), vm((4096, 128), bf),
                        vm((1024, 2048), f32), vm((1024, 256), f32), vm((16, 8, 1024), bf),
                        vm((4, 4, 8, 8, 1024), bf), vm((2, 4, 4, 8, 8, 1024), bf), vm((256, 1024), bf),
                        vm((16, 16, 128), bf), vm((16, 16, 128), bf), vm((8, 16, 16, 128), bf), vm((256, 1024), f32),
                        vm((2, 256, 1024), f32), vm((2, 1024, 256), bf),
                        vm((2, 1024, 1024), bf), vm((2, 4, 4, 16, 1024), bf),
                        vm((2, 2, 4, 16, 512), bf), vm((2, 2, 2, 4, 16, 512), bf), vm((2, 2, 4, 16, 512), bf),
                        vm((2, 4, 16, 1024), bf), vm((2, 3, 16, 1024), bf), vm((2, 4, 4, 16, 1024), bf),
                        vm((4, 4, 16, 1024), bf),
                        vm((4, 256), f32), vm((16, 4, 256), f32), vm((4, 256), f32), vm((8, 4, 256), f32),
                        dma((6,)), dma((2,)), dma((8,)), dma((8,)), dma((16,)), dma((16,)),
                        dma((20,)), dma((20,)), dma((20,)), dma((20,)), dma((4,)), dma((4,)), dma((4,)), dma((4,)),
                        dma((2, 16)), dma((2, 16)), dma((8,)), dma((8,)),
                        dma((2, 6)), dma((2, 6)), dma((2, 4)), dma((2, 4)), dma((20,)), dma((20,)), dma((20,)), dma((20,)),
                        dma((16, 4)), dma((16,)), dma((16,)), dma((16,)), dma((16,)), dma((16,)), dma((8,)), dma((8,))],
        compiler_params=pltpu.CompilerParams(collective_id=0, has_side_effects=True, vmem_limit_bytes=44 * 1024 * 1024),
        name="influence",
    )(*args)


def store_kernel(g, x, g_out, x_out, sem):
    copies = [pltpu.make_async_copy(g.at[h, pl.ds(n * 256, 256)], g_out.at[pl.ds(n * 256, 256), pl.ds(h * 1024, 1024)],
                                    sem.at[4 * h + n]) for h in range(2) for n in range(4)]
    copies.append(pltpu.make_async_copy(x, x_out, sem.at[8]))
    for c in copies:
        c.start()
    for c in copies:
        c.wait()


def store(g, x):
    f32 = jnp.float32
    inside, hbm = pl.BlockSpec(memory_space=pltpu.VMEM), pl.BlockSpec(memory_space=pltpu.HBM)
    return pl.pallas_call(
        store_kernel,
        out_shape=(jax.ShapeDtypeStruct((1024, 2048), f32), jax.ShapeDtypeStruct((1024, 256), f32)),
        in_specs=[inside] * 2,
        out_specs=(hbm, hbm),
        scratch_shapes=[pltpu.SemaphoreType.DMA((9,))],
        compiler_params=pltpu.CompilerParams(vmem_limit_bytes=16 * 1024 * 1024),
        name="store",
    )(pltpu.with_memory_space_constraint(g, pltpu.VMEM), pltpu.with_memory_space_constraint(x, pltpu.VMEM))


def whole(*args):
    return store(*run(*args))


def solution(mesh):
    in_specs = (
        P(("row", "col"), None),
        P(("row", "col"), None),
        P(),
        P(),
        P(("row", "col")),
        P("row", "col"),
        P("row", None),
    )
    out_specs = (P("row", "col"), P("row", None))
    return jax.shard_map(whole, mesh=mesh, in_specs=in_specs, out_specs=out_specs, check_vma=False)
```

```python
import functools

import jax
import jax.numpy as jnp
from jax import lax
from jax.experimental import pallas as pl
from jax.experimental.pallas import tpu as pltpu
from jax.sharding import PartitionSpec as P

MESH = pl.DeviceIdType.MESH
SEQ = 32
ITERS = 2
decay_rate = 0.5
damping = 1.0
HBM = pl.ANY


class Ring:
    def __init__(self, go, slot, lo, hi, ss, rs, base, plus, minus):
        self.go, self.slot, self.lo, self.hi = go, slot, lo, hi
        self.ss, self.rs, self.base = ss, rs, base
        self.plus, self.minus = plus, minus

    def copy(self, ref, k, dev):
        return self.go(pltpu.make_async_remote_copy(
            src_ref=ref, dst_ref=ref, send_sem=self.ss.at[self.base + k], recv_sem=self.rs.at[self.base + k],
            device_id=dev, device_id_type=MESH))

    def start(self):
        own = self.slot(0)
        self.f0 = self.copy(own, 0, self.plus)
        self.f1 = self.copy(own, 1, self.minus)

    def forward(self):
        self.f0.wait_recv()
        self.h0 = self.copy(self.lo(self.slot(3)), 2, self.plus)
        self.f1.wait_recv()
        self.h1 = self.copy(self.hi(self.slot(1)), 3, self.minus)

    def finish(self):
        self.h0.wait_recv()
        self.h1.wait_recv()


def greet(row, col):
    barrier = pltpu.get_barrier_semaphore()
    for k in range(1, 8):
        pl.semaphore_signal(barrier, inc=1, device_id=(row, lax.rem(col + k, 8)), device_id_type=MESH)
    for k in range(1, 16):
        pl.semaphore_signal(barrier, inc=1, device_id=(lax.rem(row + k, 16), col), device_id_type=MESH)
    return barrier


def kernel(act, og, p_in, p_out, lens, old_hbm, q_hbm, acc, x_out,
           act_v, og_v, pin_v, pout_v, old, q, lg, left, right, qt, y_mine, y_got, proj, w_row, w_col, last, gb, part,
           a_far, a_got, a_sum, b_sum, b_got, wc, wr, msg, got_r, msg2, got_c,
           in_sem, loc_sem, c_send, c_recv, r_send, r_recv, ya_send, ya_recv, za_send, za_recv,
           x_send, x_recv, p_send, p_recv,
           s_y, r_y, s_z, r_z, s_a, r_a, s_b, r_b, ys, yr, zs, zr, xs, xrecv, ps, pr, s_r, r_r, s_c, r_c):
    f32, bf = jnp.float32, jnp.bfloat16
    row = lax.axis_index("row")
    col = lax.axis_index("col")
    z, y = row // 4, row % 4
    x, core = col // 2, col % 2
    barrier = greet(row, col)
    loads = [pltpu.make_async_copy(a, b, in_sem.at[n]) for n, (a, b) in enumerate(
        ((p_out, pout_v), (og, og_v), (p_in, pin_v), (act, act_v), (q_hbm, q), (old_hbm, old)))]
    for c in loads[:4]:
        c.start()
    sends = []

    def go(copy):
        copy.start()
        sends.append(copy)
        return copy

    def remote(src, dst, ssem, rsem, dev):
        return pltpu.make_async_remote_copy(src_ref=src, dst_ref=dst, send_sem=ssem, recv_sem=rsem,
                                            device_id=dev, device_id_type=MESH)

    def ymod(k):
        return lax.rem(y + k, 4)

    def zmod(k):
        return lax.rem(z + k, 4)

    def at_y(k):
        return (z * 4 + ymod(k), col)

    def at_z(k):
        return (zmod(k) * 4 + y, col)

    loads[0].wait()
    loads[1].wait()
    loads[4].start()
    loads[5].start()
    low_out = jnp.dot(og_v[...], pout_v[...], preferred_element_type=f32).astype(bf).astype(f32).T
    ex = lax.broadcasted_iota(jnp.int32, (8, 256), 0)
    slot = lax.broadcasted_iota(jnp.int32, (8, 256), 1) - SEQ * ex
    count = jnp.zeros((8, 256), jnp.int32)
    for e in range(8):
        count = jnp.where(ex == e, lens[e], count)
    valid = jnp.logical_and(slot >= 0, slot < jnp.minimum(count, SEQ))
    spread = jnp.where(valid[None], low_out[:, None, :], 0.0).reshape(1024, 256).astype(bf)
    loads[2].wait()
    loads[3].wait()
    low_in = jnp.dot(act_v[...], pin_v[...], preferred_element_type=f32).astype(bf)
    grads = jnp.dot(spread, low_in, preferred_element_type=f32).reshape(16, 8, 8, 128)
    for j in range(8):
        lg[:, :, pl.ds(j * 128, 128)] = grads[:, j].astype(bf)
    loads[4].wait()
    q16 = q[...].T.astype(bf)
    qt[...] = q16
    scale = (1.0 - decay_rate) / 1024

    def begin(h):
        ri = lax.broadcasted_iota(jnp.int32, (1024, 1024), 0) + row * 1024
        ci = lax.broadcasted_iota(jnp.int32, (1024, 1024), 1) + (col * 2048 + h * 1024)
        g = decay_rate * old[:, pl.ds(h * 1024, 1024)] + jnp.where(ri == ci, damping, 0.0).astype(f32)
        acc[h] = g
        pt = jnp.dot(qt[...], g.astype(bf), preferred_element_type=f32)
        part[h] = pt.astype(bf).reshape(4, 4, 16, 1024)

    loads[5].wait()
    begin(0)
    pl.semaphore_wait(barrier, 22)

    yp, ym, zp, zm = at_y(1), at_y(3), at_z(1), at_z(3)
    xp = (row, lax.rem(x + 1, 4) * 2 + core)
    xm = (row, lax.rem(x + 3, 4) * 2 + core)
    partner = (row, x * 2 + 1 - core)
    lo5, hi5 = (lambda r: r.at[pl.ds(0, 4)]), (lambda r: r.at[pl.ds(4, 4)])
    a0 = Ring(go, lambda k: right.at[0, z, ymod(k)], lo5, hi5, ya_send, ya_recv, 0, yp, ym)
    a1 = Ring(go, lambda k: right.at[1, zmod(k), y], lo5, hi5, za_send, za_recv, 0, zp, zm)
    b0 = [Ring(go, lambda k, j=j: right.at[0, zmod(k), ymod(j)], lo5, hi5, za_send, za_recv, 4 + 4 * j, zp, zm)
          for j in range(4)]
    b1 = [Ring(go, lambda k, j=j: right.at[1, zmod(j), ymod(k)], lo5, hi5, ya_send, ya_recv, 4 + 4 * j, yp, ym)
          for j in range(4)]
    xr = Ring(go, lambda k: left.at[:, :, lax.rem(x + k, 4) * 2 + core], lambda r: r.at[pl.ds(0, 2)],
              lambda r: r.at[pl.ds(2, 2)], x_send, x_recv, 0, xp, xm)

    def to_partner(k):
        c = left.at[:, :, lax.rem(x + k, 4) * 2 + core]
        return go(remote(c, c, p_send.at[k], p_recv.at[k], partner))

    lo, hi = pl.ds(0, 512), pl.ds(512, 512)

    def chunk(h, k):
        return part.at[0, :, ymod(k)] if h == 0 else part.at[1, zmod(k)]

    near = ((yp, ym), (zp, zm))
    far, plain, joined, second = [], [], [], []

    def reduce_first(h):
        plus, minus = near[h]
        far.append((go(remote(chunk(h, 2).at[:, :, lo], a_far.at[h, 0], s_a.at[h, 0], r_a.at[h, 0], plus)),
                    go(remote(chunk(h, 2).at[:, :, hi], a_far.at[h, 1], s_a.at[h, 1], r_a.at[h, 1], minus))))
        plain.append((go(remote(chunk(h, 1).at[:, :, hi], a_got.at[h, 0, 1], s_a.at[h, 2], r_a.at[h, 2], plus)),
                      go(remote(chunk(h, 3).at[:, :, lo], a_got.at[h, 1, 0], s_a.at[h, 3], r_a.at[h, 3], minus))))

    def reduce_join(h):
        plus, minus = near[h]
        far[h][0].wait_recv()
        a_sum[h, 0] = (chunk(h, 1)[:, :, lo].astype(f32) + a_far[h, 0].astype(f32)).astype(bf)
        up = go(remote(a_sum.at[h, 0], a_got.at[h, 0, 0], s_a.at[h, 4], r_a.at[h, 4], plus))
        far[h][1].wait_recv()
        a_sum[h, 1] = (chunk(h, 3)[:, :, hi].astype(f32) + a_far[h, 1].astype(f32)).astype(bf)
        joined.append((up, go(remote(a_sum.at[h, 1], a_got.at[h, 1, 1], s_a.at[h, 5], r_a.at[h, 5], minus))))

    def reduce_second(h):
        for c in plain[h] + joined[h]:
            c.wait_recv()
        for n, lanes in enumerate((lo, hi)):
            t = chunk(h, 0)[:, :, lanes].astype(f32) + a_got[h, 0, n].astype(f32) + a_got[h, 1, n].astype(f32)
            b_sum[h, :, :, lanes] = t.astype(bf)
        second.append([])
        for k in (1, 3, 2):
            to, dev = (zmod(k), at_z(k)) if h == 0 else (ymod(k), at_y(k))
            second[h].append(go(remote(b_sum.at[h, to], b_got.at[h, k - 1], s_b.at[h, k], r_b.at[h, k], dev)))

    lol, hil = (lambda r: r.at[:, lo]), (lambda r: r.at[:, hi])
    e0 = Ring(go, lambda k: wc.at[0, z, ymod(k)], lol, hil, ys, yr, 0, yp, ym)
    e1 = Ring(go, lambda k: wc.at[1, zmod(k), y], lol, hil, zs, zr, 0, zp, zm)
    f0 = [Ring(go, lambda k, j=j: wc.at[0, zmod(k), ymod(j)], lol, hil, zs, zr, 4 + 4 * j, zp, zm) for j in range(4)]
    f1 = [Ring(go, lambda k, j=j: wc.at[1, zmod(j), ymod(k)], lol, hil, ys, yr, 4 + 4 * j, yp, ym) for j in range(4)]
    half = y % 2
    mine = core == y // 2
    away = lax.rem(x - z + 4, 4)
    root = jnp.logical_and(mine, away == 0)
    pieces = []

    def group(late, early):
        dz = jnp.where(half == 0, late, early)
        dy = jnp.where(half == 0, early, late)
        return zmod(dz), ymod(dy)

    def along(n, k):
        gz, gy = pieces[n]
        return remote(wc.at[half, gz, gy], wr.at[gz, gy], xs.at[n, k], xrecv.at[n], (row, lax.rem(x + k, 4) * 2 + core))

    def across(n, src):
        gz, gy = pieces[n]
        return remote(src.at[gz, gy], wr.at[gz, gy], ps.at[n], pr.at[n], partner)

    def relay(n, k):
        gz, gy = pieces[n]
        return remote(wr.at[gz, gy], wr.at[gz, gy], xs.at[n, k], xrecv.at[n], (row, lax.rem(x + k, 4) * 2 + core))

    def pass_on(first, stop):
        for place, k in ((1, 1), (3, 3)):
            @pl.when(jnp.logical_and(mine, away == place))
            def _(place=place, k=k):
                for n in range(first, stop):
                    if n % 2 == place // 2:
                        relay(n, k).wait_recv()
                        relay(n, k).start()

    done = [0]

    def publish(*which):
        first = len(pieces)
        pieces.extend(group(*w) for w in which)

        @pl.when(root)
        def _():
            for n in range(first, len(pieces)):
                for k in (1, 3):
                    along(n, k).start()
                across(n, wc.at[half]).start()
        pass_on(done[0], first)
        done[0] = first

    def gather_first(h):
        for c in second[h]:
            c.wait_recv()
        t = b_sum[h, z if h == 0 else y].astype(f32)
        for k in range(3):
            t += b_got[h, k].astype(f32)
        wc[h, z, y] = t.astype(bf)
        (e0, e1)[h].start()
        (f0, f1)[h][0].start()

    def left_of(h, j):
        block = left[:, ymod(j)] if h == 0 else left[zmod(j)]
        return block.astype(f32).reshape(256, 1024).T.astype(bf)

    def right_of(h, j):
        block = right[0, :, ymod(j)] if h == 0 else right[1, zmod(j)]
        return block.astype(f32).reshape(256, 1024).astype(bf)

    def multiply(h, j):
        acc[h] += scale * jnp.dot(left_of(h, j), right_of(h, j), preferred_element_type=f32)

    def examples_of(ref, c):
        return ref[:, :, c].astype(f32).reshape(128, 1024)

    def spread_of(ref):
        total = jnp.zeros((256, 1024), f32)
        for m in range(0, 8, 2):
            pair = jnp.concatenate([proj[m + n].reshape(256, 128) for n in range(2)], axis=1)
            rows = jnp.concatenate([examples_of(ref, m + n) for n in range(2)], axis=0).astype(bf)
            total += jnp.dot(pair, rows, preferred_element_type=f32)
        return total

    own_right = pltpu.make_async_copy(lg.at[pl.ds(2 * col, 2)], right.at[:, z, y, col], loc_sem.at[0])
    own_right.start()
    own_left = pltpu.make_async_copy(lg.at[row], left.at[z, y, col], loc_sem.at[1])
    own_left.start()
    stage_c, stage_r = [], []
    for k in (2, 6, 1, 7, 3, 5, 4):
        to = lax.rem(col + k, 8)
        stage_c.append(go(remote(lg.at[pl.ds(2 * to, 2)], right.at[:, z, y, col],
                                 c_send.at[k], c_recv.at[k], (row, to))))
    for k in range(1, 16):
        to = lax.rem(row + k, 16)
        stage_r.append(go(remote(lg.at[to], left.at[z, y, col], r_send.at[k], r_recv.at[k], (to, col))))
    reduce_first(0)
    begin(1)
    reduce_first(1)
    own_right.wait()
    own_left.wait()
    for c in stage_c:
        c.wait_recv()
    a0.start(); a1.start()
    b0[0].start(); b1[0].start()
    for c in stage_r:
        c.wait_recv()
    xr.start()
    pp = [to_partner(0)]
    mine_t = examples_of(left, col).T.astype(bf)
    y_mine[...] = (scale * jnp.dot(qt[...], mine_t, preferred_element_type=f32)).astype(bf).reshape(16, 16, 128)
    ysum = [go(remote(y_mine.at[lax.rem(row + k, 16)], y_got.at[k], s_y.at[0, k], r_y.at[0, k],
                      (lax.rem(row + k, 16), col))) for k in range(1, 16)]
    yr_ = Ring(go, lambda k: proj.at[lax.rem(x + k, 4) * 2 + core], lambda r: r.at[pl.ds(0, 8)],
               lambda r: r.at[pl.ds(8, 8)], s_z, r_z, 0, xp, xm)

    def y_partner(k):
        c = proj.at[lax.rem(x + k, 4) * 2 + core]
        return go(remote(c, c, s_z.at[4 + k], r_z.at[4 + k], partner))

    reduce_join(0); reduce_join(1)
    a0.forward(); a1.forward()
    b0[3].start(); b1[3].start()
    xr.forward()
    pp += [to_partner(3), to_partner(1)]
    reduce_second(0); reduce_second(1)
    b0[0].forward(); b1[0].forward()
    b0[1].start(); b1[1].start()
    a0.finish(); a1.finish()
    xr.finish()
    pp += [to_partner(2)]
    t = y_mine[row].astype(f32)
    for k in range(1, 16):
        ysum[k - 1].wait_recv()
        t += y_got[k].astype(f32)
    proj[col, row] = t.astype(bf)
    yall = [go(remote(proj.at[col, row], proj.at[col, row], s_y.at[1, k], r_y.at[1, k],
                      (lax.rem(row + k, 16), col))) for k in range(1, 16)]
    b0[3].forward(); b1[3].forward()
    b0[2].start(); b1[2].start()
    gather_first(0); gather_first(1)
    publish((0, 0))
    for c in pp:
        c.wait_recv()
    b0[0].finish(); b1[0].finish()
    multiply(0, 0)
    for c in yall:
        c.wait_recv()
    yr_.start()
    ycol = [y_partner(0)]
    b0[1].forward(); b1[1].forward()
    multiply(1, 0)
    e0.forward(); e1.forward()
    for j in (3, 1):
        f0[j].start(); f1[j].start()
    publish((0, 3), (0, 1))
    b0[3].finish(); b1[3].finish()
    multiply(0, 3)
    f0[0].forward(); f1[0].forward()
    e0.finish(); e1.finish()
    f0[2].start(); f1[2].start()
    publish((3, 0), (1, 0), (0, 2))
    b0[2].forward(); b1[2].forward()
    yr_.forward()
    ycol += [y_partner(3), y_partner(1)]
    multiply(1, 3)
    f0[3].forward(); f1[3].forward()
    publish((3, 3), (1, 3))
    yr_.finish()
    ycol += [y_partner(2)]
    for c in ycol:
        c.wait_recv()
    w_row[...] = spread_of(left)
    f0[1].forward(); f1[1].forward()
    publish((3, 1), (1, 1))
    b0[1].finish(); b1[1].finish()
    multiply(0, 1)
    f0[2].forward(); f1[2].forward()
    publish((3, 2), (1, 2))
    multiply(1, 1)
    for j in (0, 3, 1, 2):
        f0[j].finish(); f1[j].finish()
        publish((2, j))
    for h in range(2):
        gb[h] = acc[h].astype(bf)
        last[h] = left_of(h, 2)
    b0[2].finish(); b1[2].finish()
    for h in range(2):
        w_col[h] = spread_of(right.at[h]) + wc[h].reshape(256, 1024).astype(f32)

    @pl.when(root)
    def _():
        wr[...] = wc[half]
        for n in range(16):
            for k in (1, 3):
                along(n, k).wait_send()
            across(n, wc.at[half]).wait_send()

    pass_on(done[0], 16)
    for place in (1, 2, 3):
        @pl.when(jnp.logical_and(mine, away == place))
        def _(place=place):
            for n in range(16):
                if place == 2 or n % 2 != place // 2:
                    along(n, 1).wait_recv()
                across(n, wr).start()
            for n in range(16):
                if place != 2 and n % 2 == place // 2:
                    relay(n, place).wait_send()
                across(n, wr).wait_send()

    @pl.when(jnp.logical_not(mine))
    def _():
        for n in range(16):
            across(n, wr).wait_recv()

    wsum = wr[...].reshape(256, 1024).astype(f32) + w_row[...]
    wrv = wsum.astype(bf)
    v = jnp.zeros((256, 1024), f32)
    for h in range(2):
        u = (scale * jnp.dot(wrv, last[h], preferred_element_type=f32)).astype(bf)
        v += (jnp.dot(wrv, gb[h], preferred_element_type=f32)
              + jnp.dot(u, right_of(h, 2), preferred_element_type=f32)) * w_col[h]
    curve = jnp.broadcast_to(jnp.sum(v, axis=1, keepdims=True), (256, 128)).T
    w = wsum.T
    qv = q[...]
    once = jnp.where(col == 0, 1.0, 0.0).astype(f32)
    msg[0:1] = jnp.sum(qv * qv, axis=0, keepdims=True) * once
    msg[1:2] = jnp.sum(qv * w, axis=0, keepdims=True) * once
    msg[2:3] = jnp.sum(w * w, axis=0, keepdims=True) * once
    msg[3:4] = curve[3:4]
    cr = [go(remote(msg, got_r.at[k], s_r.at[k], r_r.at[k], (lax.rem(row + k, 16), col))) for k in range(1, 16)]
    for h in range(2):
        acc[h] += scale * jnp.dot(last[h], right_of(h, 2), preferred_element_type=f32)
    t = msg[...]
    for k, c in enumerate(cr):
        c.wait_recv()
        t += got_r[k + 1]
    msg2[...] = t
    cc = [go(remote(msg2, got_c.at[k], s_c.at[k], r_c.at[k], (row, lax.rem(col + k, 8)))) for k in range(1, 8)]
    for k, c in enumerate(cc):
        c.wait_recv()
        t += got_c[k + 1]
    rr, qw, ww, gg = t[0:1], t[1:2], t[2:3], t[3:4]
    s1 = rr / qw
    new = s1 * s1 * ww - rr
    beta = new / rr
    up = 1.0 + beta
    s2 = new / (up * up * qw - 2.0 * up * s1 * ww + s1 * s1 * gg)
    x_out[...] = (s1 + s2 * up) * qv - (s2 * s1) * w
    for c in sends:
        c.wait_send()


def run(*args):
    dma = pltpu.SemaphoreType.DMA
    bf, f32 = jnp.bfloat16, jnp.float32
    vm = pltpu.VMEM
    hbm = pl.BlockSpec(memory_space=pl.ANY)
    return pl.pallas_call(
        kernel,
        out_shape=(vm((2, 1024, 1024), f32), vm((1024, 256), f32)),
        in_specs=[hbm] * 4 + [pl.BlockSpec(memory_space=pltpu.SMEM)] + [hbm] * 2,
        out_specs=(pl.BlockSpec(memory_space=pltpu.VMEM),) * 2,
        scratch_shapes=[vm((256, 4096), bf), vm((256, 4096), bf), vm((4096, 128), bf), vm((4096, 128), bf),
                        vm((1024, 2048), f32), vm((1024, 256), f32), vm((16, 8, 1024), bf),
                        vm((4, 4, 8, 8, 1024), bf), vm((2, 4, 4, 8, 8, 1024), bf), vm((256, 1024), bf),
                        vm((16, 16, 128), bf), vm((16, 16, 128), bf), vm((8, 16, 16, 128), bf), vm((256, 1024), f32),
                        vm((2, 256, 1024), f32), vm((2, 1024, 256), bf),
                        vm((2, 1024, 1024), bf), vm((2, 4, 4, 16, 1024), bf),
                        vm((2, 2, 4, 16, 512), bf), vm((2, 2, 2, 4, 16, 512), bf), vm((2, 2, 4, 16, 512), bf),
                        vm((2, 4, 16, 1024), bf), vm((2, 3, 16, 1024), bf), vm((2, 4, 4, 16, 1024), bf),
                        vm((4, 4, 16, 1024), bf),
                        vm((4, 256), f32), vm((16, 4, 256), f32), vm((4, 256), f32), vm((8, 4, 256), f32),
                        dma((6,)), dma((2,)), dma((8,)), dma((8,)), dma((16,)), dma((16,)),
                        dma((20,)), dma((20,)), dma((20,)), dma((20,)), dma((4,)), dma((4,)), dma((4,)), dma((4,)),
                        dma((2, 16)), dma((2, 16)), dma((8,)), dma((8,)),
                        dma((2, 6)), dma((2, 6)), dma((2, 4)), dma((2, 4)), dma((20,)), dma((20,)), dma((20,)), dma((20,)),
                        dma((16, 4)), dma((16,)), dma((16,)), dma((16,)), dma((16,)), dma((16,)), dma((8,)), dma((8,))],
        compiler_params=pltpu.CompilerParams(collective_id=0, has_side_effects=True, vmem_limit_bytes=44 * 1024 * 1024),
        name="influence",
    )(*args)


def store_kernel(g, x, g_out, x_out, sem):
    copies = [pltpu.make_async_copy(g.at[h, pl.ds(n * 256, 256)], g_out.at[pl.ds(n * 256, 256), pl.ds(h * 1024, 1024)],
                                    sem.at[4 * h + n]) for h in range(2) for n in range(4)]
    copies.append(pltpu.make_async_copy(x, x_out, sem.at[8]))
    for c in copies:
        c.start()
    for c in copies:
        c.wait()


def store(g, x):
    f32 = jnp.float32
    inside, hbm = pl.BlockSpec(memory_space=pltpu.VMEM), pl.BlockSpec(memory_space=pltpu.HBM)
    return pl.pallas_call(
        store_kernel,
        out_shape=(jax.ShapeDtypeStruct((1024, 2048), f32), jax.ShapeDtypeStruct((1024, 256), f32)),
        in_specs=[inside] * 2,
        out_specs=(hbm, hbm),
        scratch_shapes=[pltpu.SemaphoreType.DMA((9,))],
        compiler_params=pltpu.CompilerParams(vmem_limit_bytes=16 * 1024 * 1024),
        name="store",
    )(pltpu.with_memory_space_constraint(g, pltpu.VMEM), pltpu.with_memory_space_constraint(x, pltpu.VMEM))


def whole(*args):
    return store(*run(*args))


def solution(mesh):
    in_specs = (
        P(("row", "col"), None),
        P(("row", "col"), None),
        P(),
        P(),
        P(("row", "col")),
        P("row", "col"),
        P("row", None),
    )
    out_specs = (P("row", "col"), P("row", None))
    return jax.shard_map(whole, mesh=mesh, in_specs=in_specs, out_specs=out_specs, check_vma=False)
```

```python
import functools

import jax
import jax.numpy as jnp
from jax import lax
from jax.experimental import pallas as pl
from jax.experimental.pallas import tpu as pltpu
from jax.sharding import PartitionSpec as P

MESH = pl.DeviceIdType.MESH
SEQ = 32
ITERS = 2
decay_rate = 0.5
damping = 1.0
HBM = pl.ANY


class Ring:
    def __init__(self, go, slot, lo, hi, ss, rs, base, plus, minus):
        self.go, self.slot, self.lo, self.hi = go, slot, lo, hi
        self.ss, self.rs, self.base = ss, rs, base
        self.plus, self.minus = plus, minus

    def copy(self, ref, k, dev):
        return self.go(pltpu.make_async_remote_copy(
            src_ref=ref, dst_ref=ref, send_sem=self.ss.at[self.base + k], recv_sem=self.rs.at[self.base + k],
            device_id=dev, device_id_type=MESH))

    def start(self):
        own = self.slot(0)
        self.f0 = self.copy(own, 0, self.plus)
        self.f1 = self.copy(own, 1, self.minus)

    def forward(self):
        self.f0.wait_recv()
        self.h0 = self.copy(self.lo(self.slot(3)), 2, self.plus)
        self.f1.wait_recv()
        self.h1 = self.copy(self.hi(self.slot(1)), 3, self.minus)

    def finish(self):
        self.h0.wait_recv()
        self.h1.wait_recv()


def greet(row, col):
    barrier = pltpu.get_barrier_semaphore()
    for k in range(1, 8):
        pl.semaphore_signal(barrier, inc=1, device_id=(row, lax.rem(col + k, 8)), device_id_type=MESH)
    for k in range(1, 16):
        pl.semaphore_signal(barrier, inc=1, device_id=(lax.rem(row + k, 16), col), device_id_type=MESH)
    return barrier


def kernel(act, og, p_in, p_out, lens, old_hbm, q_hbm, acc, x_out,
           act_v, og_v, pin_v, pout_v, old, q, lg, left, right, qt, y_mine, y_got, proj, w_row, w_col, last, gb, part,
           a_far, a_got, a_sum, b_sum, b_got, wc, wr, msg, got_r, msg2, got_c,
           in_sem, loc_sem, c_send, c_recv, r_send, r_recv, ya_send, ya_recv, za_send, za_recv,
           x_send, x_recv, p_send, p_recv,
           s_y, r_y, s_z, r_z, s_a, r_a, s_b, r_b, ys, yr, zs, zr, xs, xrecv, ps, pr, s_r, r_r, s_c, r_c):
    f32, bf = jnp.float32, jnp.bfloat16
    row = lax.axis_index("row")
    col = lax.axis_index("col")
    z, y = row // 4, row % 4
    x, core = col // 2, col % 2
    barrier = greet(row, col)
    loads = [pltpu.make_async_copy(a, b, in_sem.at[n]) for n, (a, b) in enumerate(
        ((p_out, pout_v), (og, og_v), (p_in, pin_v), (act, act_v), (q_hbm, q), (old_hbm, old)))]
    for c in loads[:4]:
        c.start()
    sends = []

    def go(copy):
        copy.start()
        sends.append(copy)
        return copy

    def remote(src, dst, ssem, rsem, dev):
        return pltpu.make_async_remote_copy(src_ref=src, dst_ref=dst, send_sem=ssem, recv_sem=rsem,
                                            device_id=dev, device_id_type=MESH)

    def ymod(k):
        return lax.rem(y + k, 4)

    def zmod(k):
        return lax.rem(z + k, 4)

    def at_y(k):
        return (z * 4 + ymod(k), col)

    def at_z(k):
        return (zmod(k) * 4 + y, col)

    loads[0].wait()
    loads[1].wait()
    loads[4].start()
    loads[5].start()
    low_out = jnp.dot(og_v[...], pout_v[...], preferred_element_type=f32).astype(bf).astype(f32).T
    ex = lax.broadcasted_iota(jnp.int32, (8, 256), 0)
    slot = lax.broadcasted_iota(jnp.int32, (8, 256), 1) - SEQ * ex
    count = jnp.zeros((8, 256), jnp.int32)
    for e in range(8):
        count = jnp.where(ex == e, lens[e], count)
    valid = jnp.logical_and(slot >= 0, slot < jnp.minimum(count, SEQ))
    spread = jnp.where(valid[None], low_out[:, None, :], 0.0).reshape(1024, 256).astype(bf)
    loads[2].wait()
    loads[3].wait()
    low_in = jnp.dot(act_v[...], pin_v[...], preferred_element_type=f32).astype(bf)
    grads = jnp.dot(spread, low_in, preferred_element_type=f32).reshape(16, 8, 8, 128)
    for j in range(8):
        lg[:, :, pl.ds(j * 128, 128)] = grads[:, j].astype(bf)
    loads[4].wait()
    q16 = q[...].T.astype(bf)
    qt[...] = q16
    scale = (1.0 - decay_rate) / 1024

    def begin(h):
        ri = lax.broadcasted_iota(jnp.int32, (1024, 1024), 0) + row * 1024
        ci = lax.broadcasted_iota(jnp.int32, (1024, 1024), 1) + (col * 2048 + h * 1024)
        g = decay_rate * old[:, pl.ds(h * 1024, 1024)] + jnp.where(ri == ci, damping, 0.0).astype(f32)
        acc[h] = g
        pt = jnp.dot(qt[...], g.astype(bf), preferred_element_type=f32)
        part[h] = pt.astype(bf).reshape(4, 4, 16, 1024)

    loads[5].wait()
    begin(0)
    pl.semaphore_wait(barrier, 22)

    yp, ym, zp, zm = at_y(1), at_y(3), at_z(1), at_z(3)
    xp = (row, lax.rem(x + 1, 4) * 2 + core)
    xm = (row, lax.rem(x + 3, 4) * 2 + core)
    partner = (row, x * 2 + 1 - core)
    lo5, hi5 = (lambda r: r.at[pl.ds(0, 4)]), (lambda r: r.at[pl.ds(4, 4)])
    a0 = Ring(go, lambda k: right.at[0, z, ymod(k)], lo5, hi5, ya_send, ya_recv, 0, yp, ym)
    a1 = Ring(go, lambda k: right.at[1, zmod(k), y], lo5, hi5, za_send, za_recv, 0, zp, zm)
    b0 = [Ring(go, lambda k, j=j: right.at[0, zmod(k), ymod(j)], lo5, hi5, za_send, za_recv, 4 + 4 * j, zp, zm)
          for j in range(4)]
    b1 = [Ring(go, lambda k, j=j: right.at[1, zmod(j), ymod(k)], lo5, hi5, ya_send, ya_recv, 4 + 4 * j, yp, ym)
          for j in range(4)]
    xr = Ring(go, lambda k: left.at[:, :, lax.rem(x + k, 4) * 2 + core], lambda r: r.at[pl.ds(0, 2)],
              lambda r: r.at[pl.ds(2, 2)], x_send, x_recv, 0, xp, xm)

    def to_partner(k):
        c = left.at[:, :, lax.rem(x + k, 4) * 2 + core]
        return go(remote(c, c, p_send.at[k], p_recv.at[k], partner))

    lo, hi = pl.ds(0, 512), pl.ds(512, 512)

    def chunk(h, k):
        return part.at[0, :, ymod(k)] if h == 0 else part.at[1, zmod(k)]

    near = ((yp, ym), (zp, zm))
    far, plain, joined, second = [], [], [], []

    def reduce_first(h):
        plus, minus = near[h]
        far.append((go(remote(chunk(h, 2).at[:, :, lo], a_far.at[h, 0], s_a.at[h, 0], r_a.at[h, 0], plus)),
                    go(remote(chunk(h, 2).at[:, :, hi], a_far.at[h, 1], s_a.at[h, 1], r_a.at[h, 1], minus))))
        plain.append((go(remote(chunk(h, 1).at[:, :, hi], a_got.at[h, 0, 1], s_a.at[h, 2], r_a.at[h, 2], plus)),
                      go(remote(chunk(h, 3).at[:, :, lo], a_got.at[h, 1, 0], s_a.at[h, 3], r_a.at[h, 3], minus))))

    def reduce_join(h):
        plus, minus = near[h]
        far[h][0].wait_recv()
        a_sum[h, 0] = (chunk(h, 1)[:, :, lo].astype(f32) + a_far[h, 0].astype(f32)).astype(bf)
        up = go(remote(a_sum.at[h, 0], a_got.at[h, 0, 0], s_a.at[h, 4], r_a.at[h, 4], plus))
        far[h][1].wait_recv()
        a_sum[h, 1] = (chunk(h, 3)[:, :, hi].astype(f32) + a_far[h, 1].astype(f32)).astype(bf)
        joined.append((up, go(remote(a_sum.at[h, 1], a_got.at[h, 1, 1], s_a.at[h, 5], r_a.at[h, 5], minus))))

    def reduce_second(h):
        for c in plain[h] + joined[h]:
            c.wait_recv()
        for n, lanes in enumerate((lo, hi)):
            t = chunk(h, 0)[:, :, lanes].astype(f32) + a_got[h, 0, n].astype(f32) + a_got[h, 1, n].astype(f32)
            b_sum[h, :, :, lanes] = t.astype(bf)
        second.append([])
        for k in (1, 3, 2):
            to, dev = (zmod(k), at_z(k)) if h == 0 else (ymod(k), at_y(k))
            second[h].append(go(remote(b_sum.at[h, to], b_got.at[h, k - 1], s_b.at[h, k], r_b.at[h, k], dev)))

    lol, hil = (lambda r: r.at[:, lo]), (lambda r: r.at[:, hi])
    e0 = Ring(go, lambda k: wc.at[0, z, ymod(k)], lol, hil, ys, yr, 0, yp, ym)
    e1 = Ring(go, lambda k: wc.at[1, zmod(k), y], lol, hil, zs, zr, 0, zp, zm)
    f0 = [Ring(go, lambda k, j=j: wc.at[0, zmod(k), ymod(j)], lol, hil, zs, zr, 4 + 4 * j, zp, zm) for j in range(4)]
    f1 = [Ring(go, lambda k, j=j: wc.at[1, zmod(j), ymod(k)], lol, hil, ys, yr, 4 + 4 * j, yp, ym) for j in range(4)]
    half = y % 2
    mine = core == y // 2
    root = jnp.logical_and(mine, x == z)
    pieces = []

    def group(late, early):
        dz = jnp.where(half == 0, late, early)
        dy = jnp.where(half == 0, early, late)
        return zmod(dz), ymod(dy)

    def along(n, k):
        gz, gy = pieces[n]
        return remote(wc.at[half, gz, gy], wr.at[gz, gy], xs.at[n, k], xrecv.at[n], (row, lax.rem(x + k, 4) * 2 + core))

    def across(n, src):
        gz, gy = pieces[n]
        return remote(src.at[gz, gy], wr.at[gz, gy], ps.at[n], pr.at[n], partner)

    def publish(*which):
        first = len(pieces)
        pieces.extend(group(*w) for w in which)

        @pl.when(root)
        def _():
            for n in range(first, len(pieces)):
                for k in (1, 3, 2):
                    along(n, k).start()
                across(n, wc.at[half]).start()

    def gather_first(h):
        for c in second[h]:
            c.wait_recv()
        t = b_sum[h, z if h == 0 else y].astype(f32)
        for k in range(3):
            t += b_got[h, k].astype(f32)
        wc[h, z, y] = t.astype(bf)
        (e0, e1)[h].start()
        (f0, f1)[h][0].start()

    def left_of(h, j):
        block = left[:, ymod(j)] if h == 0 else left[zmod(j)]
        return block.astype(f32).reshape(256, 1024).T.astype(bf)

    def right_of(h, j):
        block = right[0, :, ymod(j)] if h == 0 else right[1, zmod(j)]
        return block.astype(f32).reshape(256, 1024).astype(bf)

    def multiply(h, j):
        acc[h] += scale * jnp.dot(left_of(h, j), right_of(h, j), preferred_element_type=f32)

    def examples_of(ref, c):
        return ref[:, :, c].astype(f32).reshape(128, 1024)

    def spread_of(ref):
        total = jnp.zeros((256, 1024), f32)
        for m in range(0, 8, 2):
            pair = jnp.concatenate([proj[m + n].reshape(256, 128) for n in range(2)], axis=1)
            rows = jnp.concatenate([examples_of(ref, m + n) for n in range(2)], axis=0).astype(bf)
            total += jnp.dot(pair, rows, preferred_element_type=f32)
        return total

    own_right = pltpu.make_async_copy(lg.at[pl.ds(2 * col, 2)], right.at[:, z, y, col], loc_sem.at[0])
    own_right.start()
    own_left = pltpu.make_async_copy(lg.at[row], left.at[z, y, col], loc_sem.at[1])
    own_left.start()
    stage_c, stage_r = [], []
    for k in (2, 6, 1, 7, 3, 5, 4):
        to = lax.rem(col + k, 8)
        stage_c.append(go(remote(lg.at[pl.ds(2 * to, 2)], right.at[:, z, y, col],
                                 c_send.at[k], c_recv.at[k], (row, to))))
    for k in range(1, 16):
        to = lax.rem(row + k, 16)
        stage_r.append(go(remote(lg.at[to], left.at[z, y, col], r_send.at[k], r_recv.at[k], (to, col))))
    reduce_first(0)
    begin(1)
    reduce_first(1)
    own_right.wait()
    own_left.wait()
    for c in stage_c:
        c.wait_recv()
    a0.start(); a1.start()
    b0[0].start(); b1[0].start()
    for c in stage_r:
        c.wait_recv()
    xr.start()
    pp = [to_partner(0)]
    mine_t = examples_of(left, col).T.astype(bf)
    y_mine[...] = (scale * jnp.dot(qt[...], mine_t, preferred_element_type=f32)).astype(bf).reshape(16, 16, 128)
    ysum = [go(remote(y_mine.at[lax.rem(row + k, 16)], y_got.at[k], s_y.at[0, k], r_y.at[0, k],
                      (lax.rem(row + k, 16), col))) for k in range(1, 16)]
    def y_partner(k):
        c = proj.at[lax.rem(x + k, 4) * 2 + core]
        return go(remote(c, c, s_z.at[4 + k], r_z.at[4 + k], partner))

    reduce_join(0); reduce_join(1)
    a0.forward(); a1.forward()
    for j in (3, 1):
        b0[j].start(); b1[j].start()
    xr.forward()
    pp += [to_partner(3), to_partner(1)]
    reduce_second(0); reduce_second(1)
    b0[0].forward(); b1[0].forward()
    a0.finish(); a1.finish()
    b0[2].start(); b1[2].start()
    xr.finish()
    pp += [to_partner(2)]
    t = y_mine[row].astype(f32)
    for k in range(1, 16):
        ysum[k - 1].wait_recv()
        t += y_got[k].astype(f32)
    proj[col, row] = t.astype(bf)
    yall = [go(remote(proj.at[col, row], proj.at[col, row], s_y.at[1, k], r_y.at[1, k],
                      (lax.rem(row + k, 16), col))) for k in range(1, 16)]
    gather_first(0); gather_first(1)
    publish((0, 0))
    for j in (3, 1):
        b0[j].forward(); b1[j].forward()
    for c in yall:
        c.wait_recv()
    ycol = [go(remote(proj.at[col], proj.at[col], s_z.at[k], r_z.at[k], (row, lax.rem(x + k, 4) * 2 + core)))
            for k in (1, 3, 2)]
    ypart = [y_partner(0)]
    e0.forward(); e1.forward()
    for j in (3, 1):
        f0[j].start(); f1[j].start()
    publish((0, 3), (0, 1))
    for c in pp:
        c.wait_recv()
    b0[2].forward(); b1[2].forward()
    b0[0].finish(); b1[0].finish()
    multiply(0, 0)
    f0[0].forward(); f1[0].forward()
    e0.finish(); e1.finish()
    f0[2].start(); f1[2].start()
    publish((3, 0), (1, 0), (0, 2))
    multiply(1, 0)
    b0[3].finish(); b1[3].finish()
    multiply(0, 3)
    f0[3].forward(); f1[3].forward()
    publish((3, 3), (1, 3))
    multiply(1, 3)
    f0[1].forward(); f1[1].forward()
    publish((3, 1), (1, 1))
    for c, k in zip(ycol, (3, 1, 2)):
        c.wait_recv()
        ypart.append(y_partner(k))
    for c in ypart:
        c.wait_recv()
    w_row[...] = spread_of(left)
    f0[2].forward(); f1[2].forward()
    publish((3, 2), (1, 2))
    b0[1].finish(); b1[1].finish()
    multiply(0, 1)
    for j in (0, 3, 1, 2):
        f0[j].finish(); f1[j].finish()
        publish((2, j))
    multiply(1, 1)
    for h in range(2):
        gb[h] = acc[h].astype(bf)
        last[h] = left_of(h, 2)
    b0[2].finish(); b1[2].finish()
    for h in range(2):
        w_col[h] = spread_of(right.at[h]) + wc[h].reshape(256, 1024).astype(f32)

    @pl.when(root)
    def _():
        wr[...] = wc[half]
        for n in range(16):
            for k in (1, 3, 2):
                along(n, k).wait_send()
            across(n, wc.at[half]).wait_send()

    @pl.when(jnp.logical_and(mine, x != z))
    def _():
        for n in range(16):
            along(n, 1).wait_recv()
            across(n, wr).start()
        for n in range(16):
            across(n, wr).wait_send()

    @pl.when(jnp.logical_not(mine))
    def _():
        for n in range(16):
            across(n, wr).wait_recv()

    wsum = wr[...].reshape(256, 1024).astype(f32) + w_row[...]
    wrv = wsum.astype(bf)
    v = jnp.zeros((256, 1024), f32)
    for h in range(2):
        u = (scale * jnp.dot(wrv, last[h], preferred_element_type=f32)).astype(bf)
        v += (jnp.dot(wrv, gb[h], preferred_element_type=f32)
              + jnp.dot(u, right_of(h, 2), preferred_element_type=f32)) * w_col[h]
    curve = jnp.broadcast_to(jnp.sum(v, axis=1, keepdims=True), (256, 128)).T
    w = wsum.T
    qv = q[...]
    once = jnp.where(col == 0, 1.0, 0.0).astype(f32)
    msg[0:1] = jnp.sum(qv * qv, axis=0, keepdims=True) * once
    msg[1:2] = jnp.sum(qv * w, axis=0, keepdims=True) * once
    msg[2:3] = jnp.sum(w * w, axis=0, keepdims=True) * once
    msg[3:4] = curve[3:4]
    cr = [go(remote(msg, got_r.at[k], s_r.at[k], r_r.at[k], (lax.rem(row + k, 16), col))) for k in range(1, 16)]
    for h in range(2):
        acc[h] += scale * jnp.dot(last[h], right_of(h, 2), preferred_element_type=f32)
    t = msg[...]
    for k, c in enumerate(cr):
        c.wait_recv()
        t += got_r[k + 1]
    msg2[...] = t
    cc = [go(remote(msg2, got_c.at[k], s_c.at[k], r_c.at[k], (row, lax.rem(col + k, 8)))) for k in range(1, 8)]
    for k, c in enumerate(cc):
        c.wait_recv()
        t += got_c[k + 1]
    rr, qw, ww, gg = t[0:1], t[1:2], t[2:3], t[3:4]
    s1 = rr / qw
    new = s1 * s1 * ww - rr
    beta = new / rr
    up = 1.0 + beta
    s2 = new / (up * up * qw - 2.0 * up * s1 * ww + s1 * s1 * gg)
    x_out[...] = (s1 + s2 * up) * qv - (s2 * s1) * w
    for c in sends:
        c.wait_send()


def run(*args):
    dma = pltpu.SemaphoreType.DMA
    bf, f32 = jnp.bfloat16, jnp.float32
    vm = pltpu.VMEM
    hbm = pl.BlockSpec(memory_space=pl.ANY)
    return pl.pallas_call(
        kernel,
        out_shape=(vm((2, 1024, 1024), f32), vm((1024, 256), f32)),
        in_specs=[hbm] * 4 + [pl.BlockSpec(memory_space=pltpu.SMEM)] + [hbm] * 2,
        out_specs=(pl.BlockSpec(memory_space=pltpu.VMEM),) * 2,
        scratch_shapes=[vm((256, 4096), bf), vm((256, 4096), bf), vm((4096, 128), bf), vm((4096, 128), bf),
                        vm((1024, 2048), f32), vm((1024, 256), f32), vm((16, 8, 1024), bf),
                        vm((4, 4, 8, 8, 1024), bf), vm((2, 4, 4, 8, 8, 1024), bf), vm((256, 1024), bf),
                        vm((16, 16, 128), bf), vm((16, 16, 128), bf), vm((8, 16, 16, 128), bf), vm((256, 1024), f32),
                        vm((2, 256, 1024), f32), vm((2, 1024, 256), bf),
                        vm((2, 1024, 1024), bf), vm((2, 4, 4, 16, 1024), bf),
                        vm((2, 2, 4, 16, 512), bf), vm((2, 2, 2, 4, 16, 512), bf), vm((2, 2, 4, 16, 512), bf),
                        vm((2, 4, 16, 1024), bf), vm((2, 3, 16, 1024), bf), vm((2, 4, 4, 16, 1024), bf),
                        vm((4, 4, 16, 1024), bf),
                        vm((4, 256), f32), vm((16, 4, 256), f32), vm((4, 256), f32), vm((8, 4, 256), f32),
                        dma((6,)), dma((2,)), dma((8,)), dma((8,)), dma((16,)), dma((16,)),
                        dma((20,)), dma((20,)), dma((20,)), dma((20,)), dma((4,)), dma((4,)), dma((4,)), dma((4,)),
                        dma((2, 16)), dma((2, 16)), dma((8,)), dma((8,)),
                        dma((2, 6)), dma((2, 6)), dma((2, 4)), dma((2, 4)), dma((20,)), dma((20,)), dma((20,)), dma((20,)),
                        dma((16, 4)), dma((16,)), dma((16,)), dma((16,)), dma((16,)), dma((16,)), dma((8,)), dma((8,))],
        compiler_params=pltpu.CompilerParams(collective_id=0, has_side_effects=True, vmem_limit_bytes=44 * 1024 * 1024),
        name="influence",
    )(*args)


def store_kernel(g, x, g_out, x_out, sem):
    copies = [pltpu.make_async_copy(g.at[h, pl.ds(n * 256, 256)], g_out.at[pl.ds(n * 256, 256), pl.ds(h * 1024, 1024)],
                                    sem.at[4 * h + n]) for h in range(2) for n in range(4)]
    copies.append(pltpu.make_async_copy(x, x_out, sem.at[8]))
    for c in copies:
        c.start()
    for c in copies:
        c.wait()


def store(g, x):
    f32 = jnp.float32
    inside, hbm = pl.BlockSpec(memory_space=pltpu.VMEM), pl.BlockSpec(memory_space=pltpu.HBM)
    return pl.pallas_call(
        store_kernel,
        out_shape=(jax.ShapeDtypeStruct((1024, 2048), f32), jax.ShapeDtypeStruct((1024, 256), f32)),
        in_specs=[inside] * 2,
        out_specs=(hbm, hbm),
        scratch_shapes=[pltpu.SemaphoreType.DMA((9,))],
        compiler_params=pltpu.CompilerParams(vmem_limit_bytes=16 * 1024 * 1024),
        name="store",
    )(pltpu.with_memory_space_constraint(g, pltpu.VMEM), pltpu.with_memory_space_constraint(x, pltpu.VMEM))


def whole(*args):
    return store(*run(*args))


def solution(mesh):
    in_specs = (
        P(("row", "col"), None),
        P(("row", "col"), None),
        P(),
        P(),
        P(("row", "col")),
        P("row", "col"),
        P("row", None),
    )
    out_specs = (P("row", "col"), P("row", None))
    return jax.shard_map(whole, mesh=mesh, in_specs=in_specs, out_specs=out_specs, check_vma=False)
```
